32 devices in a mesh: dp: 8 (over z, x), mp: 4 (over y, core).
Axes of the slice: x: 2, y: 2, z: 4, core: 2. Of those that a mesh axis runs over, the one named last changes fastest.
Arguments:
- gene_ids: int32 [8192], P(('dp', 'mp')), may hold values from 0 to 36095, as said below
- levels: int32 [8192], P(('dp', 'mp')), may hold values from 0 to 63
- study_of_cell: int32 [8], P('dp'), may hold values from 0 to 15
- cotangent: float32 [8192, 768], P(('dp', 'mp')), may hold values from -6 to 6
- tables: float32 [5, 36096, 768], P(None, ('dp', 'mp')), may hold values from -3 to 3
- table_moments: float32 [2, 5, 36096, 768], P(None, None, ('dp', 'mp')), as said below
- level_table: float32 [64, 768], P('dp'), may hold values from -3 to 3
- level_moments: float32 [2, 64, 768], P(None, 'dp'), as said below
- qkv_weight: float32 [2, 3, 768, 768], P(None, None, 'dp'), may hold values from -0.21875 to 0.21875
- qkv_moments: float32 [2, 2, 3, 768, 768], P(None, None, None, 'dp'), as said below
- out_weight: float32 [2, 768, 768], P(None, 'dp'), may hold values from -3.5 to 3.5
- out_moments: float32 [2, 2, 768, 768], P(None, None, 'dp'), as said below
- in_weight: float32 [2, 768, 3072], P(None, 'dp', 'mp'), may hold values from -0.21875 to 0.21875
- in_moments: float32 [2, 2, 768, 3072], P(None, None, 'dp', 'mp'), as said below
- back_weight: float32 [2, 3072, 768], P(None, 'mp', 'dp'), may hold values from -0.109375 to 0.109375
- back_moments: float32 [2, 2, 3072, 768], P(None, None, 'mp', 'dp'), as said below
- norm_params: float32 [2, 3072], P(None, 'dp'), as said below
- norm_moments: float32 [2, 2, 3072], P(None, None, 'dp'), as said below
Outputs:
- encoded: float32 [8192, 768], P(('dp', 'mp'))
- new_tables: float32 [5, 36096, 768], P(None, ('dp', 'mp'))
- new_table_moments: float32 [2, 5, 36096, 768], P(None, None, ('dp', 'mp'))
- new_level_table: float32 [64, 768], P('dp')
- new_level_moments: float32 [2, 64, 768], P(None, 'dp')
- new_qkv_weight: float32 [2, 3, 768, 768], P(None, None, 'dp')
- new_qkv_moments: float32 [2, 2, 3, 768, 768], P(None, None, None, 'dp')
- new_out_weight: float32 [2, 768, 768], P(None, 'dp')
- new_out_moments: float32 [2, 2, 768, 768], P(None, None, 'dp')
- new_in_weight: float32 [2, 768, 3072], P(None, 'dp', 'mp')
- new_in_moments: float32 [2, 2, 768, 3072], P(None, None, 'dp', 'mp')
- new_back_weight: float32 [2, 3072, 768], P(None, 'mp', 'dp')
- new_back_moments: float32 [2, 2, 3072, 768], P(None, None, 'mp', 'dp')
- new_norm_params: float32 [2, 3072], P(None, 'dp')
- new_norm_moments: float32 [2, 2, 3072], P(None, None, 'dp')
The draws below stay inside these ranges and needn't reach their ends.
Inputs may be any that keep to these rules, and one draw needn't show every extreme that they name: `gene_ids`: among the 256 tokens of one device (tokens t with equal t // 256), at most 64 have genes in one block of 4512 table rows (gene // 4512 names the block), and on every device some block receives exactly 64. `table_moments`: second moments are positive. `level_moments`: second moments are positive. `qkv_moments`: second moments are positive. `out_moments`: second moments are positive. `in_moments`: second moments are positive. `back_moments`: second moments are positive. `norm_moments`: second moments are positive. `norm_params`: gains lie in 0.6 to 1.4.
All inputs are finite; a program needn't handle non-finite values.
Results may differ from the reference program's by a relative error of at most 0.014.
Values may be sent and summed in bfloat16 or wider, within the bound.
A program may use at most 320 MiB of HBM per device.

```python
import jax
import jax.numpy as jnp
from jax import lax

D = 768
HEADS = 12
HD = 64
FF = 3072
VOCAB = 36096
BINS = 64
LAYERS = 2
STUDY_TOTAL = 16
STEP = 10
TOK_DEV = 256
GRP_TOK = 1024
LEN = 1024
TOKENS = 8192
CELL_TOTAL = 8


def moment_pair(key, shape, grad_size):
    sign_key, first_key, second_key = jax.random.split(key, 3)
    magnitude = jnp.exp(jax.random.uniform(first_key, shape, jnp.float32, jnp.log(0.5), jnp.log(2.0)))
    sign = jnp.where(jax.random.bernoulli(sign_key, 0.5, shape), 1.0, -1.0)
    first = sign * magnitude * grad_size * (0.1 / 0.9)
    second = jnp.exp(jax.random.uniform(second_key, shape, jnp.float32, 0.0, jnp.log(4.0))) * grad_size * grad_size * (0.001 / 0.999)
    return jnp.stack([first, second]).astype(jnp.float32)


def draw_gene_ids(key, part):
    devices = TOKENS // TOK_DEV
    cell_groups = TOKENS // GRP_TOK
    per_owner = TOK_DEV // cell_groups
    owner_rows = VOCAB // cell_groups

    def one_device(device_key):
        order_key, split_key, place_key, row_key = jax.random.split(device_key, 4)
        owners = jax.random.permutation(order_key, cell_groups)
        shifts = jax.random.randint(split_key, (cell_groups // 2,), 0, per_owner + 1)
        shifts = shifts.at[0].set(per_owner)
        counts = jnp.zeros((cell_groups,), jnp.int32)
        counts = counts.at[owners[0::2]].set(per_owner + shifts).at[owners[1::2]].set(per_owner - shifts)
        ends = jnp.cumsum(counts)
        position = jnp.arange(TOK_DEV)
        owner_of = jnp.sum((position[:, None] >= ends[None, :]).astype(jnp.int32), axis=1)
        owner_of = owner_of[jax.random.permutation(place_key, TOK_DEV)]
        picked = jax.random.randint(row_key, (TOK_DEV,), 0, owner_rows)
        picked = picked * picked // owner_rows
        return owner_of * owner_rows + picked
    return jax.vmap(one_device)(jax.random.split(key, devices)).reshape(TOKENS).astype(jnp.int32)


def draw_table_moments(key, part):
    return moment_pair(key, (5, VOCAB, D), 0.8)


def draw_level_moments(key, part):
    return moment_pair(key, (BINS, D), 0.8 * (TOKENS // BINS) ** 0.5)


def draw_qkv_moments(key, part):
    return moment_pair(key, (LAYERS, 3, D, D), 0.6 * TOKENS ** 0.5)


def draw_out_moments(key, part):
    return moment_pair(key, (LAYERS, D, D), (3 * TOKENS // LEN) ** 0.5)


def draw_in_moments(key, part):
    return moment_pair(key, (LAYERS, D, FF), 0.35 * TOKENS ** 0.5)


def draw_back_moments(key, part):
    return moment_pair(key, (LAYERS, FF, D), 0.4 * TOKENS ** 0.5)


def draw_norm_moments(key, part):
    return moment_pair(key, (LAYERS, 4 * D), 0.8 * TOKENS ** 0.5)


def draw_norm_params(key, part):
    gain_key, bias_key = jax.random.split(key)
    gains = jax.random.uniform(gain_key, (LAYERS, 2, 1, D), jnp.float32, 0.6, 1.4)
    biases = 0.2 * jax.random.normal(bias_key, (LAYERS, 2, 1, D), jnp.float32)
    return jnp.concatenate([gains, biases], axis=2).reshape(LAYERS, 4 * D)


def set_ends(array, own_key, smallest, largest):
    place = [jax.random.randint(jax.random.fold_in(own_key, axis), (), 0, length) for axis, length in enumerate(array.shape)]
    main_axis = array.shape.index(max(array.shape))
    next_to = place[:main_axis] + [(place[main_axis] + 1) % array.shape[main_axis]] + place[main_axis + 1:]
    return array.at[tuple(place)].set(smallest).at[tuple(next_to)].set(largest)


def block_levels(key, extent, shards, least, high):
    level, own = 1.0, jax.random.fold_in(key, 6)
    for dim, blocks in shards:
        draws = jnp.exp(jax.random.uniform(jax.random.fold_in(own, dim), (blocks,), jnp.float32, least / len(shards), high / len(shards)))
        level = level * jnp.repeat(draws, extent[dim] // blocks).reshape([-1 if axis == dim else 1 for axis in range(len(extent))])
    return level


def gaussian(key, extent, deviation, bound, shards=(), held_as=jnp.bfloat16):
    loudness = block_levels(key, extent, shards, -0.22, 0.18) if shards else 1.0
    values = jax.random.normal(key, extent, jnp.float32) * deviation * loudness
    return jnp.minimum(jnp.maximum(values, -bound), bound).astype(held_as)


def setup_inputs(seed: int = 0) -> dict:
    key_list = jax.random.split(jax.random.key(seed), 19)
    gene_ids = draw_gene_ids(jax.random.fold_in(key_list[18], 71), 0)
    levels = set_ends(jax.random.randint(key_list[1], (TOKENS,), 0, BINS), jax.random.fold_in(key_list[1], 1), 0, BINS - 1).astype(jnp.int32)
    study_of_cell = set_ends(jax.random.randint(key_list[2], (CELL_TOTAL,), 0, STUDY_TOTAL), jax.random.fold_in(key_list[2], 1), 0, STUDY_TOTAL - 1).astype(jnp.int32)
    cotangent = gaussian(key_list[3], (TOKENS, D), 1.0, 6.0, ((0, 32),), jnp.float32)
    tables = gaussian(key_list[4], (5, VOCAB, D), 0.4, 3.0, ((1, 32),), jnp.float32)
    table_moments = draw_table_moments(jax.random.fold_in(key_list[18], 71), 0)
    level_table = gaussian(key_list[6], (BINS, D), 0.4, 3.0, ((0, 8),), jnp.float32)
    level_moments = draw_level_moments(jax.random.fold_in(key_list[18], 71), 0)
    qkv_weight = gaussian(key_list[8], (LAYERS, 3, D, D), D ** -0.5, 0.21875, ((2, 8),), jnp.float32)
    qkv_moments = draw_qkv_moments(jax.random.fold_in(key_list[18], 71), 0)
    out_weight = gaussian(key_list[10], (LAYERS, D, D), (max(1, 4 * D // LEN)) ** -0.5, 3.5, ((1, 8),), jnp.float32)
    out_moments = draw_out_moments(jax.random.fold_in(key_list[18], 71), 0)
    in_weight = gaussian(key_list[12], (LAYERS, D, FF), D ** -0.5, 0.21875, ((1, 8), (2, 4)), jnp.float32)
    in_moments = draw_in_moments(jax.random.fold_in(key_list[18], 71), 0)
    back_weight = gaussian(key_list[14], (LAYERS, FF, D), FF ** -0.5, 0.109375, ((1, 4), (2, 8)), jnp.float32)
    back_moments = draw_back_moments(jax.random.fold_in(key_list[18], 71), 0)
    norm_params = draw_norm_params(jax.random.fold_in(key_list[18], 71), 0)
    norm_moments = draw_norm_moments(jax.random.fold_in(key_list[18], 71), 0)
    return dict(gene_ids=gene_ids, levels=levels, study_of_cell=study_of_cell, cotangent=cotangent, tables=tables, table_moments=table_moments, level_table=level_table, level_moments=level_moments, qkv_weight=qkv_weight, qkv_moments=qkv_moments, out_weight=out_weight, out_moments=out_moments, in_weight=in_weight, in_moments=in_moments, back_weight=back_weight, back_moments=back_moments, norm_params=norm_params, norm_moments=norm_moments)


largest_value = lax.Precision.HIGHEST
beta_one = 0.9
beta_two = 0.999
adam_eps = 1e-08
norm_eps = 1e-05
rate_dense = 0.08
rate_mixing = 0.3
rate_table = 0.6
rate_norm = 0.4
decay_rate = 0.01

@jax.custom_vjp
def low(v):
    return lax.optimization_barrier(v.astype(jnp.bfloat16)).astype(jnp.float32)

@jax.custom_vjp
def low_back(v):
    return v

def low_keep(v):
    return (low(v), None)

def low_pass(kept, grad):
    return (grad,)

def back_keep(v):
    return (v, None)

def back_low(kept, grad):
    return (low(grad),)
low.defvjp(low_keep, low_pass)
low_back.defvjp(back_keep, back_low)

def layer_norm(rows, gain, bias):
    centered = rows - lax.optimization_barrier(jnp.mean(rows, axis=-1, keepdims=True))
    inverse = lax.rsqrt(lax.optimization_barrier(jnp.mean(centered * centered, axis=-1, keepdims=True)) + norm_eps)
    return centered * inverse * gain + bias

def to_heads(part):
    return part.reshape(CELL_TOTAL, LEN, HEADS, HD).transpose(0, 2, 1, 3).reshape(CELL_TOTAL * HEADS, LEN, HD)

def from_heads(part):
    return part.reshape(CELL_TOTAL, HEADS, LEN, HD).transpose(0, 2, 1, 3).reshape(CELL_TOTAL * LEN, D)

def attend_head(triple):
    query, keys, values = triple
    scores = low_back(jnp.dot(query, keys.T, precision=largest_value) * HD ** (-0.5))
    probs = jax.nn.softmax(scores, axis=-1)
    return jnp.dot(low(probs), values, precision=largest_value)

def encoder_layer(hidden, qkv_layer, out_layer, in_layer, back_layer, norm_row):
    tokens_low = low(hidden)
    parts = [low(low_back(jnp.dot(tokens_low, qkv_layer[index], precision=largest_value))) for index in range(3)]
    heads = tuple((to_heads(part) for part in parts))
    mixed = from_heads(lax.map(jax.checkpoint(attend_head), heads))
    mixed = low(low_back(mixed))
    attention = low_back(jnp.dot(mixed, out_layer, precision=largest_value))
    first = layer_norm(hidden + attention, norm_row[:D], norm_row[D:2 * D])
    first_low = low(first)
    inner = low_back(jnp.dot(first_low, in_layer, precision=largest_value))
    active = low(jax.nn.gelu(inner, approximate=False))
    feed = low_back(jnp.dot(active, back_layer, precision=largest_value))
    return layer_norm(first + feed, norm_row[2 * D:3 * D], norm_row[3 * D:])

def adam_step(weight, moments, grad, rate, decay):
    first = beta_one * moments[0] + (1.0 - beta_one) * grad
    second = beta_two * moments[1] + (1.0 - beta_two) * grad * grad
    first_hat = first / (1.0 - beta_one ** STEP)
    second_hat = second / (1.0 - beta_two ** STEP)
    new_weight = weight - rate * (first_hat / (jnp.sqrt(second_hat) + adam_eps) + decay * weight)
    return (new_weight, jnp.stack([first, second]))

def reference(gene_ids, levels, study_of_cell, cotangent, tables, table_moments, level_table, level_moments, qkv_weight, qkv_moments, out_weight, out_moments, in_weight, in_moments, back_weight, back_moments, norm_params, norm_moments):
    study_onehot = (study_of_cell[:, None] == jnp.arange(STUDY_TOTAL)[None, :]).astype(jnp.float32)
    cells_per_study = lax.optimization_barrier(jnp.sum(study_onehot, axis=0))
    cell_balance_weight = CELL_TOTAL / (STUDY_TOTAL * jnp.dot(study_onehot, cells_per_study, precision=largest_value))
    out_grad = cotangent * jnp.repeat(cell_balance_weight, LEN)[:, None]

    def forward(tables, level_table, qkv_weight, out_weight, in_weight, back_weight, norm_params):
        row_sum = lax.optimization_barrier(jnp.sum(tables, axis=0))
        hidden = low(jnp.take(row_sum, gene_ids, axis=0)) + jnp.take(low(level_table), levels, axis=0)
        for layer in range(LAYERS):
            hidden = encoder_layer(hidden, low(qkv_weight[layer]), low(out_weight[layer]), low(in_weight[layer]), low(back_weight[layer]), norm_params[layer])
        return hidden
    encoded, pullback = jax.vjp(forward, tables, level_table, qkv_weight, out_weight, in_weight, back_weight, norm_params)
    grads = pullback(out_grad)
    hits = jax.ops.segment_sum(jnp.ones_like(gene_ids), gene_ids, num_segments=VOCAB)
    touched = (hits > 0)[None, :, None]
    table_new, table_state = adam_step(tables, table_moments, grads[0], rate_table, decay_rate)
    table_new = jnp.where(touched, table_new, tables)
    table_state = jnp.where(touched[None], table_state, table_moments)
    level_new, level_state = adam_step(level_table, level_moments, grads[1], rate_table, decay_rate)
    qkv_new, qkv_state = adam_step(qkv_weight, qkv_moments, grads[2], rate_dense, decay_rate)
    out_new, out_state = adam_step(out_weight, out_moments, grads[3], rate_mixing, decay_rate)
    in_new, in_state = adam_step(in_weight, in_moments, grads[4], rate_dense, decay_rate)
    back_new, back_state = adam_step(back_weight, back_moments, grads[5], rate_dense, decay_rate)
    norm_new, norm_state = adam_step(norm_params, norm_moments, grads[6], rate_norm, 0.0)
    return (encoded, table_new, table_state, level_new, level_state, qkv_new, qkv_state, out_new, out_state, in_new, in_state, back_new, back_state, norm_new, norm_state)
```

```python
from functools import partial

import jax
import jax.numpy as jnp
from jax import lax
from jax.experimental import pallas as pl
from jax.experimental.pallas import tpu as pltpu
from jax.sharding import PartitionSpec as P

HEADS = 12
HD = 64
STUDY_TOTAL = 16
STEP = 10


largest_value = lax.Precision.HIGHEST
beta_one = 0.9
beta_two = 0.999
adam_eps = 1e-08
norm_eps = 1e-05
rate_dense = 0.08
rate_mixing = 0.3
rate_table = 0.6
rate_norm = 0.4
decay_rate = 0.01


def spread_rows(rows):
    return lax.all_gather(rows, "mp", axis=0, tiled=True)


def summed_rows(term, count):
    return lax.psum_scatter(
        term(jnp.int32(0), count * lax.axis_size("mp")).astype(jnp.bfloat16),
        "mp",
        scatter_dimension=0,
        tiled=True,
    ).astype(jnp.float32)


def norm_forward(rows, gain, bias):
    centered = rows - jnp.mean(rows, axis=-1, keepdims=True)
    inverse = lax.rsqrt(jnp.mean(centered * centered, axis=-1, keepdims=True) + norm_eps)
    normal = centered * inverse
    return (normal * gain + bias, normal, inverse)


def norm_backward(gradient, normal, inverse, gain):
    scaled = gradient * gain
    inner_part = (
        scaled
        - jnp.mean(scaled, axis=-1, keepdims=True)
        - normal * jnp.mean(scaled * normal, axis=-1, keepdims=True)
    )
    return (inner_part * inverse, jnp.sum(gradient * normal, axis=0), jnp.sum(gradient, axis=0))


def gelu_grad(inner, gradient):
    return jax.vjp(partial(jax.nn.gelu, approximate=False), inner)[1](gradient)[0]


def head_major(rows):
    return rows.reshape(rows.shape[0], HEADS, HD).transpose(1, 0, 2)


def row_major(heads):
    return heads.transpose(1, 0, 2).reshape(heads.shape[1], HEADS * HD)


def attend_forward(query, keys, values):
    scale = HD ** (-0.5)

    def one_head(pieces):
        head_query, head_keys, head_values = pieces
        scores = (
            jnp.einsum("qd,kd->qk", head_query, head_keys, preferred_element_type=jnp.float32)
            * scale
        )
        peak = jnp.max(scores, axis=-1, keepdims=True)
        raised = jnp.exp(scores - peak)
        total = jnp.sum(raised, axis=-1, keepdims=True)
        probs = (raised / total).astype(jnp.bfloat16)
        mixed = jnp.dot(probs, head_values, preferred_element_type=jnp.float32).astype(jnp.bfloat16)
        return (mixed, (peak + jnp.log(total))[:, 0])

    mixed, log_total = lax.map(one_head, (head_major(query), head_major(keys), head_major(values)))
    return (row_major(mixed), log_total)


def attend_backward(query, keys, values, mixed_grad, log_total):
    scale = HD ** (-0.5)

    def one_head(pieces):
        head_query, head_keys, head_values, head_grad, head_total = pieces
        scores = (
            jnp.einsum("qd,kd->qk", head_query, head_keys, preferred_element_type=jnp.float32)
            * scale
        )
        probs = jnp.exp(scores - head_total[:, None])
        product = jnp.einsum(
            "qd,kd->qk", head_grad, head_values, preferred_element_type=jnp.float32
        )
        center = jnp.sum(probs * product, axis=-1, keepdims=True)
        score_grad = (probs * (product - center)).astype(jnp.bfloat16)
        query_grad = (
            jnp.dot(score_grad, head_keys, preferred_element_type=jnp.float32) * scale
        ).astype(jnp.bfloat16)
        key_grad = (
            jnp.einsum("qk,qd->kd", score_grad, head_query, preferred_element_type=jnp.float32)
            * scale
        )
        value_grad = jnp.einsum(
            "qk,qd->kd", probs.astype(jnp.bfloat16), head_grad, preferred_element_type=jnp.float32
        )
        return (query_grad, key_grad, value_grad)

    query_grad, key_grad, value_grad = lax.map(
        one_head,
        (
            head_major(query),
            head_major(keys),
            head_major(values),
            head_major(mixed_grad),
            log_total,
        ),
    )
    return (row_major(query_grad), jnp.stack([row_major(key_grad), row_major(value_grad)], axis=1))


def slots_of(row_owner):
    place = jnp.arange(row_owner.shape[0])
    earlier = (row_owner[:, None] == row_owner[None, :]) & (place[None, :] < place[:, None])
    return jnp.sum(earlier.astype(jnp.int32), axis=1)


def slotted_ids(gene_ids, row_owner, slot_index, cell_groups, capacity):
    code = row_owner * capacity + slot_index
    hot = code[None, :] == jnp.arange(cell_groups * capacity)[:, None]
    found = jnp.sum(jnp.where(hot, gene_ids[None, :] + 1, 0), axis=1) - 1
    return found.reshape(cell_groups, capacity)


def adam_step(weight, moments, gradient, rate, decay):
    first = beta_one * moments[0] + (1.0 - beta_one) * gradient
    second = beta_two * moments[1] + (1.0 - beta_two) * gradient * gradient
    first_hat = first / (1.0 - beta_one**STEP)
    second_hat = second / (1.0 - beta_two**STEP)
    new_weight = weight - rate * (first_hat / (jnp.sqrt(second_hat) + adam_eps) + decay * weight)
    return (new_weight, jnp.stack([first, second]))


def general_body(
    gene_ids,
    levels,
    study_of_cell,
    cotangent,
    tables,
    table_moments,
    level_table,
    level_moments,
    qkv_weight,
    qkv_moments,
    out_weight,
    out_moments,
    in_weight,
    in_moments,
    back_weight,
    back_moments,
    norm_params,
    norm_moments,
):
    cell_groups = lax.axis_size("dp")
    rows_here = cotangent.shape[0]
    model_width = cotangent.shape[1]
    layers = qkv_weight.shape[0]
    local_cells = study_of_cell.shape[0]
    capacity = 2 * rows_here // cell_groups
    own_rows = tables.shape[1]
    block_size = own_rows * lax.axis_size("mp")
    qkv_full, out_full, in_part, back_part, level_full = (
        lax.all_gather(qkv_weight.astype(jnp.bfloat16), "dp", axis=2, tiled=True),
        lax.all_gather(out_weight.astype(jnp.bfloat16), "dp", axis=1, tiled=True),
        lax.all_gather(in_weight.astype(jnp.bfloat16), "dp", axis=1, tiled=True),
        lax.all_gather(back_weight.astype(jnp.bfloat16), "dp", axis=2, tiled=True),
        lax.all_gather(level_table.astype(jnp.bfloat16), "dp", axis=0, tiled=True),
    )
    study_onehot = (study_of_cell[:, None] == jnp.arange(STUDY_TOTAL)[None, :]).astype(jnp.float32)
    norm_full, study_all = (
        lax.all_gather(norm_params, "dp", axis=1, tiled=True),
        lax.all_gather(study_onehot, "dp", axis=0, tiled=True),
    )
    cells_per_study = jnp.sum(study_all, axis=0)
    cell_balance_weight = (
        cell_groups
        * local_cells
        / (STUDY_TOTAL * jnp.dot(study_onehot, cells_per_study, precision=largest_value))
    )
    out_grad = cotangent * cell_balance_weight[0]
    summed_tables = jnp.sum(tables, axis=0).astype(jnp.bfloat16)
    table_rows = lax.all_gather(summed_tables, "mp", axis=0, tiled=True)
    row_owner = gene_ids // block_size
    slot_index = slots_of(row_owner)
    sent_ids = slotted_ids(gene_ids, row_owner, slot_index, cell_groups, capacity)
    asked_ids = lax.all_to_all(sent_ids, "dp", split_axis=0, concat_axis=0, tiled=True)
    present = asked_ids >= 0
    safe_row = jnp.where(present, asked_ids - lax.axis_index("dp") * block_size, 0)
    found_rows = jnp.where(present[..., None], jnp.take(table_rows, safe_row, axis=0), 0)
    returned = lax.all_to_all(found_rows, "dp", split_axis=0, concat_axis=0, tiled=True)
    gene_part = returned[row_owner, slot_index].astype(jnp.float32)
    level_hot = (levels[:, None] == jnp.arange(level_full.shape[0])[None, :]).astype(jnp.bfloat16)
    hidden = gene_part + jnp.dot(level_hot, level_full, preferred_element_type=jnp.float32)
    kept = []
    for layer in range(layers):
        norm_row = norm_full[layer]
        tokens_low = hidden.astype(jnp.bfloat16)
        projected = jnp.einsum(
            "td,cdh->tch", tokens_low, qkv_full[layer], preferred_element_type=jnp.float32
        ).astype(jnp.bfloat16)
        query = projected[:, 0]
        cell_rows = spread_rows(projected[:, 1:])
        keys, values = (cell_rows[:, 0], cell_rows[:, 1])
        mixed, log_total = attend_forward(query, keys, values)
        attention = jnp.dot(mixed, out_full[layer], preferred_element_type=jnp.float32)
        first, first_normal, first_inverse = norm_forward(
            hidden + attention, norm_row[:model_width], norm_row[model_width : 2 * model_width]
        )
        first_low = first.astype(jnp.bfloat16)
        in_layer, back_layer = (in_part[layer], back_part[layer])
        first_spread = spread_rows(first_low)
        inner = jnp.dot(first_spread, in_layer, preferred_element_type=jnp.float32)
        active = jax.nn.gelu(inner, approximate=False).astype(jnp.bfloat16)

        def feed_term(start, count):
            return jnp.dot(active, back_layer, preferred_element_type=jnp.float32)

        feed = summed_rows(feed_term, rows_here)
        second, second_normal, second_inverse = norm_forward(
            first + feed, norm_row[2 * model_width : 3 * model_width], norm_row[3 * model_width :]
        )
        kept.append(
            (
                tokens_low,
                query,
                keys,
                values,
                mixed,
                log_total,
                first_normal,
                first_inverse,
                first_spread,
                inner,
                active,
                in_layer,
                back_layer,
                second_normal,
                second_inverse,
            )
        )
        hidden = second
    gradient = out_grad
    qkv_grads = [None] * layers
    out_grads = [None] * layers
    in_grads = [None] * layers
    back_grads = [None] * layers
    norm_grads = [None] * layers
    for layer in reversed(range(layers)):
        (
            tokens_low,
            query,
            keys,
            values,
            mixed,
            log_total,
            first_normal,
            first_inverse,
            first_spread,
            inner,
            active,
            in_layer,
            back_layer,
            second_normal,
            second_inverse,
        ) = kept[layer]
        norm_row = norm_full[layer]
        grad_second, gain_two, bias_two = norm_backward(
            gradient, second_normal, second_inverse, norm_row[2 * model_width : 3 * model_width]
        )
        feed_low = grad_second.astype(jnp.bfloat16)
        feed_spread = spread_rows(feed_low)
        back_grads[layer] = jnp.einsum(
            "tf,td->fd", active, feed_spread, preferred_element_type=jnp.float32
        )
        active_grad = jnp.einsum(
            "td,fd->tf", feed_spread, back_layer, preferred_element_type=jnp.float32
        )
        inner_grad = gelu_grad(inner, active_grad).astype(jnp.bfloat16)
        in_grads[layer] = jnp.einsum(
            "td,tf->df", first_spread, inner_grad, preferred_element_type=jnp.float32
        )

        def first_term(start, count):
            return jnp.einsum("tf,df->td", inner_grad, in_layer, preferred_element_type=jnp.float32)

        first_grad = summed_rows(first_term, rows_here)
        grad_first, gain_one, bias_one = norm_backward(
            grad_second + first_grad, first_normal, first_inverse, norm_row[:model_width]
        )
        norm_grads[layer] = jnp.concatenate([gain_one, bias_one, gain_two, bias_two])
        attention_low = grad_first.astype(jnp.bfloat16)
        out_grads[layer] = jnp.einsum(
            "th,td->hd", mixed, attention_low, preferred_element_type=jnp.float32
        )
        mixed_grad = jnp.einsum(
            "td,hd->th", attention_low, out_full[layer], preferred_element_type=jnp.float32
        ).astype(jnp.bfloat16)
        query_grad, pair_partial = attend_backward(query, keys, values, mixed_grad, log_total)
        pair_grad = lax.psum_scatter(
            pair_partial.astype(jnp.bfloat16), "mp", scatter_dimension=0, tiled=True
        )
        stacked = jnp.concatenate([query_grad[:, None, :], pair_grad], axis=1)
        qkv_grads[layer] = jnp.einsum(
            "td,tch->cdh", tokens_low, stacked, preferred_element_type=jnp.float32
        )
        gradient = grad_first + jnp.einsum(
            "tch,cdh->td", stacked, qkv_full[layer], preferred_element_type=jnp.float32
        )
    level_grad = jnp.dot(level_hot.astype(jnp.float32).T, gradient, precision=largest_value)
    grad_slots = (
        jnp.zeros((cell_groups, capacity, model_width), jnp.float32)
        .at[row_owner, slot_index]
        .set(gradient)
    )
    arrived = lax.all_to_all(
        grad_slots.astype(jnp.bfloat16), "dp", split_axis=0, concat_axis=0, tiled=True
    ).astype(grad_slots.dtype)
    arrived = jnp.where(present[..., None], arrived, 0.0)
    flat_rows = safe_row.reshape(-1)
    block_grad = jax.ops.segment_sum(
        arrived.reshape(-1, model_width), flat_rows, num_segments=block_size
    )
    block_hits = jax.ops.segment_sum(
        present.reshape(-1).astype(jnp.float32), flat_rows, num_segments=block_size
    )
    row_grad, hits = (
        lax.psum_scatter(
            block_grad.astype(jnp.bfloat16), "mp", scatter_dimension=0, tiled=True
        ).astype(jnp.float32),
        lax.psum_scatter(
            block_hits.astype(jnp.bfloat16), "mp", scatter_dimension=0, tiled=True
        ).astype(jnp.float32),
    )
    qkv_sum, out_sum, in_sum, back_sum, level_sum, norm_sum = (
        lax.psum_scatter(
            jnp.stack(qkv_grads).astype(jnp.bfloat16), "dp", scatter_dimension=2, tiled=True
        ).astype(jnp.float32),
        lax.psum_scatter(
            jnp.stack(out_grads).astype(jnp.bfloat16), "dp", scatter_dimension=1, tiled=True
        ).astype(jnp.float32),
        lax.psum_scatter(
            jnp.stack(in_grads).astype(jnp.bfloat16), "dp", scatter_dimension=1, tiled=True
        ).astype(jnp.float32),
        lax.psum_scatter(
            jnp.stack(back_grads).astype(jnp.bfloat16), "dp", scatter_dimension=2, tiled=True
        ).astype(jnp.float32),
        lax.psum_scatter(
            level_grad.astype(jnp.bfloat16), "dp", scatter_dimension=0, tiled=True
        ).astype(jnp.float32),
        lax.psum_scatter(
            jnp.stack(norm_grads).astype(jnp.bfloat16), "dp", scatter_dimension=1, tiled=True
        ).astype(jnp.float32),
    )
    qkv_sum, out_sum, level_sum, norm_sum = (
        lax.psum(qkv_sum.astype(jnp.bfloat16), "mp").astype(jnp.float32),
        lax.psum(out_sum.astype(jnp.bfloat16), "mp").astype(jnp.float32),
        lax.psum(level_sum.astype(jnp.bfloat16), "mp").astype(jnp.float32),
        lax.psum(norm_sum.astype(jnp.bfloat16), "mp").astype(jnp.float32),
    )
    touched = (hits > 0)[None, :, None]
    table_grad = jnp.broadcast_to(row_grad[None], tables.shape)
    table_new, table_state = adam_step(tables, table_moments, table_grad, rate_table, decay_rate)
    table_new = jnp.where(touched, table_new, tables)
    table_state = jnp.where(touched[None], table_state, table_moments)
    level_new, level_state = adam_step(
        level_table, level_moments, level_sum, rate_table, decay_rate
    )
    qkv_new, qkv_state = adam_step(qkv_weight, qkv_moments, qkv_sum, rate_dense, decay_rate)
    out_new, out_state = adam_step(out_weight, out_moments, out_sum, rate_mixing, decay_rate)
    in_new, in_state = adam_step(in_weight, in_moments, in_sum, rate_dense, decay_rate)
    back_new, back_state = adam_step(back_weight, back_moments, back_sum, rate_dense, decay_rate)
    norm_new, norm_state = adam_step(norm_params, norm_moments, norm_sum, rate_norm, 0.0)
    return (
        hidden,
        table_new,
        table_state,
        level_new,
        level_state,
        qkv_new,
        qkv_state,
        out_new,
        out_state,
        in_new,
        in_state,
        back_new,
        back_state,
        norm_new,
        norm_state,
    )


MESH = pl.DeviceIdType.MESH
SIB, FACE = 0, 1
TILE = 128


def nn(a, b):
    return lax.dot_general(a, b, (((1,), (0,)), ((), ())), preferred_element_type=jnp.float32)


def nt(a, b):
    return lax.dot_general(a, b, (((1,), (1,)), ((), ())), preferred_element_type=jnp.float32)


def tn(a, b):
    return lax.dot_general(a, b, (((0,), (0,)), ((), ())), preferred_element_type=jnp.float32)


def near_devices():
    group, member = lax.axis_index("dp"), lax.axis_index("mp")
    core = member % 2
    return (group, member + 1 - 2 * core), (group, (member + 2) % 4)


def greet(peers):
    barrier = pltpu.get_barrier_semaphore()
    for peer in peers:
        pl.semaphore_signal(barrier, inc=1, device_id=peer, device_id_type=MESH)
    pl.semaphore_wait(barrier, len(peers))


def send(source, target, sems, index, peer):
    copy = pltpu.make_async_remote_copy(
        src_ref=source,
        dst_ref=target,
        send_sem=sems[0].at[index],
        recv_sem=sems[1].at[index],
        device_id=peer,
        device_id_type=MESH,
    )
    copy.start()
    return copy


GATHER_COPIES = 5
SUM_COPIES = 3


class Gather:
    def __init__(self, buf, sems, sib, face):
        self.buf, self.sems, self.sib = buf, sems, sib
        rows = buf.shape[0] // 4
        half = rows // 2
        self.rows, self.half = rows, half
        self.across = [
            send(
                buf.at[pl.ds(i * half, half)],
                buf.at[pl.ds(2 * rows + i * half, half)],
                sems,
                i,
                face,
            )
            for i in range(2)
        ]
        self.beside = send(buf.at[pl.ds(0, rows)], buf.at[pl.ds(rows, rows)], sems, 2, sib)
        self.handed = []

    def wait_beside(self):
        self.beside.wait_recv()

    def hand_on(self, i):
        self.across[i].wait_recv()
        start = 2 * self.rows + i * self.half
        self.handed.append(
            send(
                self.buf.at[pl.ds(start, self.half)],
                self.buf.at[pl.ds(start + self.rows, self.half)],
                self.sems,
                3 + i,
                self.sib,
            )
        )

    def wait_handed(self):
        for copy in self.handed:
            copy.wait_recv()

    def finish(self):
        for copy in [*self.across, self.beside, *self.handed]:
            copy.wait_send()


class Total:
    def __init__(self, out, into, sems, sib, face):
        self.out, self.into, self.sems = out, into, sems
        self.sib, self.face = sib, face
        self.copies = []

    def give_far(self, term):
        self.out[0] = term.astype(jnp.bfloat16)
        self.copies.append(send(self.out.at[0], self.into.at[0], self.sems, 0, self.sib))

    def give_facing(self, term):
        self.copies[0].wait_recv()
        self.out[1] = (term + self.into[0].astype(jnp.float32)).astype(jnp.bfloat16)
        self.copies.append(send(self.out.at[1], self.into.at[1], self.sems, 1, self.face))

    def give_beside(self, term):
        self.out[2] = term.astype(jnp.bfloat16)
        self.copies.append(send(self.out.at[2], self.into.at[2], self.sems, 2, self.sib))

    def take(self, term):
        for copy in self.copies[1:]:
            copy.wait_recv()
        return term + self.into[2].astype(jnp.float32) + self.into[1].astype(jnp.float32)

    def finish(self):
        for copy in self.copies:
            copy.wait_send()


def gelu_pair(x):
    t = 1.0 / (1.0 + (0.3275911 * 0.7071067811865476) * jnp.abs(x))
    raised = jnp.exp(-0.5 * x * x)
    series = t * (
        0.254829592
        + t * (-0.284496736 + t * (1.421413741 + t * (-1.453152027 + t * 1.061405429)))
    )
    upper = 0.5 * series * raised
    share = jnp.where(x >= 0, 1.0 - upper, upper)
    return x * share, share + x * raised * 0.3989422804014327


def forward_kernel(
    hidden,
    qkv_w,
    out_w,
    in_w,
    back_w,
    norms,
    second,
    second_normal,
    second_inverse,
    first_normal,
    first_inverse,
    tokens,
    heads,
    mixed,
    logs,
    firsts,
    active,
    slope,
    mixed_t,
    held,
    out_a,
    into_a,
    out_b,
    into_b,
    *sems,
):
    sib, face = near_devices()
    greet((sib, face))
    gather_a, total_a = sems[0:2], sems[2:4]
    gather_b, total_b = sems[4:6], sems[6:8]
    rows = hidden.shape[0]
    share = mixed.shape[1]
    per_device = share // HD

    def block(b):
        return pl.ds(b * rows, rows)

    tokens[block(0), :] = hidden[...].astype(jnp.bfloat16)
    gather = Gather(tokens, gather_a, sib, face)

    def project(b):
        parts = nn(tokens[block(b), :], qkv_w[...])
        for j in range(3 * per_device):
            piece = parts[:, j * HD : (j + 1) * HD]
            if j < per_device:
                piece = piece * HD ** (-0.5)
            heads[j, block(b), :] = piece.astype(jnp.bfloat16)

    project(0)
    gather.wait_beside()
    project(1)
    gather.hand_on(0)
    gather.hand_on(1)
    project(2)
    gather.wait_handed()
    project(3)

    def attend(b):
        def one_head(h, carry):
            scores = nt(heads[per_device + h], heads[h, block(b), :])
            peak = jnp.max(scores, axis=0, keepdims=True)
            raised = jnp.exp(scores - peak)
            total = jnp.sum(raised, axis=0, keepdims=True)
            result = tn(heads[2 * per_device + h], raised.astype(jnp.bfloat16)) / total
            mixed_t[pl.ds(pl.multiple_of(h * HD, HD), HD), :] = result
            logs[b * per_device + h] = peak + jnp.log(total)
            return carry

        lax.fori_loop(0, per_device, one_head, 0)
        rows_mixed = mixed_t[...].T.astype(jnp.bfloat16)
        mixed[block(b), :] = rows_mixed
        return nt(rows_mixed, out_w[...])

    total = Total(out_a, into_a, total_a, sib, face)
    total.give_far(attend(3))
    total.give_facing(attend(2))
    total.give_beside(attend(1))
    attention = total.take(attend(0))

    first, normal, inverse = norm_forward(hidden[...] + attention, norms[0:1, :], norms[1:2, :])
    first_normal[...] = normal
    first_inverse[...] = inverse
    firsts[block(0), :] = first.astype(jnp.bfloat16)
    gather_two = Gather(firsts, gather_b, sib, face)

    def feed(b):
        value, gradient = gelu_pair(nn(firsts[block(b), :], in_w[...]))
        value = value.astype(jnp.bfloat16)
        active[block(b), :] = value
        slope[block(b), :] = gradient.astype(jnp.bfloat16)
        return nt(value, back_w[...])

    total_two = Total(out_b, into_b, total_b, sib, face)
    held[...] = first + feed(0)
    gather_two.wait_beside()
    term_beside = feed(1)
    gather_two.hand_on(0)
    gather_two.hand_on(1)
    term_facing = feed(2)
    gather_two.wait_handed()
    total_two.give_far(feed(3))
    total_two.give_facing(term_facing)
    total_two.give_beside(term_beside)
    summed = total_two.take(held[...])
    result, normal, inverse = norm_forward(summed, norms[2:3, :], norms[3:4, :])
    second[...] = result
    second_normal[...] = normal
    second_inverse[...] = inverse
    gather.finish()
    total.finish()
    gather_two.finish()
    total_two.finish()


def backward_kernel(
    gradient,
    qkv_w,
    out_w,
    in_w,
    back_w,
    norms,
    second_normal,
    second_inverse,
    first_normal,
    first_inverse,
    tokens,
    heads,
    mixed,
    logs,
    firsts,
    active,
    slope,
    gradient_out,
    grads,
    norm_grads,
    feeds,
    inner,
    lows,
    mixed_grad,
    probs,
    score_grad,
    head_grads,
    pieces,
    held,
    out_a,
    into_a,
    out_b,
    into_b,
    *sems,
):
    sib, face = near_devices()
    greet((sib, face))
    gather_a, total_a = sems[0:2], sems[2:4]
    gather_b, total_b = sems[4:6], sems[6:8]
    rows = gradient.shape[0]
    share = mixed.shape[1]
    width = gradient.shape[1]
    units = in_w.shape[1]
    per_device = share // HD

    def block(b):
        return pl.ds(b * rows, rows)

    grad_second, gain, bias = norm_backward(
        gradient[...], second_normal[...], second_inverse[...], norms[2:3, :]
    )
    norm_grads[2:3, :] = gain[None]
    norm_grads[3:4, :] = bias[None]
    feeds[block(0), :] = grad_second.astype(jnp.bfloat16)
    gather = Gather(feeds, gather_a, sib, face)
    held[...] = grad_second

    def feed(b):
        part = nn(feeds[block(b), :], back_w[...]) * slope[block(b), :].astype(jnp.float32)
        part = part.astype(jnp.bfloat16)
        inner[block(b), :] = part
        return nt(part, in_w[...])

    total = Total(out_a, into_a, total_a, sib, face)
    held[...] += feed(0)
    gather.wait_beside()
    term_beside = feed(1)
    gather.hand_on(0)
    gather.hand_on(1)
    term_facing = feed(2)
    gather.wait_handed()
    total.give_far(feed(3))
    total.give_facing(term_facing)
    total.give_beside(term_beside)
    after = 3 * share + share
    grads[:, after : after + units] = tn(firsts[...], inner[...]).astype(jnp.bfloat16)
    grads[:, after + units : after + 2 * units] = tn(feeds[...], active[...]).astype(jnp.bfloat16)
    summed = total.take(held[...])
    grad_first, gain, bias = norm_backward(
        summed, first_normal[...], first_inverse[...], norms[0:1, :]
    )
    norm_grads[0:1, :] = gain[None]
    norm_grads[1:2, :] = bias[None]
    lows[block(0), :] = grad_first.astype(jnp.bfloat16)
    gather_two = Gather(lows, gather_b, sib, face)
    held[...] = grad_first

    def spread(b):
        parts = nn(lows[block(b), :], out_w[...])
        for j in range(per_device):
            mixed_grad[j, block(b), :] = parts[:, j * HD : (j + 1) * HD].astype(jnp.bfloat16)

    def score(b):
        def one_head(h, carry):
            scores = nt(heads[per_device + h], heads[h, block(b), :])
            prob = jnp.exp(scores - logs[b * per_device + h])
            product = nt(heads[2 * per_device + h], mixed_grad[h, block(b), :])
            center = jnp.sum(prob * product, axis=0, keepdims=True)
            score_grad[h, :, block(b)] = (prob * (product - center)).astype(jnp.bfloat16)
            probs[h, :, block(b)] = prob.astype(jnp.bfloat16)
            return carry

        lax.fori_loop(0, per_device, one_head, 0)

    spread(0)
    score(0)
    gather_two.wait_beside()
    spread(1)
    score(1)
    gather_two.hand_on(0)
    gather_two.hand_on(1)
    spread(2)
    score(2)
    gather_two.wait_handed()
    spread(3)
    score(3)

    def close(h, carry):
        pieces[per_device + h] = nn(score_grad[h], heads[h]).astype(jnp.bfloat16)
        pieces[2 * per_device + h] = nn(probs[h], mixed_grad[h]).astype(jnp.bfloat16)
        turned = tn(heads[per_device + h], score_grad[h]) * HD ** (-0.5)
        pieces[h] = turned.T.astype(jnp.bfloat16)
        return carry

    lax.fori_loop(0, per_device, close, 0)
    for j in range(3 * per_device):
        head_grads[:, j * HD : (j + 1) * HD] = pieces[j]

    total_two = Total(out_b, into_b, total_b, sib, face)
    total_two.give_far(nt(head_grads[block(3), :], qkv_w[...]))
    total_two.give_facing(nt(head_grads[block(2), :], qkv_w[...]))
    total_two.give_beside(nt(head_grads[block(1), :], qkv_w[...]))
    held[...] += nt(head_grads[block(0), :], qkv_w[...])
    grads[:, 0 : 3 * share] = tn(tokens[...], head_grads[...]).astype(jnp.bfloat16)
    grads[:, 3 * share : after] = tn(lows[...], mixed[...]).astype(jnp.bfloat16)
    gradient_out[...] = total_two.take(held[...])
    gather.finish()
    total.finish()
    gather_two.finish()
    total_two.finish()


def exchange_scratch(rows, width):
    return [
        pltpu.VMEM((3, rows, width), jnp.bfloat16),
        pltpu.VMEM((3, rows, width), jnp.bfloat16),
        pltpu.VMEM((3, rows, width), jnp.bfloat16),
        pltpu.VMEM((3, rows, width), jnp.bfloat16),
    ] + [
        pltpu.SemaphoreType.DMA((count,))
        for count in (GATHER_COPIES, GATHER_COPIES, SUM_COPIES, SUM_COPIES) * 2
    ]


def in_vmem(count):
    return [pl.BlockSpec(memory_space=pltpu.VMEM)] * count


def kernel_params(collective_id):
    return pltpu.CompilerParams(
        collective_id=collective_id, has_side_effects=True, vmem_limit_bytes=60 * 2**20
    )


def layer_forward(hidden, weights, norms):
    rows, width = hidden.shape
    cell = 4 * rows
    qkv_w, out_w, in_w, back_w = weights
    share = out_w.shape[1]
    per_device = share // HD
    units = in_w.shape[1]
    f32, low = jnp.float32, jnp.bfloat16
    shapes = [
        ((rows, width), f32),
        ((rows, width), f32),
        ((rows, 1), f32),
        ((rows, width), f32),
        ((rows, 1), f32),
        ((cell, width), low),
        ((3 * per_device, cell, HD), low),
        ((cell, share), low),
        ((4 * per_device, 1, rows), f32),
        ((cell, width), low),
        ((cell, units), low),
        ((cell, units), low),
    ]
    flops = 2 * cell * width * (4 * share + 2 * units) + 4 * cell * cell * share
    return pl.pallas_call(
        forward_kernel,
        out_shape=[jax.ShapeDtypeStruct(*s) for s in shapes],
        in_specs=in_vmem(6),
        out_specs=in_vmem(len(shapes)),
        scratch_shapes=[pltpu.VMEM((share, rows), f32), pltpu.VMEM((rows, width), f32)]
        + exchange_scratch(rows, width),
        compiler_params=kernel_params(1),
        cost_estimate=pl.CostEstimate(
            flops=flops, bytes_accessed=100_000_000, transcendentals=cell * cell * per_device
        ),
        name="layer_forward",
    )(hidden, qkv_w, out_w, in_w, back_w, norms)


def layer_backward(gradient, weights, norms, kept):
    rows, width = gradient.shape
    cell = 4 * rows
    qkv_w, out_w, in_w, back_w = weights
    share = out_w.shape[1]
    per_device = share // HD
    units = in_w.shape[1]
    f32, low = jnp.float32, jnp.bfloat16
    shapes = [
        ((rows, width), f32),
        ((width, 4 * share + 2 * units), low),
        ((4, width), f32),
    ]
    flops = 4 * cell * width * (4 * share + 2 * units) + 10 * cell * cell * share
    return pl.pallas_call(
        backward_kernel,
        out_shape=[jax.ShapeDtypeStruct(*s) for s in shapes],
        in_specs=in_vmem(6 + len(kept)),
        out_specs=in_vmem(len(shapes)),
        scratch_shapes=[
            pltpu.VMEM((cell, width), low),
            pltpu.VMEM((cell, units), low),
            pltpu.VMEM((cell, width), low),
            pltpu.VMEM((per_device, cell, HD), low),
            pltpu.VMEM((per_device, cell, cell), low),
            pltpu.VMEM((per_device, cell, cell), low),
            pltpu.VMEM((cell, 3 * share), low),
            pltpu.VMEM((3 * per_device, cell, HD), low),
            pltpu.VMEM((rows, width), f32),
        ]
        + exchange_scratch(rows, width),
        compiler_params=kernel_params(2),
        cost_estimate=pl.CostEstimate(
            flops=flops, bytes_accessed=150_000_000, transcendentals=cell * cell * per_device
        ),
        name="layer_backward",
    )(gradient, qkv_w, out_w, in_w, back_w, norms, *kept)


def fast_body(
    gene_ids,
    levels,
    study_of_cell,
    cotangent,
    tables,
    table_moments,
    level_table,
    level_moments,
    qkv_weight,
    qkv_moments,
    out_weight,
    out_moments,
    in_weight,
    in_moments,
    back_weight,
    back_moments,
    norm_params,
    norm_moments,
):
    low = jnp.bfloat16
    groups = lax.axis_size("dp")
    members = lax.axis_size("mp")
    member = lax.axis_index("mp")
    rows_here, width = cotangent.shape
    layers = qkv_weight.shape[0]
    local_cells = study_of_cell.shape[0]
    capacity = 2 * rows_here // groups
    own_rows = tables.shape[1]
    block_size = own_rows * members
    depth = qkv_weight.shape[2]
    share = width // members
    units = in_weight.shape[2]

    qkv_mine = lax.dynamic_slice_in_dim(qkv_weight, member * share, share, axis=3).astype(low)
    qkv_mine = qkv_mine.transpose(0, 2, 1, 3).reshape(layers, depth, 3 * share)
    out_turned = lax.all_to_all(
        out_weight.astype(low), "dp", split_axis=2, concat_axis=1, tiled=True
    )
    out_mine = lax.dynamic_slice_in_dim(out_turned, member * share, share, axis=1)
    out_mine = out_mine.transpose(0, 2, 1)
    in_mine = in_weight.astype(low)
    back_mine = back_weight.astype(low).transpose(0, 2, 1)

    def spread(pieces):
        whole = lax.all_gather(jnp.concatenate(pieces, axis=1), "dp", axis=0, tiled=True)
        ends, start = [], 0
        for piece in pieces:
            ends.append(whole[:, start : start + piece.shape[1]])
            start += piece.shape[1]
        return ends

    weights = []
    for layer in range(layers):
        if layer == 0:
            pair = spread([qkv_mine[layer], out_mine[layer]])
            pair += spread([in_mine[layer], back_mine[layer]])
            weights.append(pair)
        else:
            weights.append(
                spread([qkv_mine[layer], out_mine[layer], in_mine[layer], back_mine[layer]])
            )

    study_onehot = (study_of_cell[:, None] == jnp.arange(STUDY_TOTAL)[None, :]).astype(jnp.float32)
    level_full = lax.all_gather(level_table.astype(low), "dp", axis=0, tiled=True)
    small = jnp.concatenate(
        [norm_params.reshape(-1), jnp.sum(study_onehot, axis=0)]
    )
    small_all = lax.all_gather(small, "dp", axis=0)
    cells_per_study = jnp.sum(small_all[:, -STUDY_TOTAL:], axis=0)
    norm_full = (
        small_all[:, :-STUDY_TOTAL]
        .reshape(groups, layers, -1)
        .transpose(1, 0, 2)
        .reshape(layers, 4, width)
    )
    cell_balance_weight = (
        groups
        * local_cells
        / (STUDY_TOTAL * jnp.dot(study_onehot, cells_per_study, precision=largest_value))
    )

    summed_tables = jnp.sum(tables, axis=0).astype(low)
    table_rows = lax.all_gather(summed_tables, "mp", axis=0, tiled=True)
    row_owner = gene_ids // block_size
    slot_index = slots_of(row_owner)
    sent_ids = slotted_ids(gene_ids, row_owner, slot_index, groups, capacity)
    asked_ids = lax.all_to_all(sent_ids, "dp", split_axis=0, concat_axis=0, tiled=True)
    present = asked_ids >= 0
    safe_row = jnp.where(present, asked_ids - lax.axis_index("dp") * block_size, 0)
    found_rows = jnp.where(present[..., None], jnp.take(table_rows, safe_row, axis=0), 0)
    returned = lax.all_to_all(found_rows, "dp", split_axis=0, concat_axis=0, tiled=True)
    code = row_owner * capacity + slot_index
    slot_hot = (code[:, None] == jnp.arange(groups * capacity)[None, :]).astype(low)
    gene_part = jnp.dot(
        slot_hot, returned.reshape(groups * capacity, width), preferred_element_type=jnp.float32
    )
    level_hot = (levels[:, None] == jnp.arange(level_full.shape[0])[None, :]).astype(low)
    hidden = gene_part + jnp.dot(level_hot, level_full, preferred_element_type=jnp.float32)

    kept = []
    for layer in range(layers):
        hidden, *saved = layer_forward(hidden, weights[layer], norm_full[layer])
        kept.append(saved)

    gradient = cotangent * cell_balance_weight[0]
    sums = [None] * layers
    norm_grads = [None] * layers
    for layer in reversed(range(layers)):
        gradient, grads, norm_grads[layer] = layer_backward(
            gradient, weights[layer], norm_full[layer], kept[layer]
        )
        sums[layer] = lax.psum_scatter(grads, "dp", scatter_dimension=0, tiled=True)

    slots = jnp.dot(slot_hot.T, gradient.astype(low), preferred_element_type=low)
    arrived = lax.all_to_all(
        slots.reshape(groups, capacity, width), "dp", split_axis=0, concat_axis=0, tiled=True
    )
    arrived_all = lax.all_gather(arrived.reshape(-1, width), "mp", axis=0, tiled=True)
    asked_all = lax.all_gather(asked_ids.reshape(-1), "mp", axis=0, tiled=True)
    first_row = lax.axis_index("dp") * block_size + member * own_rows
    row_hot = (asked_all[None, :] == first_row + jnp.arange(own_rows)[:, None]).astype(low)
    row_grad = jnp.dot(row_hot, arrived_all, preferred_element_type=jnp.float32)
    hits = jnp.sum(row_hot.astype(jnp.float32), axis=1)
    level_grad = jnp.dot(level_hot.astype(jnp.float32).T, gradient, precision=largest_value)

    small_grads = jnp.concatenate(
        [level_grad, jnp.stack(norm_grads).reshape(-1, width)], axis=0
    ).astype(low)
    small_sum = lax.psum(small_grads, ("dp", "mp")).astype(jnp.float32)
    place = lax.axis_index("dp")
    level_rows = level_table.shape[0]
    level_sum = lax.dynamic_slice_in_dim(small_sum, place * level_rows, level_rows, axis=0)
    columns = norm_params.shape[1]
    norm_sum = lax.dynamic_slice_in_dim(
        small_sum[level_full.shape[0] :].reshape(layers, -1), place * columns, columns, axis=1
    )

    stacked = jnp.stack(sums)
    mixing = lax.all_gather(stacked[:, :, : 4 * share], "mp", axis=0)
    qkv_sum = (
        mixing[..., : 3 * share]
        .reshape(members, layers, depth, 3, share)
        .transpose(1, 3, 2, 0, 4)
        .reshape(layers, 3, depth, width)
        .astype(jnp.float32)
    )
    out_cols = mixing[..., 3 * share :].transpose(1, 2, 0, 3).reshape(layers, depth, width)
    out_rows = lax.all_to_all(out_cols, "dp", split_axis=2, concat_axis=1, tiled=True)
    out_sum = out_rows.transpose(0, 2, 1).astype(jnp.float32)
    in_sum = stacked[:, :, 4 * share : 4 * share + units].astype(jnp.float32)
    back_sum = stacked[:, :, 4 * share + units :].transpose(0, 2, 1).astype(jnp.float32)

    touched = (hits > 0)[None, :, None]
    table_grad = jnp.broadcast_to(row_grad[None], tables.shape)
    table_new, table_state = adam_step(tables, table_moments, table_grad, rate_table, decay_rate)
    table_new = jnp.where(touched, table_new, tables)
    table_state = jnp.where(touched[None], table_state, table_moments)
    level_new, level_state = adam_step(
        level_table, level_moments, level_sum, rate_table, decay_rate
    )
    qkv_new, qkv_state = adam_step(qkv_weight, qkv_moments, qkv_sum, rate_dense, decay_rate)
    out_new, out_state = adam_step(out_weight, out_moments, out_sum, rate_mixing, decay_rate)
    in_new, in_state = adam_step(in_weight, in_moments, in_sum, rate_dense, decay_rate)
    back_new, back_state = adam_step(back_weight, back_moments, back_sum, rate_dense, decay_rate)
    norm_new, norm_state = adam_step(norm_params, norm_moments, norm_sum, rate_norm, 0.0)
    return (
        hidden,
        table_new,
        table_state,
        level_new,
        level_state,
        qkv_new,
        qkv_state,
        out_new,
        out_state,
        in_new,
        in_state,
        back_new,
        back_state,
        norm_new,
        norm_state,
    )


def solution(mesh):
    return jax.shard_map(
        fast_body if mesh.shape["mp"] == 4 else general_body,
        mesh=mesh,
        in_specs=(
            P(("dp", "mp")),
            P(("dp", "mp")),
            P("dp"),
            P(("dp", "mp"), None),
            P(None, ("dp", "mp"), None),
            P(None, None, ("dp", "mp"), None),
            P("dp", None),
            P(None, "dp", None),
            P(None, None, "dp", None),
            P(None, None, None, "dp", None),
            P(None, "dp", None),
            P(None, None, "dp", None),
            P(None, "dp", "mp"),
            P(None, None, "dp", "mp"),
            P(None, "mp", "dp"),
            P(None, None, "mp", "dp"),
            P(None, "dp"),
            P(None, None, "dp"),
        ),
        out_specs=(
            P(("dp", "mp"), None),
            P(None, ("dp", "mp"), None),
            P(None, None, ("dp", "mp"), None),
            P("dp", None),
            P(None, "dp", None),
            P(None, None, "dp", None),
            P(None, None, None, "dp", None),
            P(None, "dp", None),
            P(None, None, "dp", None),
            P(None, "dp", "mp"),
            P(None, None, "dp", "mp"),
            P(None, "mp", "dp"),
            P(None, None, "mp", "dp"),
            P(None, "dp"),
            P(None, None, "dp"),
        ),
        check_vma=False,
    )
```

```python
import math
from functools import partial

import jax
import jax.numpy as jnp
from jax import lax
from jax.experimental import pallas as pl
from jax.experimental.pallas import tpu as pltpu
from jax.sharding import PartitionSpec as P

HEADS = 12
HD = 64
STUDY_TOTAL = 16
STEP = 10


largest_value = lax.Precision.HIGHEST
beta_one = 0.9
beta_two = 0.999
adam_eps = 1e-08
norm_eps = 1e-05
rate_dense = 0.08
rate_mixing = 0.3
rate_table = 0.6
rate_norm = 0.4
decay_rate = 0.01


def spread_rows(rows):
    return lax.all_gather(rows, "mp", axis=0, tiled=True)


def summed_rows(term, count):
    return lax.psum_scatter(
        term(jnp.int32(0), count * lax.axis_size("mp")).astype(jnp.bfloat16),
        "mp",
        scatter_dimension=0,
        tiled=True,
    ).astype(jnp.float32)


def norm_forward(rows, gain, bias):
    centered = rows - jnp.mean(rows, axis=-1, keepdims=True)
    inverse = lax.rsqrt(jnp.mean(centered * centered, axis=-1, keepdims=True) + norm_eps)
    normal = centered * inverse
    return (normal * gain + bias, normal, inverse)


def norm_backward(gradient, normal, inverse, gain):
    scaled = gradient * gain
    inner_part = (
        scaled
        - jnp.mean(scaled, axis=-1, keepdims=True)
        - normal * jnp.mean(scaled * normal, axis=-1, keepdims=True)
    )
    return (inner_part * inverse, jnp.sum(gradient * normal, axis=0), jnp.sum(gradient, axis=0))


def gelu_grad(inner, gradient):
    return jax.vjp(partial(jax.nn.gelu, approximate=False), inner)[1](gradient)[0]


def head_major(rows):
    return rows.reshape(rows.shape[0], HEADS, HD).transpose(1, 0, 2)


def row_major(heads):
    return heads.transpose(1, 0, 2).reshape(heads.shape[1], HEADS * HD)


def attend_forward(query, keys, values):
    scale = HD ** (-0.5)

    def one_head(pieces):
        head_query, head_keys, head_values = pieces
        scores = (
            jnp.einsum("qd,kd->qk", head_query, head_keys, preferred_element_type=jnp.float32)
            * scale
        )
        peak = jnp.max(scores, axis=-1, keepdims=True)
        raised = jnp.exp(scores - peak)
        total = jnp.sum(raised, axis=-1, keepdims=True)
        probs = (raised / total).astype(jnp.bfloat16)
        mixed = jnp.dot(probs, head_values, preferred_element_type=jnp.float32).astype(jnp.bfloat16)
        return (mixed, (peak + jnp.log(total))[:, 0])

    mixed, log_total = lax.map(one_head, (head_major(query), head_major(keys), head_major(values)))
    return (row_major(mixed), log_total)


def attend_backward(query, keys, values, mixed_grad, log_total):
    scale = HD ** (-0.5)

    def one_head(pieces):
        head_query, head_keys, head_values, head_grad, head_total = pieces
        scores = (
            jnp.einsum("qd,kd->qk", head_query, head_keys, preferred_element_type=jnp.float32)
            * scale
        )
        probs = jnp.exp(scores - head_total[:, None])
        product = jnp.einsum(
            "qd,kd->qk", head_grad, head_values, preferred_element_type=jnp.float32
        )
        center = jnp.sum(probs * product, axis=-1, keepdims=True)
        score_grad = (probs * (product - center)).astype(jnp.bfloat16)
        query_grad = (
            jnp.dot(score_grad, head_keys, preferred_element_type=jnp.float32) * scale
        ).astype(jnp.bfloat16)
        key_grad = (
            jnp.einsum("qk,qd->kd", score_grad, head_query, preferred_element_type=jnp.float32)
            * scale
        )
        value_grad = jnp.einsum(
            "qk,qd->kd", probs.astype(jnp.bfloat16), head_grad, preferred_element_type=jnp.float32
        )
        return (query_grad, key_grad, value_grad)

    query_grad, key_grad, value_grad = lax.map(
        one_head,
        (
            head_major(query),
            head_major(keys),
            head_major(values),
            head_major(mixed_grad),
            log_total,
        ),
    )
    return (row_major(query_grad), jnp.stack([row_major(key_grad), row_major(value_grad)], axis=1))


def slots_of(row_owner):
    place = jnp.arange(row_owner.shape[0])
    earlier = (row_owner[:, None] == row_owner[None, :]) & (place[None, :] < place[:, None])
    return jnp.sum(earlier.astype(jnp.int32), axis=1)


def slotted_ids(gene_ids, row_owner, slot_index, cell_groups, capacity):
    code = row_owner * capacity + slot_index
    hot = code[None, :] == jnp.arange(cell_groups * capacity)[:, None]
    found = jnp.sum(jnp.where(hot, gene_ids[None, :] + 1, 0), axis=1) - 1
    return found.reshape(cell_groups, capacity)


def adam_step(weight, moments, gradient, rate, decay):
    first = beta_one * moments[0] + (1.0 - beta_one) * gradient
    second = beta_two * moments[1] + (1.0 - beta_two) * gradient * gradient
    first_hat = first / (1.0 - beta_one**STEP)
    second_hat = second / (1.0 - beta_two**STEP)
    new_weight = weight - rate * (first_hat / (jnp.sqrt(second_hat) + adam_eps) + decay * weight)
    return (new_weight, jnp.stack([first, second]))


def general_body(
    gene_ids,
    levels,
    study_of_cell,
    cotangent,
    tables,
    table_moments,
    level_table,
    level_moments,
    qkv_weight,
    qkv_moments,
    out_weight,
    out_moments,
    in_weight,
    in_moments,
    back_weight,
    back_moments,
    norm_params,
    norm_moments,
):
    cell_groups = lax.axis_size("dp")
    rows_here = cotangent.shape[0]
    model_width = cotangent.shape[1]
    layers = qkv_weight.shape[0]
    local_cells = study_of_cell.shape[0]
    capacity = 2 * rows_here // cell_groups
    own_rows = tables.shape[1]
    block_size = own_rows * lax.axis_size("mp")
    qkv_full, out_full, in_part, back_part, level_full = (
        lax.all_gather(qkv_weight.astype(jnp.bfloat16), "dp", axis=2, tiled=True),
        lax.all_gather(out_weight.astype(jnp.bfloat16), "dp", axis=1, tiled=True),
        lax.all_gather(in_weight.astype(jnp.bfloat16), "dp", axis=1, tiled=True),
        lax.all_gather(back_weight.astype(jnp.bfloat16), "dp", axis=2, tiled=True),
        lax.all_gather(level_table.astype(jnp.bfloat16), "dp", axis=0, tiled=True),
    )
    study_onehot = (study_of_cell[:, None] == jnp.arange(STUDY_TOTAL)[None, :]).astype(jnp.float32)
    norm_full, study_all = (
        lax.all_gather(norm_params, "dp", axis=1, tiled=True),
        lax.all_gather(study_onehot, "dp", axis=0, tiled=True),
    )
    cells_per_study = jnp.sum(study_all, axis=0)
    cell_balance_weight = (
        cell_groups
        * local_cells
        / (STUDY_TOTAL * jnp.dot(study_onehot, cells_per_study, precision=largest_value))
    )
    out_grad = cotangent * cell_balance_weight[0]
    summed_tables = jnp.sum(tables, axis=0).astype(jnp.bfloat16)
    table_rows = lax.all_gather(summed_tables, "mp", axis=0, tiled=True)
    row_owner = gene_ids // block_size
    slot_index = slots_of(row_owner)
    sent_ids = slotted_ids(gene_ids, row_owner, slot_index, cell_groups, capacity)
    asked_ids = lax.all_to_all(sent_ids, "dp", split_axis=0, concat_axis=0, tiled=True)
    present = asked_ids >= 0
    safe_row = jnp.where(present, asked_ids - lax.axis_index("dp") * block_size, 0)
    found_rows = jnp.where(present[..., None], jnp.take(table_rows, safe_row, axis=0), 0)
    returned = lax.all_to_all(found_rows, "dp", split_axis=0, concat_axis=0, tiled=True)
    gene_part = returned[row_owner, slot_index].astype(jnp.float32)
    level_hot = (levels[:, None] == jnp.arange(level_full.shape[0])[None, :]).astype(jnp.bfloat16)
    hidden = gene_part + jnp.dot(level_hot, level_full, preferred_element_type=jnp.float32)
    kept = []
    for layer in range(layers):
        norm_row = norm_full[layer]
        tokens_low = hidden.astype(jnp.bfloat16)
        projected = jnp.einsum(
            "td,cdh->tch", tokens_low, qkv_full[layer], preferred_element_type=jnp.float32
        ).astype(jnp.bfloat16)
        query = projected[:, 0]
        cell_rows = spread_rows(projected[:, 1:])
        keys, values = (cell_rows[:, 0], cell_rows[:, 1])
        mixed, log_total = attend_forward(query, keys, values)
        attention = jnp.dot(mixed, out_full[layer], preferred_element_type=jnp.float32)
        first, first_normal, first_inverse = norm_forward(
            hidden + attention, norm_row[:model_width], norm_row[model_width : 2 * model_width]
        )
        first_low = first.astype(jnp.bfloat16)
        in_layer, back_layer = (in_part[layer], back_part[layer])
        first_spread = spread_rows(first_low)
        inner = jnp.dot(first_spread, in_layer, preferred_element_type=jnp.float32)
        active = jax.nn.gelu(inner, approximate=False).astype(jnp.bfloat16)

        def feed_term(start, count):
            return jnp.dot(active, back_layer, preferred_element_type=jnp.float32)

        feed = summed_rows(feed_term, rows_here)
        second, second_normal, second_inverse = norm_forward(
            first + feed, norm_row[2 * model_width : 3 * model_width], norm_row[3 * model_width :]
        )
        kept.append(
            (
                tokens_low,
                query,
                keys,
                values,
                mixed,
                log_total,
                first_normal,
                first_inverse,
                first_spread,
                inner,
                active,
                in_layer,
                back_layer,
                second_normal,
                second_inverse,
            )
        )
        hidden = second
    gradient = out_grad
    qkv_grads = [None] * layers
    out_grads = [None] * layers
    in_grads = [None] * layers
    back_grads = [None] * layers
    norm_grads = [None] * layers
    for layer in reversed(range(layers)):
        (
            tokens_low,
            query,
            keys,
            values,
            mixed,
            log_total,
            first_normal,
            first_inverse,
            first_spread,
            inner,
            active,
            in_layer,
            back_layer,
            second_normal,
            second_inverse,
        ) = kept[layer]
        norm_row = norm_full[layer]
        grad_second, gain_two, bias_two = norm_backward(
            gradient, second_normal, second_inverse, norm_row[2 * model_width : 3 * model_width]
        )
        feed_low = grad_second.astype(jnp.bfloat16)
        feed_spread = spread_rows(feed_low)
        back_grads[layer] = jnp.einsum(
            "tf,td->fd", active, feed_spread, preferred_element_type=jnp.float32
        )
        active_grad = jnp.einsum(
            "td,fd->tf", feed_spread, back_layer, preferred_element_type=jnp.float32
        )
        inner_grad = gelu_grad(inner, active_grad).astype(jnp.bfloat16)
        in_grads[layer] = jnp.einsum(
            "td,tf->df", first_spread, inner_grad, preferred_element_type=jnp.float32
        )

        def first_term(start, count):
            return jnp.einsum("tf,df->td", inner_grad, in_layer, preferred_element_type=jnp.float32)

        first_grad = summed_rows(first_term, rows_here)
        grad_first, gain_one, bias_one = norm_backward(
            grad_second + first_grad, first_normal, first_inverse, norm_row[:model_width]
        )
        norm_grads[layer] = jnp.concatenate([gain_one, bias_one, gain_two, bias_two])
        attention_low = grad_first.astype(jnp.bfloat16)
        out_grads[layer] = jnp.einsum(
            "th,td->hd", mixed, attention_low, preferred_element_type=jnp.float32
        )
        mixed_grad = jnp.einsum(
            "td,hd->th", attention_low, out_full[layer], preferred_element_type=jnp.float32
        ).astype(jnp.bfloat16)
        query_grad, pair_partial = attend_backward(query, keys, values, mixed_grad, log_total)
        pair_grad = lax.psum_scatter(
            pair_partial.astype(jnp.bfloat16), "mp", scatter_dimension=0, tiled=True
        )
        stacked = jnp.concatenate([query_grad[:, None, :], pair_grad], axis=1)
        qkv_grads[layer] = jnp.einsum(
            "td,tch->cdh", tokens_low, stacked, preferred_element_type=jnp.float32
        )
        gradient = grad_first + jnp.einsum(
            "tch,cdh->td", stacked, qkv_full[layer], preferred_element_type=jnp.float32
        )
    level_grad = jnp.dot(level_hot.astype(jnp.float32).T, gradient, precision=largest_value)
    grad_slots = (
        jnp.zeros((cell_groups, capacity, model_width), jnp.float32)
        .at[row_owner, slot_index]
        .set(gradient)
    )
    arrived = lax.all_to_all(
        grad_slots.astype(jnp.bfloat16), "dp", split_axis=0, concat_axis=0, tiled=True
    ).astype(grad_slots.dtype)
    arrived = jnp.where(present[..., None], arrived, 0.0)
    flat_rows = safe_row.reshape(-1)
    block_grad = jax.ops.segment_sum(
        arrived.reshape(-1, model_width), flat_rows, num_segments=block_size
    )
    block_hits = jax.ops.segment_sum(
        present.reshape(-1).astype(jnp.float32), flat_rows, num_segments=block_size
    )
    row_grad, hits = (
        lax.psum_scatter(
            block_grad.astype(jnp.bfloat16), "mp", scatter_dimension=0, tiled=True
        ).astype(jnp.float32),
        lax.psum_scatter(
            block_hits.astype(jnp.bfloat16), "mp", scatter_dimension=0, tiled=True
        ).astype(jnp.float32),
    )
    qkv_sum, out_sum, in_sum, back_sum, level_sum, norm_sum = (
        lax.psum_scatter(
            jnp.stack(qkv_grads).astype(jnp.bfloat16), "dp", scatter_dimension=2, tiled=True
        ).astype(jnp.float32),
        lax.psum_scatter(
            jnp.stack(out_grads).astype(jnp.bfloat16), "dp", scatter_dimension=1, tiled=True
        ).astype(jnp.float32),
        lax.psum_scatter(
            jnp.stack(in_grads).astype(jnp.bfloat16), "dp", scatter_dimension=1, tiled=True
        ).astype(jnp.float32),
        lax.psum_scatter(
            jnp.stack(back_grads).astype(jnp.bfloat16), "dp", scatter_dimension=2, tiled=True
        ).astype(jnp.float32),
        lax.psum_scatter(
            level_grad.astype(jnp.bfloat16), "dp", scatter_dimension=0, tiled=True
        ).astype(jnp.float32),
        lax.psum_scatter(
            jnp.stack(norm_grads).astype(jnp.bfloat16), "dp", scatter_dimension=1, tiled=True
        ).astype(jnp.float32),
    )
    qkv_sum, out_sum, level_sum, norm_sum = (
        lax.psum(qkv_sum.astype(jnp.bfloat16), "mp").astype(jnp.float32),
        lax.psum(out_sum.astype(jnp.bfloat16), "mp").astype(jnp.float32),
        lax.psum(level_sum.astype(jnp.bfloat16), "mp").astype(jnp.float32),
        lax.psum(norm_sum.astype(jnp.bfloat16), "mp").astype(jnp.float32),
    )
    touched = (hits > 0)[None, :, None]
    table_grad = jnp.broadcast_to(row_grad[None], tables.shape)
    table_new, table_state = adam_step(tables, table_moments, table_grad, rate_table, decay_rate)
    table_new = jnp.where(touched, table_new, tables)
    table_state = jnp.where(touched[None], table_state, table_moments)
    level_new, level_state = adam_step(
        level_table, level_moments, level_sum, rate_table, decay_rate
    )
    qkv_new, qkv_state = adam_step(qkv_weight, qkv_moments, qkv_sum, rate_dense, decay_rate)
    out_new, out_state = adam_step(out_weight, out_moments, out_sum, rate_mixing, decay_rate)
    in_new, in_state = adam_step(in_weight, in_moments, in_sum, rate_dense, decay_rate)
    back_new, back_state = adam_step(back_weight, back_moments, back_sum, rate_dense, decay_rate)
    norm_new, norm_state = adam_step(norm_params, norm_moments, norm_sum, rate_norm, 0.0)
    return (
        hidden,
        table_new,
        table_state,
        level_new,
        level_state,
        qkv_new,
        qkv_state,
        out_new,
        out_state,
        in_new,
        in_state,
        back_new,
        back_state,
        norm_new,
        norm_state,
    )


MESH = pl.DeviceIdType.MESH
SIB, FACE = 0, 1
TILE = 128


def nn(a, b):
    return lax.dot_general(a, b, (((1,), (0,)), ((), ())), preferred_element_type=jnp.float32)


def nt(a, b):
    return lax.dot_general(a, b, (((1,), (1,)), ((), ())), preferred_element_type=jnp.float32)


def tn(a, b):
    return lax.dot_general(a, b, (((0,), (0,)), ((), ())), preferred_element_type=jnp.float32)


def near_devices():
    group, member = lax.axis_index("dp"), lax.axis_index("mp")
    core = member % 2
    return (group, member + 1 - 2 * core), (group, (member + 2) % 4)


def greet(peers):
    barrier = pltpu.get_barrier_semaphore()
    for peer in peers:
        pl.semaphore_signal(barrier, inc=1, device_id=peer, device_id_type=MESH)
    pl.semaphore_wait(barrier, len(peers))


def send(source, target, sems, index, peer):
    copy = pltpu.make_async_remote_copy(
        src_ref=source,
        dst_ref=target,
        send_sem=sems[0].at[index],
        recv_sem=sems[1].at[index],
        device_id=peer,
        device_id_type=MESH,
    )
    copy.start()
    return copy


GATHER_COPIES = 5
SUM_COPIES = 3


def columns_of(group):
    return group // 2, group % 2


def group_peers():
    group, member = lax.axis_index("dp"), lax.axis_index("mp")
    count = lax.axis_size("dp")
    return [((group + k) % count, member) for k in range(1, count)]


def mates():
    group, member = lax.axis_index("dp"), lax.axis_index("mp")
    count = lax.axis_size("mp")
    return [(group, (member + k) % count) for k in range(1, count)]


class Spread:
    def __init__(self, parts, sems):
        group, member = lax.axis_index("dp"), lax.axis_index("mp")
        depth = lax.axis_size("dp") // 2
        z, x = columns_of(group)
        self.beside = (group + 1 - 2 * x, member)
        self.depth, self.sems, self.parts = depth, sems, parts
        self.came = [((z + depth - k) % depth) * 2 + x for k in range(1, depth)]
        self.along, self.own, self.handed = [], [], []
        for p, (mine, whole) in enumerate(parts):
            whole[group] = mine[...]
            self.along.append(
                [
                    send(mine, whole.at[group], sems, (p, k - 1), (((z + k) % depth) * 2 + x, member))
                    for k in range(1, depth)
                ]
            )
            self.own.append(send(mine, whole.at[group], sems, (p, depth - 1), self.beside))

    def hand_on(self):
        for p, (_, whole) in enumerate(self.parts):
            for k in range(1, self.depth):
                self.along[p][k - 1].wait_recv()
                source = self.came[k - 1]
                self.handed.append(
                    send(
                        whole.at[source],
                        whole.at[source],
                        self.sems,
                        (p, self.depth - 1 + k),
                        self.beside,
                    )
                )

    def finish(self):
        for copy in [*self.own, *self.handed]:
            copy.wait_recv()
        for copy in [*sum(self.along, []), *self.own, *self.handed]:
            copy.wait_send()


def spread_sems(parts):
    copies = 2 * (lax.axis_size("dp") // 2) - 1
    return [pltpu.SemaphoreType.DMA((parts, copies))] * 2


class Reduce:
    def __init__(self, parts, sems):
        group, member = lax.axis_index("dp"), lax.axis_index("mp")
        self.depth = lax.axis_size("dp") // 2
        self.z, self.x = columns_of(group)
        self.member, self.parts, self.sems = member, parts, sems
        beside = (group + 1 - 2 * self.x, member)
        self.first = [
            send(source.at[:, 1 - self.x], near, sems, (p, 0), beside)
            for p, (source, near, _, _) in enumerate(parts)
        ]
        self.along = []

    def middle(self):
        for p, (source, near, sent, come) in enumerate(self.parts):
            self.first[p].wait_recv()
            for k in range(1, self.depth):
                z = (self.z + k) % self.depth
                term = source[z, self.x].astype(jnp.float32) + near[z].astype(jnp.float32)
                sent[k - 1] = term.astype(sent.dtype)
                self.along.append(
                    send(
                        sent.at[k - 1],
                        come.at[k - 1],
                        self.sems,
                        (p, k),
                        (z * 2 + self.x, self.member),
                    )
                )

    def finish(self):
        totals = []
        for copy in self.along:
            copy.wait_recv()
        for source, near, _, come in self.parts:
            term = source[self.z, self.x].astype(jnp.float32) + near[self.z].astype(jnp.float32)
            for k in range(1, self.depth):
                term = term + come[k - 1].astype(jnp.float32)
            totals.append(term)
        for copy in [*self.first, *self.along]:
            copy.wait_send()
        return totals


def reduce_sems(parts):
    return [pltpu.SemaphoreType.DMA((parts, lax.axis_size("dp") // 2))] * 2


def reduce_scratch(rows, columns, dtype):
    depth = lax.axis_size("dp") // 2
    return [
        pltpu.VMEM((depth, rows, columns), dtype),
        pltpu.VMEM((depth - 1, rows, columns), dtype),
        pltpu.VMEM((depth - 1, rows, columns), dtype),
    ]


class MixReduce:
    def __init__(self, source, near, sent, come, sems):
        group, member = lax.axis_index("dp"), lax.axis_index("mp")
        self.depth = lax.axis_size("dp") // 2
        self.z, self.x = columns_of(group)
        self.member, self.sems = member, sems
        self.source, self.near, self.sent, self.come = source, near, sent, come
        beside = (group + 1 - 2 * self.x, member)
        self.first = send(source.at[1 - self.x], near, sems, 0, beside)

    def copy(self):
        slot = (self.member + self.depth - self.z + self.depth - 1) % self.depth
        return pltpu.make_async_remote_copy(
            src_ref=self.sent,
            dst_ref=self.come.at[slot],
            send_sem=self.sems[0].at[1 + slot],
            recv_sem=self.sems[1].at[1 + slot],
            device_id=(self.member * 2 + self.x, self.member),
            device_id_type=MESH,
        )

    def middle(self):
        self.first.wait_recv()
        term = self.source[self.x].astype(jnp.float32) + self.near[...].astype(jnp.float32)
        self.sent[...] = term.astype(self.sent.dtype)

        @pl.when(self.z != self.member)
        def _():
            self.copy().start()

    def finish(self):
        @pl.when(self.z == self.member)
        def _():
            for slot in range(self.depth - 1):
                pltpu.make_async_remote_copy(
                    src_ref=self.sent,
                    dst_ref=self.come.at[slot],
                    send_sem=self.sems[0].at[1 + slot],
                    recv_sem=self.sems[1].at[1 + slot],
                    device_id=((self.member * 2 + self.x + 2) % (2 * self.depth), self.member),
                    device_id_type=MESH,
                ).wait_recv()

        @pl.when(self.z != self.member)
        def _():
            self.copy().wait_send()

        self.first.wait_send()

    def total(self):
        term = self.source[self.x].astype(jnp.float32) + self.near[...].astype(jnp.float32)
        for slot in range(self.depth - 1):
            term = term + self.come[slot].astype(jnp.float32)
        return term


def mix_reduce_scratch(rows, columns, dtype):
    depth = lax.axis_size("dp") // 2
    return [
        pltpu.VMEM((rows, columns), dtype),
        pltpu.VMEM((rows, columns), dtype),
        pltpu.VMEM((depth - 1, rows, columns), dtype),
    ] + [pltpu.SemaphoreType.DMA((depth,))] * 2


class Gather:
    def __init__(self, buf, sems, sib, face):
        self.buf, self.sems, self.sib = buf, sems, sib
        rows = buf.shape[0] // 4
        half = rows // 2
        self.rows, self.half = rows, half
        self.across = [
            send(
                buf.at[pl.ds(i * half, half)],
                buf.at[pl.ds(2 * rows + i * half, half)],
                sems,
                i,
                face,
            )
            for i in range(2)
        ]
        self.beside = send(buf.at[pl.ds(0, rows)], buf.at[pl.ds(rows, rows)], sems, 2, sib)
        self.handed = []

    def wait_beside(self):
        self.beside.wait_recv()

    def hand_on(self, i):
        self.across[i].wait_recv()
        start = 2 * self.rows + i * self.half
        self.handed.append(
            send(
                self.buf.at[pl.ds(start, self.half)],
                self.buf.at[pl.ds(start + self.rows, self.half)],
                self.sems,
                3 + i,
                self.sib,
            )
        )

    def wait_handed(self):
        for copy in self.handed:
            copy.wait_recv()

    def finish(self):
        for copy in [*self.across, self.beside, *self.handed]:
            copy.wait_send()


class Total:
    def __init__(self, out, into, sems, sib, face):
        self.out, self.into, self.sems = out, into, sems
        self.sib, self.face = sib, face
        self.copies = []

    def give_far(self, term):
        self.out[0] = term.astype(jnp.bfloat16)
        self.copies.append(send(self.out.at[0], self.into.at[0], self.sems, 0, self.sib))

    def give_facing(self, term):
        self.copies[0].wait_recv()
        self.out[1] = (term + self.into[0].astype(jnp.float32)).astype(jnp.bfloat16)
        self.copies.append(send(self.out.at[1], self.into.at[1], self.sems, 1, self.face))

    def give_beside(self, term):
        self.out[2] = term.astype(jnp.bfloat16)
        self.copies.append(send(self.out.at[2], self.into.at[2], self.sems, 2, self.sib))

    def take(self, term):
        for copy in self.copies[1:]:
            copy.wait_recv()
        return term + self.into[2].astype(jnp.float32) + self.into[1].astype(jnp.float32)

    def finish(self):
        for copy in self.copies:
            copy.wait_send()


def gelu_pair(x):
    t = 1.0 / (1.0 + (0.3275911 * 0.7071067811865476) * jnp.abs(x))
    raised = jnp.exp(-0.5 * x * x)
    series = t * (
        0.254829592
        + t * (-0.284496736 + t * (1.421413741 + t * (-1.453152027 + t * 1.061405429)))
    )
    upper = 0.5 * series * raised
    share = jnp.where(x >= 0, 1.0 - upper, upper)
    return x * share, share + x * raised * 0.3989422804014327


def rows_joined(ref):
    blocks = ref[...]
    return blocks.reshape(blocks.shape[0] * blocks.shape[1], blocks.shape[2])


def around(peers):
    group, member = lax.axis_index("dp"), lax.axis_index("mp")
    depth = lax.axis_size("dp") // 2
    z, x = columns_of(group)
    along = [(((z + k) % depth) * 2 + x, member) for k in range(1, depth)]
    return [*peers, *along, (group + 1 - 2 * x, member)]


def forward_kernel(ahead, *refs):
    refs = iter(refs)
    take = lambda count: [next(refs) for _ in range(count)]
    hidden, qkv_w, out_w, in_w, back_w, norms = take(6)
    mine = take(ahead)
    second, second_normal, second_inverse, first_normal, first_inverse = take(5)
    tokens, heads, mixed, logs, firsts, active, slope = take(7)
    whole = take(ahead)
    mixed_t, held, out_a, into_a, out_b, into_b = take(6)
    gather_a, total_a, gather_b, total_b = take(2), take(2), take(2), take(2)
    sib, face = near_devices()
    greet(around([sib, face]) if ahead else [sib, face])
    rows = hidden.shape[0]
    share = mixed.shape[1]
    per_device = share // HD

    def block(b):
        return pl.ds(b * rows, rows)

    tokens[block(0), :] = hidden[...].astype(jnp.bfloat16)
    gather = Gather(tokens, gather_a, sib, face)
    spread = Spread(list(zip(mine, whole)), take(2)) if ahead else None

    def project(b):
        parts = nn(tokens[block(b), :], rows_joined(qkv_w))
        for j in range(3 * per_device):
            piece = parts[:, j * HD : (j + 1) * HD]
            if j < per_device:
                piece = piece * HD ** (-0.5)
            heads[j, block(b), :] = piece.astype(jnp.bfloat16)

    project(0)
    gather.wait_beside()
    project(1)
    gather.hand_on(0)
    gather.hand_on(1)
    project(2)
    gather.wait_handed()
    project(3)

    def attend(b):
        def one_head(h, carry):
            scores = nt(heads[per_device + h], heads[h, block(b), :])
            peak = jnp.max(scores, axis=0, keepdims=True)
            raised = jnp.exp(scores - peak)
            total = jnp.sum(raised, axis=0, keepdims=True)
            result = tn(heads[2 * per_device + h], raised.astype(jnp.bfloat16)) / total
            mixed_t[pl.ds(pl.multiple_of(h * HD, HD), HD), :] = result
            logs[b * per_device + h] = peak + jnp.log(total)
            return carry

        lax.fori_loop(0, per_device, one_head, 0)
        rows_mixed = mixed_t[...].T.astype(jnp.bfloat16)
        mixed[block(b), :] = rows_mixed
        return nn(rows_mixed, rows_joined(out_w))

    total = Total(out_a, into_a, total_a, sib, face)
    total.give_far(attend(3))
    total.give_facing(attend(2))
    total.give_beside(attend(1))
    attention = total.take(attend(0))

    first, normal, inverse = norm_forward(hidden[...] + attention, norms[0:1, :], norms[1:2, :])
    first_normal[...] = normal
    first_inverse[...] = inverse
    firsts[block(0), :] = first.astype(jnp.bfloat16)
    gather_two = Gather(firsts, gather_b, sib, face)
    if ahead:
        spread.hand_on()

    def feed(b):
        value, gradient = gelu_pair(nn(firsts[block(b), :], rows_joined(in_w)))
        value = value.astype(jnp.bfloat16)
        active[block(b), :] = value
        slope[block(b), :] = gradient.astype(jnp.bfloat16)
        return nt(value, rows_joined(back_w))

    total_two = Total(out_b, into_b, total_b, sib, face)
    held[...] = first + feed(0)
    gather_two.wait_beside()
    term_beside = feed(1)
    gather_two.hand_on(0)
    gather_two.hand_on(1)
    term_facing = feed(2)
    gather_two.wait_handed()
    total_two.give_far(feed(3))
    total_two.give_facing(term_facing)
    total_two.give_beside(term_beside)
    summed = total_two.take(held[...])
    result, normal, inverse = norm_forward(summed, norms[2:3, :], norms[3:4, :])
    second[...] = result
    second_normal[...] = normal
    second_inverse[...] = inverse
    gather.finish()
    total.finish()
    gather_two.finish()
    total_two.finish()
    if ahead:
        spread.finish()


def backward_kernel(last, *refs):
    refs = iter(refs)
    take = lambda count: [next(refs) for _ in range(count)]
    gradient, qkv_w, out_w, in_w, back_w, norms = take(6)
    second_normal, second_inverse, first_normal, first_inverse = take(4)
    tokens, heads, mixed, logs, firsts, active, slope = take(7)
    extra = take(1 if last else 2)
    gradient_out, norm_grads, qkv_g, out_g, in_sum, back_sum = take(6)
    prior_sums = take(0 if last else 2)
    feeds, inner, lows, mixed_grad, probs, score_grad, head_grads, pieces, held = take(9)
    in_g, back_g = take(2)
    own_parts = [(in_g, *take(3)), (back_g, *take(3))]
    out_a, into_a, out_b, into_b = take(4)
    gather_a, total_a, gather_b, total_b = take(2), take(2), take(2), take(2)
    own_sems = take(2)
    sib, face = near_devices()
    greet(around([sib, face]))
    rows = gradient.shape[0]
    share = mixed.shape[1]
    per_device = share // HD
    if not last:
        prior = Reduce([(extra[0], *take(3))], take(2))
        prior_mix = MixReduce(extra[1], *take(3), take(2))

    def block(b):
        return pl.ds(b * rows, rows)

    arriving = gradient[...]
    if last:
        arriving = arriving * extra[0][...]
    grad_second, gain, bias = norm_backward(
        arriving, second_normal[...], second_inverse[...], norms[2:3, :]
    )
    norm_grads[2:3, :] = gain[None]
    norm_grads[3:4, :] = bias[None]
    feeds[block(0), :] = grad_second.astype(jnp.bfloat16)
    gather = Gather(feeds, gather_a, sib, face)
    held[...] = grad_second

    def feed(b):
        part = nn(feeds[block(b), :], rows_joined(back_w)) * slope[block(b), :].astype(jnp.float32)
        part = part.astype(jnp.bfloat16)
        inner[block(b), :] = part
        return nt(part, rows_joined(in_w))

    total = Total(out_a, into_a, total_a, sib, face)
    held[...] += feed(0)
    gather.wait_beside()
    term_beside = feed(1)
    gather.hand_on(0)
    gather.hand_on(1)
    term_facing = feed(2)
    gather.wait_handed()
    total.give_far(feed(3))
    total.give_facing(term_facing)
    total.give_beside(term_beside)
    in_g[...] = tn(firsts[...], inner[...]).astype(jnp.bfloat16).reshape(in_g.shape)
    back_g[...] = tn(feeds[...], active[...]).astype(jnp.bfloat16).reshape(back_g.shape)
    if not last:
        prior.middle()
        prior_mix.middle()
    own = Reduce(own_parts, own_sems)
    summed = total.take(held[...])
    grad_first, gain, bias = norm_backward(
        summed, first_normal[...], first_inverse[...], norms[0:1, :]
    )
    norm_grads[0:1, :] = gain[None]
    norm_grads[1:2, :] = bias[None]
    lows[block(0), :] = grad_first.astype(jnp.bfloat16)
    gather_two = Gather(lows, gather_b, sib, face)
    held[...] = grad_first

    def spread(b):
        parts = nt(lows[block(b), :], rows_joined(out_w))
        for j in range(per_device):
            mixed_grad[j, block(b), :] = parts[:, j * HD : (j + 1) * HD].astype(jnp.bfloat16)

    def score(b):
        def one_head(h, carry):
            scores = nt(heads[per_device + h], heads[h, block(b), :])
            prob = jnp.exp(scores - logs[b * per_device + h])
            product = nt(heads[2 * per_device + h], mixed_grad[h, block(b), :])
            center = jnp.sum(prob * product, axis=0, keepdims=True)
            score_grad[h, :, block(b)] = (prob * (product - center)).astype(jnp.bfloat16)
            probs[h, :, block(b)] = prob.astype(jnp.bfloat16)
            return carry

        lax.fori_loop(0, per_device, one_head, 0)

    spread(0)
    score(0)
    gather_two.wait_beside()
    spread(1)
    score(1)
    gather_two.hand_on(0)
    gather_two.hand_on(1)
    spread(2)
    score(2)
    gather_two.wait_handed()
    spread(3)
    score(3)

    def close(h, carry):
        pieces[per_device + h] = nn(score_grad[h], heads[h]).astype(jnp.bfloat16)
        pieces[2 * per_device + h] = nn(probs[h], mixed_grad[h]).astype(jnp.bfloat16)
        turned = tn(heads[per_device + h], score_grad[h]) * HD ** (-0.5)
        pieces[h] = turned.T.astype(jnp.bfloat16)
        return carry

    lax.fori_loop(0, per_device, close, 0)
    for j in range(3 * per_device):
        head_grads[:, j * HD : (j + 1) * HD] = pieces[j]

    total_two = Total(out_b, into_b, total_b, sib, face)
    weight = rows_joined(qkv_w)
    total_two.give_far(nt(head_grads[block(3), :], weight))
    total_two.give_facing(nt(head_grads[block(2), :], weight))
    total_two.give_beside(nt(head_grads[block(1), :], weight))
    own.middle()
    held[...] += nt(head_grads[block(0), :], weight)
    qkv_g[...] = tn(tokens[...], head_grads[...]).astype(jnp.bfloat16).reshape(qkv_g.shape)
    out_g[...] = tn(mixed[...], lows[...]).astype(jnp.bfloat16).reshape(out_g.shape)
    gradient_out[...] = total_two.take(held[...])
    if not last:
        prior_sums[0][...] = prior.finish()[0]
        prior_mix.finish()
        prior_sums[1][...] = prior_mix.total()
    gather.finish()
    total.finish()
    gather_two.finish()
    total_two.finish()
    whole_in, whole_back = own.finish()
    in_sum[...] = whole_in
    back_sum[...] = whole_back.T


def start_kernel(*refs):
    refs = iter(refs)
    take = lambda count: [next(refs) for _ in range(count)]
    sent_ids, codes, levels, table_rows, small = take(5)
    mine, out_mine = take(3), take(2)
    hidden, asked, scale = take(3)
    norms = take(2)
    whole, out_whole = take(3), take(2)
    small_all, found, returned, out_a, into_a = take(5)
    total_a, small_sems, spread_sem, out_sems, id_sems, near_sems, row_sems = [take(2) for _ in range(7)]
    group, member = lax.axis_index("dp"), lax.axis_index("mp")
    groups, members = lax.axis_size("dp"), lax.axis_size("mp")
    depth = groups // 2
    z, x = columns_of(group)
    beside = (group + 1 - 2 * x, member)
    peers = group_peers()
    sib, face = near_devices()
    far = (group, (sib[1] + 2) % members)
    greet([*peers, *mates()])

    asked[0, group] = sent_ids[group]
    id_copies = [
        send(sent_ids.at[peer[0]], asked.at[0, group], id_sems, k, peer)
        for k, peer in enumerate(peers)
    ]
    small_spread = Spread([(small, small_all)], small_sems)
    for copy in id_copies:
        copy.wait_recv()
    near_copies = [
        send(asked.at[0], asked.at[k + 1], near_sems, k, peer)
        for k, peer in enumerate((sib, face, far))
    ]
    spread = Spread(list(zip(mine, whole)), spread_sem)

    def root_copies():
        return [
            pltpu.make_async_remote_copy(
                src_ref=mine_out,
                dst_ref=target.at[x],
                send_sem=out_sems[0].at[p, k],
                recv_sem=out_sems[1].at[p, 0],
                device_id=(((z + k) % depth) * 2 + x, member),
                device_id_type=MESH,
            )
            for p, (mine_out, target) in enumerate(zip(out_mine, out_whole))
            for k in range(1, depth)
        ]

    @pl.when(z == member)
    def _():
        for copy in root_copies():
            copy.start()
        for mine_out, target in zip(out_mine, out_whole):
            target[x] = mine_out[...]

    for copy in near_copies:
        copy.wait_recv()
    own_rows = table_rows.shape[0]
    first_row = ((group * members + member) * own_rows).astype(jnp.float32)
    capacity = asked.shape[3]

    def lookup(r):
        line = jnp.concatenate([asked[r, c] for c in range(groups)], axis=1).astype(jnp.float32)
        line = jnp.broadcast_to(line - first_row, (8, groups * capacity)).T[:, 0:1]
        place = lax.broadcasted_iota(jnp.int32, (groups * capacity, own_rows), 1)
        hot = (line == place.astype(jnp.float32)).astype(jnp.bfloat16)
        return nn(hot, table_rows[...])

    total = Total(out_a, into_a, total_a, sib, face)
    total.give_far(lookup(3))
    total.give_facing(lookup(2))
    total.give_beside(lookup(1))
    own = lookup(0)
    small_spread.hand_on()
    spread.hand_on()

    @pl.when(z != member)
    def _():
        for p in range(2):
            pltpu.make_async_remote_copy(
                src_ref=out_mine[p],
                dst_ref=out_whole[p].at[x],
                send_sem=out_sems[0].at[p, 0],
                recv_sem=out_sems[1].at[p, 0],
                device_id=beside,
                device_id_type=MESH,
            ).wait_recv()

    out_copies = [
        pltpu.make_async_remote_copy(
            src_ref=target.at[x],
            dst_ref=target.at[x],
            send_sem=out_sems[0].at[p, depth],
            recv_sem=out_sems[1].at[p, 1],
            device_id=beside,
            device_id_type=MESH,
        )
        for p, target in enumerate(out_whole)
    ]
    for copy in out_copies:
        copy.start()
    found[...] = total.take(own).astype(jnp.bfloat16).reshape(found.shape)
    row_copies = [
        send(found.at[peer[0]], returned.at[group], row_sems, k, peer)
        for k, peer in enumerate(peers)
    ]
    returned[group] = found[group]
    small_spread.finish()
    for layer, target in enumerate(norms):
        half = target.shape[1] // 2
        for c in range(groups):
            start = (c % 2) * half
            target[c // 2 : c // 2 + 1, start : start + half] = small_all[
                c, 8:9, layer * half : (layer + 1) * half
            ]
    counts = small_all[0, 9:10, :]
    for c in range(1, groups):
        counts = counts + small_all[c, 9:10, :]
    same = jnp.sum(counts * small[9:10, :], axis=1, keepdims=True)
    scale[...] = groups / (STUDY_TOTAL * same)
    level_rows = 8 * groups
    level_full = jnp.concatenate([small_all[c, 0:8, :] for c in range(groups)], axis=0)
    rows = hidden.shape[0]
    level_place = lax.broadcasted_iota(jnp.int32, (rows, level_rows), 1)
    level_hot = (levels[...] == level_place).astype(jnp.bfloat16)
    level_part = nn(level_hot, level_full.astype(jnp.bfloat16))
    slot_place = lax.broadcasted_iota(jnp.int32, (rows, groups * capacity), 1)
    slot_hot = (codes[...] == slot_place).astype(jnp.bfloat16)
    for copy in row_copies:
        copy.wait_recv()
    hidden[...] = nn(slot_hot, rows_joined(returned)) + level_part

    for copy in [*id_copies, *near_copies, *row_copies]:
        copy.wait_send()
    total.finish()
    spread.finish()
    for copy in out_copies:
        copy.wait()

    @pl.when(z == member)
    def _():
        for copy in root_copies():
            copy.wait_send()


def end_kernel(*refs):
    refs = iter(refs)
    take = lambda count: [next(refs) for _ in range(count)]
    gradient, codes, levels, asked, qkv_g, out_g, norm_zero, norm_one, qkv_one, out_one = take(10)
    row_grad, hits, qkv_sum, out_sum, small_sum = take(5)
    slots, arrived, small_g, small_in, qkv_out, qkv_in, out_out, out_in = take(8)
    qkv_parts, small_parts, mix_parts = take(3), take(3), take(3)
    mix_sems, qkv_sems, small_sems, gather_sems, row_sems, mate_sems = [take(2) for _ in range(6)]
    group, member = lax.axis_index("dp"), lax.axis_index("mp")
    groups, members = lax.axis_size("dp"), lax.axis_size("mp")
    z, x = columns_of(group)
    peers, near = group_peers(), mates()
    sib, face = near_devices()
    greet([*peers, *near])
    rows, width = gradient.shape
    capacity = slots.shape[1]
    count = groups * capacity

    slot_place = lax.broadcasted_iota(jnp.int32, (rows, count), 1)
    slot_hot = (codes[...] == slot_place).astype(jnp.bfloat16)
    high = gradient[...].astype(jnp.bfloat16)
    slots[...] = tn(slot_hot, high).astype(jnp.bfloat16).reshape(slots.shape)
    row_copies = [
        send(slots.at[peer[0]], arrived.at[pl.ds(group * capacity, capacity)], row_sems, k, peer)
        for k, peer in enumerate(peers)
    ]
    arrived[pl.ds(group * capacity, capacity), :] = slots[group]
    qkv_reduce = Reduce([(qkv_g, *qkv_parts)], qkv_sems)
    mix = MixReduce(out_g, *mix_parts, mix_sems)

    level_place = lax.broadcasted_iota(jnp.int32, (rows, 8 * groups), 1)
    level_hot = (levels[...] == level_place).astype(jnp.bfloat16)
    rest = (gradient[...] - high.astype(jnp.float32)).astype(jnp.bfloat16)
    level_grad = tn(level_hot, high) + tn(level_hot, rest)
    half = width // 2
    for c in range(groups):
        small_g[c // 2, c % 2, 0:8, :] = level_grad[c * 8 : (c + 1) * 8, :]
        start = (c % 2) * half
        for layer, source in enumerate((norm_zero, norm_one)):
            small_g[c // 2, c % 2, 8:9, layer * half : (layer + 1) * half] = source[
                c // 2 : c // 2 + 1, start : start + half
            ]
        small_g[c // 2, c % 2, 9:16, :] = jnp.zeros((7, width), jnp.float32)
    small_reduce = Reduce([(small_g, *small_parts)], small_sems)

    for copy in row_copies:
        copy.wait_recv()
    gather = Gather(arrived, gather_sems, sib, face)
    qkv_reduce.middle()
    mix.middle()
    small_reduce.middle()

    own_rows = row_grad.shape[0]
    first_row = (group * members + member) * own_rows

    def collect(r):
        line = jnp.concatenate([asked[r, c] for c in range(groups)], axis=1) - first_row
        place = lax.broadcasted_iota(jnp.int32, (own_rows, count), 0)
        hot = (line == place).astype(jnp.float32)
        part = nn(hot.astype(jnp.bfloat16), arrived[pl.ds(r * count, count), :])
        if r:
            row_grad[...] += part
            hits[...] += jnp.sum(hot, axis=1, keepdims=True)
        else:
            row_grad[...] = part
            hits[...] = jnp.sum(hot, axis=1, keepdims=True)

    collect(0)
    gather.wait_beside()
    collect(1)
    gather.hand_on(0)
    gather.hand_on(1)

    qkv_out[0] = qkv_reduce.finish()[0].astype(jnp.bfloat16)
    qkv_out[1] = qkv_one[...].astype(jnp.bfloat16)
    small_in[member] = small_reduce.finish()[0]
    mix.finish()
    out_out[0] = mix.total().astype(jnp.bfloat16)
    out_out[1] = out_one[...].astype(jnp.bfloat16)
    qkv_in[member] = qkv_out[...]
    mate_copies = []
    for k, mate in enumerate(near):
        mate_copies.append(send(qkv_out, qkv_in.at[member], mate_sems, k, mate))
        mate_copies.append(
            send(small_in.at[member], small_in.at[member], mate_sems, members + k, mate)
        )

    def root_copies(count=members - 1):
        return [
            pltpu.make_async_remote_copy(
                src_ref=out_out,
                dst_ref=out_in,
                send_sem=mate_sems[0].at[2 * members + k],
                recv_sem=mate_sems[1].at[2 * members],
                device_id=near[k],
                device_id_type=MESH,
            )
            for k in range(count)
        ]

    @pl.when(z == member)
    def _():
        for copy in root_copies():
            copy.start()
        out_in[...] = out_out[...]

    collect(2)
    gather.wait_handed()
    collect(3)

    @pl.when(z != member)
    def _():
        root_copies(1)[0].wait_recv()

    for copy in mate_copies:
        copy.wait_recv()
    out_sum[...] = out_in[...].astype(jnp.float32)
    total = small_in[0]
    for m in range(1, members):
        total = total + small_in[m]
    small_sum[...] = total
    share = qkv_out.shape[2] // 3
    for layer in range(2):
        for m in range(members):
            piece = qkv_in[m, layer].astype(jnp.float32)
            for c in range(3):
                qkv_sum[layer, c, :, m * share : (m + 1) * share] = piece[
                    :, c * share : (c + 1) * share
                ]

    for copy in [*row_copies, *mate_copies]:
        copy.wait_send()
    gather.finish()

    @pl.when(z == member)
    def _():
        for copy in root_copies():
            copy.wait_send()


def exchange_scratch(rows, width):
    return [pltpu.VMEM((3, rows, width), jnp.bfloat16) for _ in range(4)] + [
        pltpu.SemaphoreType.DMA((count,))
        for count in (GATHER_COPIES, GATHER_COPIES, SUM_COPIES, SUM_COPIES) * 2
    ]


def run_kernel(kernel, collective_id, name, inputs, outputs, scratch, flops=0, exps=0):
    moved = sum(math.prod(a.shape) * a.dtype.itemsize for a in inputs)
    return pl.pallas_call(
        kernel,
        out_shape=[jax.ShapeDtypeStruct(*o) for o in outputs],
        in_specs=[pl.BlockSpec(memory_space=pltpu.VMEM)] * len(inputs),
        out_specs=[pl.BlockSpec(memory_space=pltpu.VMEM)] * len(outputs),
        scratch_shapes=scratch,
        compiler_params=pltpu.CompilerParams(
            collective_id=collective_id, has_side_effects=True, vmem_limit_bytes=60 * 2**20
        ),
        cost_estimate=pl.CostEstimate(flops=flops, bytes_accessed=moved, transcendentals=exps),
        name=name,
    )(*inputs)


def layer_forward(hidden, weights, norms, ahead):
    rows, width = hidden.shape
    cell = 4 * rows
    qkv_w, out_w, in_w, back_w = weights
    share = out_w.shape[0] * out_w.shape[1]
    per_device = share // HD
    units = in_w.shape[2]
    groups = in_w.shape[0]
    f32, low = jnp.float32, jnp.bfloat16
    outputs = [
        ((rows, width), f32),
        ((rows, width), f32),
        ((rows, 1), f32),
        ((rows, width), f32),
        ((rows, 1), f32),
        ((cell, width), low),
        ((3 * per_device, cell, HD), low),
        ((cell, share), low),
        ((4 * per_device, 1, rows), f32),
        ((cell, width), low),
        ((cell, units), low),
        ((cell, units), low),
    ] + [((groups, *part.shape), low) for part in ahead]
    flops = 2 * cell * width * (4 * share + 2 * units) + 4 * cell * cell * share
    results = run_kernel(
        partial(forward_kernel, len(ahead)),
        1 if ahead else 2,
        "layer_forward",
        [hidden, qkv_w, out_w, in_w, back_w, norms, *ahead],
        outputs,
        [pltpu.VMEM((share, rows), f32), pltpu.VMEM((rows, width), f32)]
        + exchange_scratch(rows, width)
        + (spread_sems(len(ahead)) if ahead else []),
        flops,
        cell * cell * per_device,
    )
    return results[0], results[1:12], results[12:]


def layer_backward(gradient, weights, norms, kept, extra, last):
    rows, width = gradient.shape
    cell = 4 * rows
    qkv_w, out_w, in_w, back_w = weights
    share = out_w.shape[0] * out_w.shape[1]
    per_device = share // HD
    units = in_w.shape[2]
    depth = in_w.shape[0] // 2
    part = in_w.shape[1]
    f32, low = jnp.float32, jnp.bfloat16
    outputs = [
        ((rows, width), f32),
        ((4, width), f32),
        ((depth, 2, part, 3 * share), low),
        ((2, part, width), low),
        ((part, units), f32),
        ((units, part), f32),
    ]
    if not last:
        outputs += [((part, 3 * share), f32), ((part, width), f32)]
    scratch = [
        pltpu.VMEM((cell, width), low),
        pltpu.VMEM((cell, units), low),
        pltpu.VMEM((cell, width), low),
        pltpu.VMEM((per_device, cell, HD), low),
        pltpu.VMEM((per_device, cell, cell), low),
        pltpu.VMEM((per_device, cell, cell), low),
        pltpu.VMEM((cell, 3 * share), low),
        pltpu.VMEM((3 * per_device, cell, HD), low),
        pltpu.VMEM((rows, width), f32),
        pltpu.VMEM((depth, 2, part, units), low),
        pltpu.VMEM((depth, 2, part, units), low),
    ]
    scratch += reduce_scratch(part, units, low) * 2
    scratch += exchange_scratch(rows, width)
    scratch += reduce_sems(2)
    if not last:
        scratch += reduce_scratch(part, 3 * share, low) + reduce_sems(1)
        scratch += mix_reduce_scratch(part, width, low)
    flops = 4 * cell * width * (4 * share + 2 * units) + 10 * cell * cell * share
    return run_kernel(
        partial(backward_kernel, last),
        3 if last else 4,
        "layer_backward",
        [gradient, qkv_w, out_w, in_w, back_w, norms, *kept, *extra],
        outputs,
        scratch,
        flops,
        cell * cell * per_device,
    )


def table_kernel_stacked(weight, moments, gradient, hits, new_weight, new_moments):
    touched = hits[...] > 0
    grad = gradient[...]
    old, old_first, old_second = weight[0], moments[0, 0], moments[1, 0]
    first = beta_one * old_first + (1.0 - beta_one) * grad
    second = beta_two * old_second + (1.0 - beta_two) * grad * grad
    first_hat = first / (1.0 - beta_one**STEP)
    second_hat = second / (1.0 - beta_two**STEP)
    new = old - rate_table * (first_hat / (jnp.sqrt(second_hat) + adam_eps) + decay_rate * old)
    new_weight[0] = jnp.where(touched, new, old)
    new_moments[0, 0] = jnp.where(touched, first, old_first)
    new_moments[1, 0] = jnp.where(touched, second, old_second)


def update_tables(tables, moments, row_grad, hits):
    count, own_rows, width = tables.shape
    step = own_rows // 3
    table_block = pl.BlockSpec((1, step, width), lambda i, t: (t, i, 0))
    moment_block = pl.BlockSpec((2, 1, step, width), lambda i, t: (0, t, i, 0))
    return pl.pallas_call(
        table_kernel_stacked,
        grid=(own_rows // step, count),
        in_specs=[
            table_block,
            moment_block,
            pl.BlockSpec((step, width), lambda i, t: (i, 0)),
            pl.BlockSpec((step, 1), lambda i, t: (i, 0)),
        ],
        out_specs=[table_block, moment_block],
        out_shape=[
            jax.ShapeDtypeStruct(tables.shape, tables.dtype),
            jax.ShapeDtypeStruct(moments.shape, moments.dtype),
        ],
        compiler_params=pltpu.CompilerParams(vmem_limit_bytes=56 * 2**20),
        cost_estimate=pl.CostEstimate(
            flops=20 * tables.size, bytes_accessed=24 * tables.size, transcendentals=tables.size
        ),
        name="table_update",
    )(tables, moments, row_grad, hits)


def fast_body(
    gene_ids,
    levels,
    study_of_cell,
    cotangent,
    tables,
    table_moments,
    level_table,
    level_moments,
    qkv_weight,
    qkv_moments,
    out_weight,
    out_moments,
    in_weight,
    in_moments,
    back_weight,
    back_moments,
    norm_params,
    norm_moments,
):
    low = jnp.bfloat16
    groups = lax.axis_size("dp")
    members = lax.axis_size("mp")
    member = lax.axis_index("mp")
    rows_here, width = cotangent.shape
    layers = qkv_weight.shape[0]
    local_cells = study_of_cell.shape[0]
    capacity = 2 * rows_here // groups
    own_rows = tables.shape[1]
    block_size = own_rows * members
    depth = qkv_weight.shape[2]
    share = width // members
    units = in_weight.shape[2]

    assert groups == 2 * members and layers == 2 and local_cells == 1
    f32 = jnp.float32
    qkv_mine = lax.dynamic_slice_in_dim(qkv_weight, member * share, share, axis=3).astype(low)
    qkv_mine = qkv_mine.transpose(0, 2, 1, 3).reshape(layers, depth, 3 * share)
    out_mine = out_weight.astype(low)
    in_mine = in_weight.astype(low)
    back_mine = back_weight.astype(low).transpose(0, 2, 1)
    level_rows = level_table.shape[0]
    study_onehot = (study_of_cell[:, None] == jnp.arange(width)[None, :]).astype(f32)
    small = jnp.concatenate(
        [
            level_table.astype(low).astype(f32),
            norm_params.reshape(1, width),
            study_onehot,
            jnp.zeros((16 - level_rows - 2, width), f32),
        ]
    )
    row_owner = gene_ids // block_size
    slot_index = slots_of(row_owner)
    sent_ids = slotted_ids(gene_ids, row_owner, slot_index, groups, capacity)
    codes = (row_owner * capacity + slot_index)[:, None]
    level_column = levels[:, None]
    summed_tables = jnp.sum(tables, axis=0).astype(low)

    slots = groups * capacity
    copies = 2 * (groups // 2) - 1
    dma = pltpu.SemaphoreType.DMA
    hidden, asked, scale, *more = run_kernel(
        start_kernel,
        5,
        "start",
        [
            sent_ids[:, None, :],
            codes,
            level_column,
            summed_tables,
            small,
            qkv_mine[0],
            in_mine[0],
            back_mine[0],
            out_mine[0],
            out_mine[1],
        ],
        [
            ((rows_here, width), f32),
            ((members, groups, 1, capacity), jnp.int32),
            ((1, 1), f32),
            ((4, width), f32),
            ((4, width), f32),
            ((groups, depth, 3 * share), low),
            ((groups, depth, units), low),
            ((groups, depth, units), low),
            ((2, depth, width), low),
            ((2, depth, width), low),
        ],
        [
            pltpu.VMEM((groups, 16, width), f32),
            pltpu.VMEM((groups, capacity, width), low),
            pltpu.VMEM((groups, capacity, width), low),
            pltpu.VMEM((3, slots, width), low),
            pltpu.VMEM((3, slots, width), low),
        ]
        + [dma((SUM_COPIES,))] * 2
        + [dma((1, copies))] * 2
        + [dma((3, copies))] * 2
        + [dma((2, groups // 2 + 1))] * 2
        + [dma((groups - 1,))] * 2
        + [dma((3,))] * 2
        + [dma((groups - 1,))] * 2,
    )
    norms, (qkv_w, in_w, back_w), out_w = more[0:2], more[2:5], more[5:7]

    hidden, kept_zero, ahead = layer_forward(
        hidden,
        (qkv_w, out_w[0], in_w, back_w),
        norms[0],
        [qkv_mine[1], in_mine[1], back_mine[1]],
    )
    weights_one = (ahead[0], out_w[1], ahead[1], ahead[2])
    hidden, kept_one, _ = layer_forward(hidden, weights_one, norms[1], [])
    gradient, norm_one, qkv_one, out_one, in_one, back_one = layer_backward(
        cotangent, weights_one, norms[1], kept_one, [scale], True
    )
    gradient, norm_zero, qkv_zero, out_zero, in_zero, back_zero, qkv_one, out_one = layer_backward(
        gradient,
        (qkv_w, out_w[0], in_w, back_w),
        norms[0],
        kept_zero,
        [qkv_one, out_one],
        False,
    )
    row_grad, hits, qkv_sum, out_sum, small_sum = run_kernel(
        end_kernel,
        6,
        "finish",
        [
            gradient,
            codes,
            level_column,
            asked,
            qkv_zero,
            out_zero,
            norm_zero,
            norm_one,
            qkv_one,
            out_one,
        ],
        [
            ((own_rows, width), f32),
            ((own_rows, 1), f32),
            ((layers, 3, depth, width), f32),
            ((layers, depth, width), f32),
            ((16, width), f32),
        ],
        [
            pltpu.VMEM((groups, capacity, width), low),
            pltpu.VMEM((4 * slots, width), low),
            pltpu.VMEM((groups // 2, 2, 16, width), f32),
            pltpu.VMEM((members, 16, width), f32),
            pltpu.VMEM((2, depth, 3 * share), low),
            pltpu.VMEM((members, 2, depth, 3 * share), low),
            pltpu.VMEM((2, depth, width), low),
            pltpu.VMEM((2, depth, width), low),
        ]
        + reduce_scratch(depth, 3 * share, low)
        + reduce_scratch(16, width, f32)
        + mix_reduce_scratch(depth, width, low)
        + reduce_sems(1)
        + reduce_sems(1)
        + [dma((GATHER_COPIES,))] * 2
        + [dma((groups - 1,))] * 2
        + [dma((3 * members,))] * 2,
    )

    table_new, table_state = update_tables(tables, table_moments, row_grad, hits)
    level_sum = small_sum[:level_rows]
    norm_sum = small_sum[level_rows].reshape(layers, -1)
    in_sum = jnp.stack([in_zero, in_one])
    back_sum = jnp.stack([back_zero, back_one])
    level_new, level_state = adam_step(
        level_table, level_moments, level_sum, rate_table, decay_rate
    )
    qkv_new, qkv_state = adam_step(qkv_weight, qkv_moments, qkv_sum, rate_dense, decay_rate)
    out_new, out_state = adam_step(out_weight, out_moments, out_sum, rate_mixing, decay_rate)
    in_new, in_state = adam_step(in_weight, in_moments, in_sum, rate_dense, decay_rate)
    back_new, back_state = adam_step(back_weight, back_moments, back_sum, rate_dense, decay_rate)
    norm_new, norm_state = adam_step(norm_params, norm_moments, norm_sum, rate_norm, 0.0)
    return (
        hidden,
        table_new,
        table_state,
        level_new,
        level_state,
        qkv_new,
        qkv_state,
        out_new,
        out_state,
        in_new,
        in_state,
        back_new,
        back_state,
        norm_new,
        norm_state,
    )


def solution(mesh):
    return jax.shard_map(
        fast_body if (mesh.shape["dp"], mesh.shape["mp"]) == (8, 4) else general_body,
        mesh=mesh,
        in_specs=(
            P(("dp", "mp")),
            P(("dp", "mp")),
            P("dp"),
            P(("dp", "mp"), None),
            P(None, ("dp", "mp"), None),
            P(None, None, ("dp", "mp"), None),
            P("dp", None),
            P(None, "dp", None),
            P(None, None, "dp", None),
            P(None, None, None, "dp", None),
            P(None, "dp", None),
            P(None, None, "dp", None),
            P(None, "dp", "mp"),
            P(None, None, "dp", "mp"),
            P(None, "mp", "dp"),
            P(None, None, "mp", "dp"),
            P(None, "dp"),
            P(None, None, "dp"),
        ),
        out_specs=(
            P(("dp", "mp"), None),
            P(None, ("dp", "mp"), None),
            P(None, None, ("dp", "mp"), None),
            P("dp", None),
            P(None, "dp", None),
            P(None, None, "dp", None),
            P(None, None, None, "dp", None),
            P(None, "dp", None),
            P(None, None, "dp", None),
            P(None, "dp", "mp"),
            P(None, None, "dp", "mp"),
            P(None, "mp", "dp"),
            P(None, None, "mp", "dp"),
            P(None, "dp"),
            P(None, None, "dp"),
        ),
        check_vma=False,
    )
```

```python
import math
from functools import partial

import jax
import jax.numpy as jnp
from jax import lax
from jax.experimental import pallas as pl
from jax.experimental.pallas import tpu as pltpu
from jax.sharding import PartitionSpec as P

HEADS = 12
HD = 64
STUDY_TOTAL = 16
STEP = 10


largest_value = lax.Precision.HIGHEST
beta_one = 0.9
beta_two = 0.999
adam_eps = 1e-08
norm_eps = 1e-05
rate_dense = 0.08
rate_mixing = 0.3
rate_table = 0.6
rate_norm = 0.4
decay_rate = 0.01


def spread_rows(rows):
    return lax.all_gather(rows, "mp", axis=0, tiled=True)


def summed_rows(term, count):
    return lax.psum_scatter(
        term(jnp.int32(0), count * lax.axis_size("mp")).astype(jnp.bfloat16),
        "mp",
        scatter_dimension=0,
        tiled=True,
    ).astype(jnp.float32)


def norm_forward(rows, gain, bias):
    centered = rows - jnp.mean(rows, axis=-1, keepdims=True)
    inverse = lax.rsqrt(jnp.mean(centered * centered, axis=-1, keepdims=True) + norm_eps)
    normal = centered * inverse
    return (normal * gain + bias, normal, inverse)


def norm_backward(gradient, normal, inverse, gain):
    scaled = gradient * gain
    inner_part = (
        scaled
        - jnp.mean(scaled, axis=-1, keepdims=True)
        - normal * jnp.mean(scaled * normal, axis=-1, keepdims=True)
    )
    return (inner_part * inverse, jnp.sum(gradient * normal, axis=0), jnp.sum(gradient, axis=0))


def gelu_grad(inner, gradient):
    return jax.vjp(partial(jax.nn.gelu, approximate=False), inner)[1](gradient)[0]


def head_major(rows):
    return rows.reshape(rows.shape[0], HEADS, HD).transpose(1, 0, 2)


def row_major(heads):
    return heads.transpose(1, 0, 2).reshape(heads.shape[1], HEADS * HD)


def attend_forward(query, keys, values):
    scale = HD ** (-0.5)

    def one_head(pieces):
        head_query, head_keys, head_values = pieces
        scores = (
            jnp.einsum("qd,kd->qk", head_query, head_keys, preferred_element_type=jnp.float32)
            * scale
        )
        peak = jnp.max(scores, axis=-1, keepdims=True)
        raised = jnp.exp(scores - peak)
        total = jnp.sum(raised, axis=-1, keepdims=True)
        probs = (raised / total).astype(jnp.bfloat16)
        mixed = jnp.dot(probs, head_values, preferred_element_type=jnp.float32).astype(jnp.bfloat16)
        return (mixed, (peak + jnp.log(total))[:, 0])

    mixed, log_total = lax.map(one_head, (head_major(query), head_major(keys), head_major(values)))
    return (row_major(mixed), log_total)


def attend_backward(query, keys, values, mixed_grad, log_total):
    scale = HD ** (-0.5)

    def one_head(pieces):
        head_query, head_keys, head_values, head_grad, head_total = pieces
        scores = (
            jnp.einsum("qd,kd->qk", head_query, head_keys, preferred_element_type=jnp.float32)
            * scale
        )
        probs = jnp.exp(scores - head_total[:, None])
        product = jnp.einsum(
            "qd,kd->qk", head_grad, head_values, preferred_element_type=jnp.float32
        )
        center = jnp.sum(probs * product, axis=-1, keepdims=True)
        score_grad = (probs * (product - center)).astype(jnp.bfloat16)
        query_grad = (
            jnp.dot(score_grad, head_keys, preferred_element_type=jnp.float32) * scale
        ).astype(jnp.bfloat16)
        key_grad = (
            jnp.einsum("qk,qd->kd", score_grad, head_query, preferred_element_type=jnp.float32)
            * scale
        )
        value_grad = jnp.einsum(
            "qk,qd->kd", probs.astype(jnp.bfloat16), head_grad, preferred_element_type=jnp.float32
        )
        return (query_grad, key_grad, value_grad)

    query_grad, key_grad, value_grad = lax.map(
        one_head,
        (
            head_major(query),
            head_major(keys),
            head_major(values),
            head_major(mixed_grad),
            log_total,
        ),
    )
    return (row_major(query_grad), jnp.stack([row_major(key_grad), row_major(value_grad)], axis=1))


def slots_of(row_owner):
    place = jnp.arange(row_owner.shape[0])
    earlier = (row_owner[:, None] == row_owner[None, :]) & (place[None, :] < place[:, None])
    return jnp.sum(earlier.astype(jnp.int32), axis=1)


def slotted_ids(gene_ids, row_owner, slot_index, cell_groups, capacity):
    code = row_owner * capacity + slot_index
    hot = code[None, :] == jnp.arange(cell_groups * capacity)[:, None]
    found = jnp.sum(jnp.where(hot, gene_ids[None, :] + 1, 0), axis=1) - 1
    return found.reshape(cell_groups, capacity)


def adam_step(weight, moments, gradient, rate, decay):
    first = beta_one * moments[0] + (1.0 - beta_one) * gradient
    second = beta_two * moments[1] + (1.0 - beta_two) * gradient * gradient
    first_hat = first / (1.0 - beta_one**STEP)
    second_hat = second / (1.0 - beta_two**STEP)
    new_weight = weight - rate * (first_hat / (jnp.sqrt(second_hat) + adam_eps) + decay * weight)
    return (new_weight, jnp.stack([first, second]))


def general_body(
    gene_ids,
    levels,
    study_of_cell,
    cotangent,
    tables,
    table_moments,
    level_table,
    level_moments,
    qkv_weight,
    qkv_moments,
    out_weight,
    out_moments,
    in_weight,
    in_moments,
    back_weight,
    back_moments,
    norm_params,
    norm_moments,
):
    cell_groups = lax.axis_size("dp")
    rows_here = cotangent.shape[0]
    model_width = cotangent.shape[1]
    layers = qkv_weight.shape[0]
    local_cells = study_of_cell.shape[0]
    capacity = 2 * rows_here // cell_groups
    own_rows = tables.shape[1]
    block_size = own_rows * lax.axis_size("mp")
    qkv_full, out_full, in_part, back_part, level_full = (
        lax.all_gather(qkv_weight.astype(jnp.bfloat16), "dp", axis=2, tiled=True),
        lax.all_gather(out_weight.astype(jnp.bfloat16), "dp", axis=1, tiled=True),
        lax.all_gather(in_weight.astype(jnp.bfloat16), "dp", axis=1, tiled=True),
        lax.all_gather(back_weight.astype(jnp.bfloat16), "dp", axis=2, tiled=True),
        lax.all_gather(level_table.astype(jnp.bfloat16), "dp", axis=0, tiled=True),
    )
    study_onehot = (study_of_cell[:, None] == jnp.arange(STUDY_TOTAL)[None, :]).astype(jnp.float32)
    norm_full, study_all = (
        lax.all_gather(norm_params, "dp", axis=1, tiled=True),
        lax.all_gather(study_onehot, "dp", axis=0, tiled=True),
    )
    cells_per_study = jnp.sum(study_all, axis=0)
    cell_balance_weight = (
        cell_groups
        * local_cells
        / (STUDY_TOTAL * jnp.dot(study_onehot, cells_per_study, precision=largest_value))
    )
    out_grad = cotangent * cell_balance_weight[0]
    summed_tables = jnp.sum(tables, axis=0).astype(jnp.bfloat16)
    table_rows = lax.all_gather(summed_tables, "mp", axis=0, tiled=True)
    row_owner = gene_ids // block_size
    slot_index = slots_of(row_owner)
    sent_ids = slotted_ids(gene_ids, row_owner, slot_index, cell_groups, capacity)
    asked_ids = lax.all_to_all(sent_ids, "dp", split_axis=0, concat_axis=0, tiled=True)
    present = asked_ids >= 0
    safe_row = jnp.where(present, asked_ids - lax.axis_index("dp") * block_size, 0)
    found_rows = jnp.where(present[..., None], jnp.take(table_rows, safe_row, axis=0), 0)
    returned = lax.all_to_all(found_rows, "dp", split_axis=0, concat_axis=0, tiled=True)
    gene_part = returned[row_owner, slot_index].astype(jnp.float32)
    level_hot = (levels[:, None] == jnp.arange(level_full.shape[0])[None, :]).astype(jnp.bfloat16)
    hidden = gene_part + jnp.dot(level_hot, level_full, preferred_element_type=jnp.float32)
    kept = []
    for layer in range(layers):
        norm_row = norm_full[layer]
        tokens_low = hidden.astype(jnp.bfloat16)
        projected = jnp.einsum(
            "td,cdh->tch", tokens_low, qkv_full[layer], preferred_element_type=jnp.float32
        ).astype(jnp.bfloat16)
        query = projected[:, 0]
        cell_rows = spread_rows(projected[:, 1:])
        keys, values = (cell_rows[:, 0], cell_rows[:, 1])
        mixed, log_total = attend_forward(query, keys, values)
        attention = jnp.dot(mixed, out_full[layer], preferred_element_type=jnp.float32)
        first, first_normal, first_inverse = norm_forward(
            hidden + attention, norm_row[:model_width], norm_row[model_width : 2 * model_width]
        )
        first_low = first.astype(jnp.bfloat16)
        in_layer, back_layer = (in_part[layer], back_part[layer])
        first_spread = spread_rows(first_low)
        inner = jnp.dot(first_spread, in_layer, preferred_element_type=jnp.float32)
        active = jax.nn.gelu(inner, approximate=False).astype(jnp.bfloat16)

        def feed_term(start, count):
            return jnp.dot(active, back_layer, preferred_element_type=jnp.float32)

        feed = summed_rows(feed_term, rows_here)
        second, second_normal, second_inverse = norm_forward(
            first + feed, norm_row[2 * model_width : 3 * model_width], norm_row[3 * model_width :]
        )
        kept.append(
            (
                tokens_low,
                query,
                keys,
                values,
                mixed,
                log_total,
                first_normal,
                first_inverse,
                first_spread,
                inner,
                active,
                in_layer,
                back_layer,
                second_normal,
                second_inverse,
            )
        )
        hidden = second
    gradient = out_grad
    qkv_grads = [None] * layers
    out_grads = [None] * layers
    in_grads = [None] * layers
    back_grads = [None] * layers
    norm_grads = [None] * layers
    for layer in reversed(range(layers)):
        (
            tokens_low,
            query,
            keys,
            values,
            mixed,
            log_total,
            first_normal,
            first_inverse,
            first_spread,
            inner,
            active,
            in_layer,
            back_layer,
            second_normal,
            second_inverse,
        ) = kept[layer]
        norm_row = norm_full[layer]
        grad_second, gain_two, bias_two = norm_backward(
            gradient, second_normal, second_inverse, norm_row[2 * model_width : 3 * model_width]
        )
        feed_low = grad_second.astype(jnp.bfloat16)
        feed_spread = spread_rows(feed_low)
        back_grads[layer] = jnp.einsum(
            "tf,td->fd", active, feed_spread, preferred_element_type=jnp.float32
        )
        active_grad = jnp.einsum(
            "td,fd->tf", feed_spread, back_layer, preferred_element_type=jnp.float32
        )
        inner_grad = gelu_grad(inner, active_grad).astype(jnp.bfloat16)
        in_grads[layer] = jnp.einsum(
            "td,tf->df", first_spread, inner_grad, preferred_element_type=jnp.float32
        )

        def first_term(start, count):
            return jnp.einsum("tf,df->td", inner_grad, in_layer, preferred_element_type=jnp.float32)

        first_grad = summed_rows(first_term, rows_here)
        grad_first, gain_one, bias_one = norm_backward(
            grad_second + first_grad, first_normal, first_inverse, norm_row[:model_width]
        )
        norm_grads[layer] = jnp.concatenate([gain_one, bias_one, gain_two, bias_two])
        attention_low = grad_first.astype(jnp.bfloat16)
        out_grads[layer] = jnp.einsum(
            "th,td->hd", mixed, attention_low, preferred_element_type=jnp.float32
        )
        mixed_grad = jnp.einsum(
            "td,hd->th", attention_low, out_full[layer], preferred_element_type=jnp.float32
        ).astype(jnp.bfloat16)
        query_grad, pair_partial = attend_backward(query, keys, values, mixed_grad, log_total)
        pair_grad = lax.psum_scatter(
            pair_partial.astype(jnp.bfloat16), "mp", scatter_dimension=0, tiled=True
        )
        stacked = jnp.concatenate([query_grad[:, None, :], pair_grad], axis=1)
        qkv_grads[layer] = jnp.einsum(
            "td,tch->cdh", tokens_low, stacked, preferred_element_type=jnp.float32
        )
        gradient = grad_first + jnp.einsum(
            "tch,cdh->td", stacked, qkv_full[layer], preferred_element_type=jnp.float32
        )
    level_grad = jnp.dot(level_hot.astype(jnp.float32).T, gradient, precision=largest_value)
    grad_slots = (
        jnp.zeros((cell_groups, capacity, model_width), jnp.float32)
        .at[row_owner, slot_index]
        .set(gradient)
    )
    arrived = lax.all_to_all(
        grad_slots.astype(jnp.bfloat16), "dp", split_axis=0, concat_axis=0, tiled=True
    ).astype(grad_slots.dtype)
    arrived = jnp.where(present[..., None], arrived, 0.0)
    flat_rows = safe_row.reshape(-1)
    block_grad = jax.ops.segment_sum(
        arrived.reshape(-1, model_width), flat_rows, num_segments=block_size
    )
    block_hits = jax.ops.segment_sum(
        present.reshape(-1).astype(jnp.float32), flat_rows, num_segments=block_size
    )
    row_grad, hits = (
        lax.psum_scatter(
            block_grad.astype(jnp.bfloat16), "mp", scatter_dimension=0, tiled=True
        ).astype(jnp.float32),
        lax.psum_scatter(
            block_hits.astype(jnp.bfloat16), "mp", scatter_dimension=0, tiled=True
        ).astype(jnp.float32),
    )
    qkv_sum, out_sum, in_sum, back_sum, level_sum, norm_sum = (
        lax.psum_scatter(
            jnp.stack(qkv_grads).astype(jnp.bfloat16), "dp", scatter_dimension=2, tiled=True
        ).astype(jnp.float32),
        lax.psum_scatter(
            jnp.stack(out_grads).astype(jnp.bfloat16), "dp", scatter_dimension=1, tiled=True
        ).astype(jnp.float32),
        lax.psum_scatter(
            jnp.stack(in_grads).astype(jnp.bfloat16), "dp", scatter_dimension=1, tiled=True
        ).astype(jnp.float32),
        lax.psum_scatter(
            jnp.stack(back_grads).astype(jnp.bfloat16), "dp", scatter_dimension=2, tiled=True
        ).astype(jnp.float32),
        lax.psum_scatter(
            level_grad.astype(jnp.bfloat16), "dp", scatter_dimension=0, tiled=True
        ).astype(jnp.float32),
        lax.psum_scatter(
            jnp.stack(norm_grads).astype(jnp.bfloat16), "dp", scatter_dimension=1, tiled=True
        ).astype(jnp.float32),
    )
    qkv_sum, out_sum, level_sum, norm_sum = (
        lax.psum(qkv_sum.astype(jnp.bfloat16), "mp").astype(jnp.float32),
        lax.psum(out_sum.astype(jnp.bfloat16), "mp").astype(jnp.float32),
        lax.psum(level_sum.astype(jnp.bfloat16), "mp").astype(jnp.float32),
        lax.psum(norm_sum.astype(jnp.bfloat16), "mp").astype(jnp.float32),
    )
    touched = (hits > 0)[None, :, None]
    table_grad = jnp.broadcast_to(row_grad[None], tables.shape)
    table_new, table_state = adam_step(tables, table_moments, table_grad, rate_table, decay_rate)
    table_new = jnp.where(touched, table_new, tables)
    table_state = jnp.where(touched[None], table_state, table_moments)
    level_new, level_state = adam_step(
        level_table, level_moments, level_sum, rate_table, decay_rate
    )
    qkv_new, qkv_state = adam_step(qkv_weight, qkv_moments, qkv_sum, rate_dense, decay_rate)
    out_new, out_state = adam_step(out_weight, out_moments, out_sum, rate_mixing, decay_rate)
    in_new, in_state = adam_step(in_weight, in_moments, in_sum, rate_dense, decay_rate)
    back_new, back_state = adam_step(back_weight, back_moments, back_sum, rate_dense, decay_rate)
    norm_new, norm_state = adam_step(norm_params, norm_moments, norm_sum, rate_norm, 0.0)
    return (
        hidden,
        table_new,
        table_state,
        level_new,
        level_state,
        qkv_new,
        qkv_state,
        out_new,
        out_state,
        in_new,
        in_state,
        back_new,
        back_state,
        norm_new,
        norm_state,
    )


MESH = pl.DeviceIdType.MESH
SIB, FACE = 0, 1
TILE = 128


def nn(a, b):
    return lax.dot_general(a, b, (((1,), (0,)), ((), ())), preferred_element_type=jnp.float32)


def nt(a, b):
    return lax.dot_general(a, b, (((1,), (1,)), ((), ())), preferred_element_type=jnp.float32)


def tn(a, b):
    return lax.dot_general(a, b, (((0,), (0,)), ((), ())), preferred_element_type=jnp.float32)


def near_devices():
    group, member = lax.axis_index("dp"), lax.axis_index("mp")
    core = member % 2
    return (group, member + 1 - 2 * core), (group, (member + 2) % 4)


def greet(peers):
    barrier = pltpu.get_barrier_semaphore()
    for peer in peers:
        pl.semaphore_signal(barrier, inc=1, device_id=peer, device_id_type=MESH)
    pl.semaphore_wait(barrier, len(peers))


def send(source, target, sems, index, peer):
    copy = pltpu.make_async_remote_copy(
        src_ref=source,
        dst_ref=target,
        send_sem=sems[0].at[index],
        recv_sem=sems[1].at[index],
        device_id=peer,
        device_id_type=MESH,
    )
    copy.start()
    return copy


PIECES = 2


def columns_of(group):
    return group // 2, group % 2


def group_peers():
    group, member = lax.axis_index("dp"), lax.axis_index("mp")
    count = lax.axis_size("dp")
    return [((group + k) % count, member) for k in range(1, count)]


def mates():
    group, member = lax.axis_index("dp"), lax.axis_index("mp")
    count = lax.axis_size("mp")
    return [(group, (member + k) % count) for k in range(1, count)]


class Spread:
    def __init__(self, mine, whole, sems, part):
        group, member = lax.axis_index("dp"), lax.axis_index("mp")
        depth = lax.axis_size("dp") // 2
        z, x = columns_of(group)
        self.beside = (group + 1 - 2 * x, member)
        self.whole, self.sems, self.part, self.depth = whole, sems, part, depth
        self.came = [((z + depth - k) % depth) * 2 + x for k in range(1, depth)]
        self.along = [
            send(mine, whole.at[group], sems, (part, k - 1), (((z + k) % depth) * 2 + x, member))
            for k in range(1, depth)
        ]
        self.across = [send(mine, whole.at[group], sems, (part, depth - 1), self.beside)]
        whole[group] = mine[...]

    def hand_on(self):
        for k in range(1, self.depth):
            self.along[k - 1].wait_recv()
            block = self.whole.at[self.came[k - 1]]
            self.across.append(
                send(block, block, self.sems, (self.part, self.depth - 1 + k), self.beside)
            )

    def arrive(self):
        for copy in self.across:
            copy.wait_recv()

    def finish(self):
        for copy in [*self.along, *self.across]:
            copy.wait_send()


class Reduce:
    def __init__(self, source, near, come, sems, line):
        group, self.member = lax.axis_index("dp"), lax.axis_index("mp")
        self.depth = lax.axis_size("dp") // 2
        self.z, self.x = columns_of(group)
        self.source, self.near, self.come = source, near, come
        self.sems, self.line, self.copies = sems, line, []
        if source is not None:
            beside = (group + 1 - 2 * self.x, self.member)
            self.first = send(source.at[:, 1 - self.x], near, sems, (line, 0), beside)

    def pair(self, z):
        term = self.near[z].astype(jnp.float32)
        return term if self.source is None else term + self.source[z, self.x].astype(jnp.float32)

    def add_up(self):
        self.first.wait_recv()
        for z in range(self.depth):
            self.near[z] = self.pair(z).astype(self.near.dtype)
        self.first.wait_send()

    def middle(self):
        if self.source is not None:
            self.first.wait_recv()
        for k in range(1, self.depth):
            z = (self.z + k) % self.depth
            if self.source is not None:
                self.near[z] = self.pair(z).astype(self.near.dtype)
            self.copies.append(
                send(
                    self.near.at[z],
                    self.come.at[k - 1],
                    self.sems,
                    (self.line, k),
                    (z * 2 + self.x, self.member),
                )
            )

    def finish(self):
        term = self.pair(self.z)
        for k, copy in enumerate(self.copies):
            copy.wait_recv()
            term = term + self.come[k].astype(jnp.float32)
        for copy in self.copies:
            copy.wait_send()
        if self.source is not None:
            self.first.wait_send()
        return term


def reduce_scratch(rows, columns, dtype):
    depth = lax.axis_size("dp") // 2
    return [pltpu.VMEM((depth, rows, columns), dtype), pltpu.VMEM((depth - 1, rows, columns), dtype)]


def dma_sems(*shape):
    return [pltpu.SemaphoreType.DMA(shape)] * 2


class MixReduce:
    def __init__(self, source, near, come, sems, line):
        group, self.member = lax.axis_index("dp"), lax.axis_index("mp")
        self.depth = lax.axis_size("dp") // 2
        self.z, self.x = columns_of(group)
        self.sems, self.line = sems, line
        self.source, self.near, self.come = source, near, come
        if source is not None:
            beside = (group + 1 - 2 * self.x, self.member)
            self.first = send(source.at[1 - self.x], near, sems, (line, 0), beside)

    def copy(self, slot, there):
        return pltpu.make_async_remote_copy(
            src_ref=self.near,
            dst_ref=self.come.at[slot],
            send_sem=self.sems[0].at[self.line, 1 + slot],
            recv_sem=self.sems[1].at[self.line, 1 + slot],
            device_id=(there, self.member),
            device_id_type=MESH,
        )

    def to_root(self):
        slot = (self.member + 2 * self.depth - self.z - 1) % self.depth
        return self.copy(slot, self.member * 2 + self.x)

    def add_up(self):
        self.first.wait_recv()
        term = self.source[self.x].astype(jnp.float32) + self.near[...].astype(jnp.float32)
        self.near[...] = term.astype(self.near.dtype)
        self.first.wait_send()

    def middle(self):
        if self.source is not None:
            self.add_up()

        @pl.when(self.z != self.member)
        def _():
            self.to_root().start()

    def finish(self):
        @pl.when(self.z == self.member)
        def _():
            for slot in range(self.depth - 1):
                self.copy(slot, (self.member * 2 + self.x + 2) % (2 * self.depth)).wait_recv()

        @pl.when(self.z != self.member)
        def _():
            self.to_root().wait_send()

        term = self.near[...].astype(jnp.float32)
        for slot in range(self.depth - 1):
            term = term + self.come[slot].astype(jnp.float32)
        return term


class Gather:
    def __init__(self, buf, sems, line, pieces=PIECES):
        self.buf, self.sems, self.line, self.pieces = buf, sems, line, pieces
        self.sib, self.face = near_devices()
        self.rows = buf.shape[0] // 4
        self.size = self.rows // pieces
        self.across, self.beside, self.handed = [], [], []

    def piece(self, b, i):
        return self.buf.at[pl.ds(b * self.rows + i * self.size, self.size)]

    def start(self, i):
        mine = self.piece(0, i)
        self.across.append(send(mine, self.piece(2, i), self.sems, (self.line, i), self.face))
        self.beside.append(
            send(mine, self.piece(1, i), self.sems, (self.line, self.pieces + i), self.sib)
        )

    def wait_beside(self):
        for copy in self.beside:
            copy.wait_recv()

    def hand_on(self, i):
        self.across[i].wait_recv()
        self.handed.append(
            send(
                self.piece(2, i),
                self.piece(3, i),
                self.sems,
                (self.line, 2 * self.pieces + i),
                self.sib,
            )
        )

    def wait_handed(self, i):
        self.handed[i].wait_recv()

    def finish(self):
        for copy in [*self.across, *self.beside, *self.handed]:
            copy.wait_send()


class Total:
    def __init__(self, out, into, sems, line, pieces=PIECES):
        self.out, self.into, self.sems, self.line, self.pieces = out, into, sems, line, pieces
        self.sib, self.face = near_devices()
        self.size = out.shape[1] // pieces
        self.far, self.facing, self.beside = [], [], []

    def give(self, b, i, term, peer):
        piece = pl.ds(i * self.size, self.size)
        self.out[b, piece, :] = term.astype(jnp.bfloat16)
        return send(
            self.out.at[b, piece],
            self.into.at[b, piece],
            self.sems,
            (self.line, b * self.pieces + i),
            peer,
        )

    def came(self, b, i):
        return self.into[b, pl.ds(i * self.size, self.size), :].astype(jnp.float32)

    def part(self, term, i):
        return term[i * self.size : (i + 1) * self.size]

    def give_far(self, i, term):
        self.far.append(self.give(0, i, term, self.sib))

    def give_facing(self, i, term):
        self.far[i].wait_recv()
        self.facing.append(self.give(1, i, term + self.came(0, i), self.face))

    def give_beside(self, i, term):
        self.beside.append(self.give(2, i, term, self.sib))

    def take(self, i, term):
        self.beside[i].wait_recv()
        self.facing[i].wait_recv()
        return term + self.came(2, i) + self.came(1, i)

    def finish(self):
        for copy in [*self.far, *self.facing, *self.beside]:
            copy.wait_send()


def gelu_pair(x):
    t = 1.0 / (1.0 + (0.3275911 * 0.7071067811865476) * jnp.abs(x))
    raised = jnp.exp(-0.5 * x * x)
    series = t * (
        0.254829592
        + t * (-0.284496736 + t * (1.421413741 + t * (-1.453152027 + t * 1.061405429)))
    )
    upper = 0.5 * series * raised
    share = jnp.where(x >= 0, 1.0 - upper, upper)
    return x * share, share + x * raised * 0.3989422804014327


def rows_joined(ref):
    blocks = ref[...]
    return blocks.reshape(blocks.shape[0] * blocks.shape[1], blocks.shape[2])


def around(peers):
    group, member = lax.axis_index("dp"), lax.axis_index("mp")
    depth = lax.axis_size("dp") // 2
    z, x = columns_of(group)
    along = [(((z + k) % depth) * 2 + x, member) for k in range(1, depth)]
    return [*peers, *along, (group + 1 - 2 * x, member)]


def layers_kernel(*refs):
    refs = iter(refs)
    take = lambda count: [next(refs) for _ in range(count)]
    hidden, cotangent, scale = take(3)
    norms = take(2)
    qkv_zero, out_zero, out_one = take(3)
    mine = take(5)
    encoded, gradient_out = take(2)
    norm_grads = take(2)
    qkv_pair, out_pair = take(2)
    in_sums, back_sums = take(2), take(2)
    qkv_sum, out_sum = take(2)
    in_zero, back_zero, qkv_one, in_one, back_one = whole = take(5)
    saved = [take(11), take(11)]
    mixed_t, held, out, into = take(4)
    feeds, inner, lows, mixed_grad, key_grad, value_grad, query_grad, head_grads = take(8)
    in_g, back_g, qkv_g, out_g = take(4)
    in_near, in_come, back_near, back_come = take(2), take(1), take(2), take(1)
    qkv_parts, out_parts = take(2), take(2)
    gather_sems, total_sems, spread_sem = take(2), take(2), take(2)
    in_sems, back_sems, qkv_sems, out_sems = take(2), take(2), take(2), take(2)
    weights = [(qkv_zero, out_zero, in_zero, back_zero), (qkv_one, out_one, in_one, back_one)]
    greet(around(near_devices()))
    rows = hidden.shape[0]
    size = rows // PIECES
    share = mixed_t.shape[0]
    per_device = share // HD
    pieces = range(PIECES)

    def block(b):
        return pl.ds(b * rows, rows)

    def piece(b, i):
        return pl.ds(b * rows + i * size, size)

    def spread_of(part):
        return Spread(mine[part], whole[part], spread_sem, part)

    def send_tokens(layer, i, value):
        saved[layer][4][piece(0, i), :] = value.astype(jnp.bfloat16)
        gathers[layer].start(i)

    gathers = [Gather(saved[layer][4], gather_sems, layer) for layer in range(2)]
    for i in pieces:
        send_tokens(0, i, hidden[piece(0, i), :])
    spreads = [spread_of(part) for part in range(5)]
    held[...] = hidden[...]

    def forward(layer, after_projection, after_far, after_attention, before_feed, after_feed, close):
        second_normal, second_inverse, first_normal, first_inverse = saved[layer][:4]
        tokens, heads, mixed, logs, firsts, active, slope = saved[layer][4:]
        qkv_w, out_w, in_w, back_w = weights[layer]
        gather, norm = gathers[layer], norms[layer]

        def project(place):
            parts = nn(tokens[place, :], rows_joined(qkv_w))
            for j in range(3 * per_device):
                part = parts[:, j * HD : (j + 1) * HD]
                if j < per_device:
                    part = part * HD ** (-0.5)
                heads[j, place, :] = part.astype(jnp.bfloat16)

        project(block(0))
        gather.wait_beside()
        project(block(1))
        for i in pieces:
            gather.hand_on(i)
            project(piece(2, i))
        for i in pieces:
            gather.wait_handed(i)
        project(block(3))
        gather.finish()
        after_projection()

        def attend(b):
            def one_head(h, carry):
                scores = nt(heads[per_device + h], heads[h, block(b), :])
                peak = jnp.max(scores, axis=0, keepdims=True)
                raised = jnp.exp(scores - peak)
                total = jnp.sum(raised, axis=0, keepdims=True)
                result = tn(heads[2 * per_device + h], raised.astype(jnp.bfloat16)) / total
                mixed_t[pl.ds(pl.multiple_of(h * HD, HD), HD), :] = result
                logs[b * per_device + h] = peak + jnp.log(total)
                return carry

            lax.fori_loop(0, per_device, one_head, 0)
            rows_mixed = mixed_t[...].T.astype(jnp.bfloat16)
            mixed[block(b), :] = rows_mixed
            return nn(rows_mixed, rows_joined(out_w))

        total = Total(out, into, total_sems, layer)
        term = attend(3)
        for i in pieces:
            total.give_far(i, total.part(term, i))
        term = attend(2)
        for i in pieces:
            total.give_facing(i, total.part(term, i))
        after_far()
        term = attend(1)
        for i in pieces:
            total.give_beside(i, total.part(term, i))
        held[...] += attend(0)
        after_attention()
        gather_two = Gather(firsts, gather_sems, 2 + layer)
        for i in pieces:
            place = piece(0, i)
            first, normal, inverse = norm_forward(
                total.take(i, held[place, :]), norm[0:1, :], norm[1:2, :]
            )
            firsts[place, :] = first.astype(jnp.bfloat16)
            gather_two.start(i)
            first_normal[place, :] = normal
            first_inverse[place, :] = inverse
            held[place, :] = first
        total.finish()
        before_feed()

        def feed(place):
            value, gradient = gelu_pair(nn(firsts[place, :], rows_joined(in_w)))
            value = value.astype(jnp.bfloat16)
            active[place, :] = value
            slope[place, :] = gradient.astype(jnp.bfloat16)
            return nt(value, rows_joined(back_w))

        total = Total(out, into, total_sems, 2 + layer)
        held[...] += feed(block(0))
        gather_two.wait_beside()
        term = feed(block(1))
        for i in pieces:
            total.give_beside(i, total.part(term, i))
        for i in pieces:
            gather_two.hand_on(i)
            term = feed(piece(2, i))
            gather_two.wait_handed(i)
            total.give_far(i, feed(piece(3, i)))
            total.give_facing(i, term)
        after_feed()
        for i in pieces:
            place = piece(0, i)
            result, normal, inverse = norm_forward(
                total.take(i, held[place, :]), norm[2:3, :], norm[3:4, :]
            )
            second_normal[place, :] = normal
            second_inverse[place, :] = inverse
            close(i, result)
        gather_two.finish()
        total.finish()

    def note(layer, row, i, gain, bias):
        target = norm_grads[layer]
        if i:
            gain, bias = gain + target[row, :], bias + target[row + 1, :]
        target[row : row + 1, :] = gain[None]
        target[row + 1 : row + 2, :] = bias[None]

    feed_gathers = [Gather(feeds, gather_sems, 4 + layer) for layer in range(2)]

    def send_feed_grad(layer, i, gradient):
        place = piece(0, i)
        grad_second, gain, bias = norm_backward(
            gradient, saved[layer][0][place, :], saved[layer][1][place, :], norms[layer][2:3, :]
        )
        feeds[place, :] = grad_second.astype(jnp.bfloat16)
        feed_gathers[layer].start(i)
        note(layer, 2, i, gain, bias)
        held[place, :] = grad_second

    def backward(layer, before_in, after_back, after_score, close_in, close):
        _, _, first_normal, first_inverse = saved[layer][:4]
        tokens, heads, mixed, logs, firsts, active, slope = saved[layer][4:]
        qkv_w, out_w, in_w, back_w = weights[layer]
        gather = feed_gathers[layer]

        def feed(place):
            part = nn(feeds[place, :], rows_joined(back_w)) * slope[place, :].astype(jnp.float32)
            part = part.astype(jnp.bfloat16)
            inner[place, :] = part
            return nt(part, rows_joined(in_w))

        total = Total(out, into, total_sems, 4 + layer)
        held[...] += feed(block(0))
        gather.wait_beside()
        term = feed(block(1))
        for i in pieces:
            total.give_beside(i, total.part(term, i))
        for i in pieces:
            gather.hand_on(i)
            term = feed(piece(2, i))
            gather.wait_handed(i)
            total.give_far(i, feed(piece(3, i)))
            total.give_facing(i, term)
        gather.finish()
        before_in()
        in_g[...] = tn(firsts[...], inner[...]).astype(jnp.bfloat16).reshape(in_g.shape)
        in_reduce = Reduce(in_g, in_near[layer], in_come[0], in_sems, layer)
        gather_two = Gather(lows, gather_sems, 6 + layer)
        for i in pieces:
            place = piece(0, i)
            grad_first, gain, bias = norm_backward(
                total.take(i, held[place, :]),
                first_normal[place, :],
                first_inverse[place, :],
                norms[layer][0:1, :],
            )
            lows[place, :] = grad_first.astype(jnp.bfloat16)
            gather_two.start(i)
            note(layer, 0, i, gain, bias)
            held[place, :] = grad_first
        total.finish()
        back_g[...] = tn(feeds[...], active[...]).astype(jnp.bfloat16).reshape(back_g.shape)
        back_reduce = Reduce(back_g, back_near[layer], back_come[0], back_sems, layer)
        after_back()

        def spread(place):
            parts = nt(lows[place, :], rows_joined(out_w))
            for j in range(per_device):
                mixed_grad[j, place, :] = parts[:, j * HD : (j + 1) * HD].astype(jnp.bfloat16)

        def score(b):
            def one_head(h, carry):
                query, key = heads[h, block(b), :], heads[per_device + h]
                upper = mixed_grad[h, block(b), :]
                prob = jnp.exp(nt(key, query) - logs[b * per_device + h])
                product = nt(heads[2 * per_device + h], upper)
                center = jnp.sum(prob * product, axis=0, keepdims=True)
                score_grad = (prob * (product - center)).astype(jnp.bfloat16)
                key_term = nn(score_grad, query)
                value_term = nn(prob.astype(jnp.bfloat16), upper)
                if b:
                    key_term, value_term = key_term + key_grad[h], value_term + value_grad[h]
                key_grad[h] = key_term
                value_grad[h] = value_term
                turned = tn(key, score_grad) * HD ** (-0.5)
                query_grad[h, block(b), :] = turned.T.astype(jnp.bfloat16)
                return carry

            lax.fori_loop(0, per_device, one_head, 0)

        spread(block(0))
        score(0)
        for i in pieces:
            gather_two.hand_on(i)
        gather_two.wait_beside()
        spread(block(1))
        score(1)
        after_score()
        in_reduce.middle()
        spread(block(2))
        score(2)
        for i in pieces:
            gather_two.wait_handed(i)
        spread(block(3))
        score(3)
        gather_two.finish()
        back_reduce.middle()
        for h in range(per_device):
            for c, grad in enumerate((query_grad, key_grad, value_grad)):
                start = c * share + h * HD
                head_grads[:, start : start + HD] = grad[h].astype(jnp.bfloat16)

        total = Total(out, into, total_sems, 6 + layer)
        weight = rows_joined(qkv_w)
        term = nt(head_grads[block(3), :], weight)
        for i in pieces:
            total.give_far(i, total.part(term, i))
        term = nt(head_grads[block(2), :], weight)
        for i in pieces:
            total.give_facing(i, total.part(term, i))
        term = nt(head_grads[block(1), :], weight)
        for i in pieces:
            total.give_beside(i, total.part(term, i))
        held[...] += nt(head_grads[block(0), :], weight)
        qkv_g[...] = tn(tokens[...], head_grads[...]).astype(jnp.bfloat16).reshape(qkv_g.shape)
        out_g[...] = tn(mixed[...], lows[...]).astype(jnp.bfloat16).reshape(out_g.shape)
        close_in()
        for i in pieces:
            close(i, total.take(i, held[piece(0, i), :]))
        total.finish()
        return in_reduce, back_reduce

    def between(i, result):
        held[piece(0, i), :] = result
        send_tokens(1, i, result)

    def before_feed_zero():
        spreads[0].arrive()
        spreads[1].arrive()

    def after_attention_zero():
        spreads[1].hand_on()
        spreads[2].hand_on()

    forward(
        0,
        spreads[0].hand_on,
        lambda: None,
        after_attention_zero,
        before_feed_zero,
        spreads[3].hand_on,
        between,
    )
    spreads[2].arrive()

    def turn(i, result):
        encoded[piece(0, i), :] = result
        send_feed_grad(1, i, cotangent[piece(0, i), :] * scale[...])

    def before_feed_one():
        spreads[3].arrive()
        spreads[4].arrive()

    forward(
        1,
        spreads[4].hand_on,
        lambda: None,
        lambda: None,
        before_feed_one,
        lambda: None,
        turn,
    )
    for spread in spreads:
        spread.finish()

    reduces = []
    none = lambda: None

    def start_prior():
        reduces.append(Reduce(qkv_g, *qkv_parts, qkv_sems, 0))
        reduces.append(MixReduce(out_g, *out_parts, out_sems, 0))

    in_reduce, back_reduce = backward(
        1,
        none,
        none,
        none,
        start_prior,
        lambda i, value: send_feed_grad(0, i, value),
    )
    in_sums[1][...] = in_reduce.finish()
    back_sums[1][...] = back_reduce.finish().T

    def prior_middle():
        for reduce in reduces:
            reduce.middle()

    def prior_finish():
        qkv_sum[...] = reduces[0].finish()
        out_sum[...] = reduces[1].finish()

    def start_pair():
        reduces.append(Reduce(qkv_g, qkv_pair, None, qkv_sems, 1))
        reduces.append(MixReduce(out_g, out_pair, None, out_sems, 1))

    def last(i, value):
        gradient_out[piece(0, i), :] = value

    in_reduce, back_reduce = backward(0, prior_middle, none, prior_finish, start_pair, last)
    in_sums[0][...] = in_reduce.finish()
    back_sums[0][...] = back_reduce.finish().T
    for reduce in reduces[2:]:
        reduce.add_up()


def halves():
    depth = lax.axis_size("dp") // 2
    steps = [*range(1, depth), 0]
    return [[(k, (k + 1 + half) % 2) for k in steps] for half in range(2)]


def group_at(step, back=False):
    group = lax.axis_index("dp")
    depth = lax.axis_size("dp") // 2
    z, x = columns_of(group)
    along = depth - step[0] if back else step[0]
    return ((z + along) % depth) * 2 + (x + step[1]) % 2


def start_kernel(*refs):
    refs = iter(refs)
    take = lambda count: [next(refs) for _ in range(count)]
    sent_ids, codes, levels, table_rows, small = take(5)
    mine, out_mine = take(1), take(2)
    hidden, asked, scale = take(3)
    norms = take(2)
    whole, out_whole = take(1), take(2)
    small_all, found, returned, out_a, into_a = take(5)
    total_a, small_sems, spread_sem, out_sems, id_sems, near_sems, row_sems = [take(2) for _ in range(7)]
    group, member = lax.axis_index("dp"), lax.axis_index("mp")
    groups, members = lax.axis_size("dp"), lax.axis_size("mp")
    depth = groups // 2
    z, x = columns_of(group)
    beside = (group + 1 - 2 * x, member)
    peers = group_peers()
    sib, face = near_devices()
    far = (group, (sib[1] + 2) % members)
    greet([*peers, *mates()])

    id_copies = [
        send(sent_ids.at[peer[0]], asked.at[0, group], id_sems, k, peer)
        for k, peer in enumerate(peers)
    ]
    asked[0, group] = sent_ids[group]
    small_spread = Spread(small, small_all, small_sems, 0)
    for copy in id_copies:
        copy.wait_recv()
    near_copies = [
        send(asked.at[0], asked.at[k + 1], near_sems, k, peer)
        for k, peer in enumerate((sib, face, far))
    ]
    spreads = [Spread(a, b, spread_sem, p) for p, (a, b) in enumerate(zip(mine, whole))]

    def root_copies():
        return [
            pltpu.make_async_remote_copy(
                src_ref=mine_out,
                dst_ref=target.at[x],
                send_sem=out_sems[0].at[p, k],
                recv_sem=out_sems[1].at[p, 0],
                device_id=(((z + k) % depth) * 2 + x, member),
                device_id_type=MESH,
            )
            for p, (mine_out, target) in enumerate(zip(out_mine, out_whole))
            for k in range(1, depth)
        ]

    @pl.when(z == member)
    def _():
        for copy in root_copies():
            copy.start()
        for mine_out, target in zip(out_mine, out_whole):
            target[x] = mine_out[...]

    for copy in near_copies:
        copy.wait_recv()
    own_rows = table_rows.shape[0]
    first_row = ((group * members + member) * own_rows).astype(jnp.float32)
    capacity = asked.shape[3]
    half_slots = depth * capacity

    def lookup(r, half):
        line = jnp.concatenate([asked[r, group_at(step)] for step in halves()[half]], axis=1)
        line = line.astype(jnp.float32) - first_row
        line = jnp.broadcast_to(line, (8, half_slots)).T[:, 0:1]
        place = lax.broadcasted_iota(jnp.int32, (half_slots, own_rows), 1)
        hot = (line == place.astype(jnp.float32)).astype(jnp.bfloat16)
        return nn(hot, table_rows[...])

    total = Total(out_a, into_a, total_a, 0, 2)
    for half in range(2):
        total.give_far(half, lookup(3, half))
        total.give_facing(half, lookup(2, half))
    for half in range(2):
        total.give_beside(half, lookup(1, half))
    own = [lookup(0, half) for half in range(2)]
    small_spread.hand_on()

    @pl.when(z != member)
    def _():
        for p in range(2):
            pltpu.make_async_remote_copy(
                src_ref=out_mine[p],
                dst_ref=out_whole[p].at[x],
                send_sem=out_sems[0].at[p, 0],
                recv_sem=out_sems[1].at[p, 0],
                device_id=beside,
                device_id_type=MESH,
            ).wait_recv()

    out_copies = [
        pltpu.make_async_remote_copy(
            src_ref=target.at[x],
            dst_ref=target.at[x],
            send_sem=out_sems[0].at[p, depth],
            recv_sem=out_sems[1].at[p, 1],
            device_id=beside,
            device_id_type=MESH,
        )
        for p, target in enumerate(out_whole)
    ]
    for copy in out_copies:
        copy.start()
    row_copies = []
    for half, steps in enumerate(halves()):
        rows_found = total.take(half, own[half]).astype(jnp.bfloat16)
        found[half * depth : (half + 1) * depth] = rows_found.reshape(depth, capacity, -1)
        for n, step in enumerate(steps):
            slot = half * depth + n
            if step == (0, 0):
                returned[group] = found[slot]
            else:
                row_copies.append(
                    send(
                        found.at[slot],
                        returned.at[group],
                        row_sems,
                        slot,
                        (group_at(step), member),
                    )
                )
        if half == 0:
            spreads[0].hand_on()
    small_spread.arrive()
    for layer, target in enumerate(norms):
        half = target.shape[1] // 2
        for c in range(groups):
            start = (c % 2) * half
            target[c // 2 : c // 2 + 1, start : start + half] = small_all[
                c, 8:9, layer * half : (layer + 1) * half
            ]
    counts = small_all[0, 9:10, :]
    for c in range(1, groups):
        counts = counts + small_all[c, 9:10, :]
    same = jnp.sum(counts * small[9:10, :], axis=1, keepdims=True)
    scale[...] = groups / (STUDY_TOTAL * same)
    level_rows = 8 * groups
    level_full = jnp.concatenate([small_all[c, 0:8, :] for c in range(groups)], axis=0)
    rows = hidden.shape[0]
    level_place = lax.broadcasted_iota(jnp.int32, (rows, level_rows), 1)
    level_hot = (levels[...] == level_place).astype(jnp.bfloat16)
    level_part = nn(level_hot, level_full.astype(jnp.bfloat16))
    slot_place = lax.broadcasted_iota(jnp.int32, (rows, groups * capacity), 1)
    slot_hot = (codes[...] == slot_place).astype(jnp.bfloat16)
    for copy in row_copies:
        copy.wait_recv()
    hidden[...] = nn(slot_hot, rows_joined(returned)) + level_part

    for copy in [*id_copies, *near_copies, *row_copies]:
        copy.wait_send()
    total.finish()
    for spread in spreads:
        spread.arrive()
    for spread in (small_spread, *spreads):
        spread.finish()
    for copy in out_copies:
        copy.wait()

    @pl.when(z == member)
    def _():
        for copy in root_copies():
            copy.wait_send()


def end_kernel(*refs):
    refs = iter(refs)
    take = lambda count: [next(refs) for _ in range(count)]
    gradient, codes, levels, asked, qkv_pair, out_pair = take(6)
    norm_zero, norm_one, qkv_one, out_one = take(4)
    row_grad, hits, qkv_sum, out_sum, small_sum = take(5)
    slots, arrived, small_g, small_in, qkv_out, qkv_in, out_out, out_in = take(8)
    qkv_come, small_near, small_come, mix_come = take(4)
    mix_sems, qkv_sems, small_sems, gather_sems, row_sems, mate_sems = [take(2) for _ in range(6)]
    group, member = lax.axis_index("dp"), lax.axis_index("mp")
    groups, members = lax.axis_size("dp"), lax.axis_size("mp")
    depth = groups // 2
    z, x = columns_of(group)
    peers, near = group_peers(), mates()
    greet([*peers, *near])
    rows, width = gradient.shape
    capacity = slots.shape[1]
    count = groups * capacity
    half_count = depth * capacity

    slot_place = lax.broadcasted_iota(jnp.int32, (rows, count), 1)
    slot_hot = (codes[...] == slot_place).astype(jnp.bfloat16)
    high = gradient[...].astype(jnp.bfloat16)
    slots[...] = tn(slot_hot, high).astype(jnp.bfloat16).reshape(slots.shape)
    row_copies = []
    for half, steps in enumerate(halves()):
        copies = []
        for n, step in enumerate(steps):
            slot = half * depth + n
            target = arrived.at[pl.ds(slot * capacity, capacity)]
            if step == (0, 0):
                arrived[slot * capacity : (slot + 1) * capacity, :] = slots[group]
            else:
                there = group_at(step)
                copies.append(send(slots.at[there], target, row_sems, slot, (there, member)))
        row_copies.append(copies)
    qkv_reduce = Reduce(None, qkv_pair, qkv_come, qkv_sems, 0)
    qkv_reduce.middle()
    mix = MixReduce(None, out_pair, mix_come, mix_sems, 0)
    mix.middle()

    level_place = lax.broadcasted_iota(jnp.int32, (rows, 8 * groups), 1)
    level_hot = (levels[...] == level_place).astype(jnp.bfloat16)
    rest = (gradient[...] - high.astype(jnp.float32)).astype(jnp.bfloat16)
    level_grad = tn(level_hot, high) + tn(level_hot, rest)
    half_width = width // 2
    for c in range(groups):
        small_g[c // 2, c % 2, 0:8, :] = level_grad[c * 8 : (c + 1) * 8, :]
        start = (c % 2) * half_width
        for layer, source in enumerate((norm_zero, norm_one)):
            small_g[c // 2, c % 2, 8:9, layer * half_width : (layer + 1) * half_width] = source[
                c // 2 : c // 2 + 1, start : start + half_width
            ]
        small_g[c // 2, c % 2, 9:16, :] = jnp.zeros((7, width), jnp.float32)
    small_reduce = Reduce(small_g, small_near, small_come, small_sems, 0)

    gather = Gather(arrived, gather_sems, 0, 2)
    for half in range(2):
        for copy in row_copies[half]:
            copy.wait_recv()
        gather.start(half)
        if half == 0:
            small_reduce.middle()

    own_rows = row_grad.shape[0]
    first_row = (group * members + member) * own_rows

    def collect(blocks, which):
        line = jnp.concatenate(
            [
                asked[r, group_at(step, back=True)]
                for r in blocks
                for half in which
                for step in halves()[half]
            ],
            axis=1,
        )
        line = line - first_row
        slots_here = line.shape[1]
        place = lax.broadcasted_iota(jnp.int32, (own_rows, slots_here), 0)
        hot = (line == place).astype(jnp.float32)
        source = jnp.concatenate(
            [
                arrived[pl.ds(r * count + half * half_count, half_count), :]
                for r in blocks
                for half in which
            ],
            axis=0,
        )
        part = nn(hot.astype(jnp.bfloat16), source)
        found = jnp.sum(hot, axis=1, keepdims=True)
        if blocks[0]:
            row_grad[...] += part
            hits[...] += found
        else:
            row_grad[...] = part
            hits[...] = found

    gather.wait_beside()
    collect([0, 1], [0, 1])
    gather.hand_on(0)

    small_in[member] = small_reduce.finish()
    out_out[0] = mix.finish().astype(jnp.bfloat16)
    out_out[1] = out_one[...].astype(jnp.bfloat16)
    qkv_out[0] = qkv_reduce.finish().astype(jnp.bfloat16)
    qkv_out[1] = qkv_one[...].astype(jnp.bfloat16)
    gather.hand_on(1)
    mate_copies = []
    for k, mate in enumerate(near):
        mate_copies.append(send(qkv_out, qkv_in.at[member], mate_sems, k, mate))
        mate_copies.append(
            send(small_in.at[member], small_in.at[member], mate_sems, members + k, mate)
        )
    qkv_in[member] = qkv_out[...]

    def root_copies(number=members - 1):
        return [
            pltpu.make_async_remote_copy(
                src_ref=out_out,
                dst_ref=out_in,
                send_sem=mate_sems[0].at[2 * members + k],
                recv_sem=mate_sems[1].at[2 * members],
                device_id=near[k],
                device_id_type=MESH,
            )
            for k in range(number)
        ]

    @pl.when(z == member)
    def _():
        for copy in root_copies():
            copy.start()
        out_in[...] = out_out[...]

    gather.wait_handed(0)
    collect([2, 3], [0])
    gather.wait_handed(1)
    collect([2, 3], [1])

    @pl.when(z != member)
    def _():
        root_copies(1)[0].wait_recv()

    for copy in mate_copies:
        copy.wait_recv()
    out_sum[...] = out_in[...].astype(jnp.float32)
    total = small_in[0]
    for m in range(1, members):
        total = total + small_in[m]
    small_sum[...] = total
    share = qkv_out.shape[2] // 3
    for layer in range(2):
        for m in range(members):
            part = qkv_in[m, layer].astype(jnp.float32)
            for c in range(3):
                qkv_sum[layer, c, :, m * share : (m + 1) * share] = part[
                    :, c * share : (c + 1) * share
                ]

    for copy in [*sum(row_copies, []), *mate_copies]:
        copy.wait_send()
    gather.finish()

    @pl.when(z == member)
    def _():
        for copy in root_copies():
            copy.wait_send()


def run_kernel(kernel, collective_id, name, inputs, outputs, scratch, flops=0, exps=0):
    moved = sum(math.prod(a.shape) * a.dtype.itemsize for a in inputs)
    return pl.pallas_call(
        kernel,
        out_shape=[jax.ShapeDtypeStruct(*o) for o in outputs],
        in_specs=[pl.BlockSpec(memory_space=pltpu.VMEM)] * len(inputs),
        out_specs=[pl.BlockSpec(memory_space=pltpu.VMEM)] * len(outputs),
        scratch_shapes=scratch,
        compiler_params=pltpu.CompilerParams(
            collective_id=collective_id, has_side_effects=True, vmem_limit_bytes=60 * 2**20
        ),
        cost_estimate=pl.CostEstimate(flops=flops, bytes_accessed=moved, transcendentals=exps),
        name=name,
    )(*inputs)


def run_layers(hidden, cotangent, scale, norms, qkv_zero, out_w, mine):
    rows, width = hidden.shape
    cell = 4 * rows
    groups, part, columns = qkv_zero.shape
    depth = groups // 2
    share = columns // 3
    per_device = share // HD
    units = mine[0].shape[1]
    f32, low = jnp.float32, jnp.bfloat16
    outputs = [
        ((rows, width), f32),
        ((rows, width), f32),
        ((4, width), f32),
        ((4, width), f32),
        ((depth, part, columns), low),
        ((part, width), low),
        ((part, units), f32),
        ((part, units), f32),
        ((units, part), f32),
        ((units, part), f32),
        ((part, columns), f32),
        ((part, width), f32),
    ]
    kept = [
        pltpu.VMEM((rows, width), f32),
        pltpu.VMEM((rows, 1), f32),
        pltpu.VMEM((rows, width), f32),
        pltpu.VMEM((rows, 1), f32),
        pltpu.VMEM((cell, width), low),
        pltpu.VMEM((3 * per_device, cell, HD), low),
        pltpu.VMEM((cell, share), low),
        pltpu.VMEM((4 * per_device, 1, rows), f32),
        pltpu.VMEM((cell, width), low),
        pltpu.VMEM((cell, units), low),
        pltpu.VMEM((cell, units), low),
    ]
    scratch = [pltpu.VMEM((groups, *piece.shape), low) for piece in mine] + kept * 2
    scratch += [
        pltpu.VMEM((share, rows), f32),
        pltpu.VMEM((rows, width), f32),
        pltpu.VMEM((3, rows, width), low),
        pltpu.VMEM((3, rows, width), low),
        pltpu.VMEM((cell, width), low),
        pltpu.VMEM((cell, units), low),
        pltpu.VMEM((cell, width), low),
        pltpu.VMEM((per_device, cell, HD), low),
        pltpu.VMEM((per_device, cell, HD), f32),
        pltpu.VMEM((per_device, cell, HD), f32),
        pltpu.VMEM((per_device, cell, HD), low),
        pltpu.VMEM((cell, columns), low),
        pltpu.VMEM((depth, 2, part, units), low),
        pltpu.VMEM((depth, 2, part, units), low),
        pltpu.VMEM((depth, 2, part, columns), low),
        pltpu.VMEM((2, part, width), low),
    ]
    near, come = reduce_scratch(part, units, low)
    scratch += [near, near, come] * 2 + reduce_scratch(part, columns, low)
    scratch += [pltpu.VMEM((part, width), low), pltpu.VMEM((depth - 1, part, width), low)]
    scratch += dma_sems(8, 3 * PIECES) + dma_sems(8, 3 * PIECES) + dma_sems(5, 2 * depth - 1)
    scratch += dma_sems(2, depth) * 4
    flops = 12 * cell * width * (4 * share + 2 * units) + 28 * cell * cell * share
    return run_kernel(
        layers_kernel,
        1,
        "layers",
        [hidden, cotangent, scale, *norms, qkv_zero, *out_w, *mine],
        outputs,
        scratch,
        flops,
        4 * cell * cell * per_device,
    )


def table_kernel_stacked(weight, moments, gradient, hits, new_weight, new_moments):
    touched = hits[...] > 0
    grad = gradient[...]
    old, old_first, old_second = weight[0], moments[0, 0], moments[1, 0]
    first = beta_one * old_first + (1.0 - beta_one) * grad
    second = beta_two * old_second + (1.0 - beta_two) * grad * grad
    first_hat = first / (1.0 - beta_one**STEP)
    second_hat = second / (1.0 - beta_two**STEP)
    new = old - rate_table * (first_hat / (jnp.sqrt(second_hat) + adam_eps) + decay_rate * old)
    new_weight[0] = jnp.where(touched, new, old)
    new_moments[0, 0] = jnp.where(touched, first, old_first)
    new_moments[1, 0] = jnp.where(touched, second, old_second)


def update_tables(tables, moments, row_grad, hits):
    count, own_rows, width = tables.shape
    step = own_rows // 3
    table_block = pl.BlockSpec((1, step, width), lambda i, t: (t, i, 0))
    moment_block = pl.BlockSpec((2, 1, step, width), lambda i, t: (0, t, i, 0))
    return pl.pallas_call(
        table_kernel_stacked,
        grid=(own_rows // step, count),
        in_specs=[
            table_block,
            moment_block,
            pl.BlockSpec((step, width), lambda i, t: (i, 0)),
            pl.BlockSpec((step, 1), lambda i, t: (i, 0)),
        ],
        out_specs=[table_block, moment_block],
        out_shape=[
            jax.ShapeDtypeStruct(tables.shape, tables.dtype),
            jax.ShapeDtypeStruct(moments.shape, moments.dtype),
        ],
        compiler_params=pltpu.CompilerParams(vmem_limit_bytes=56 * 2**20),
        cost_estimate=pl.CostEstimate(
            flops=20 * tables.size, bytes_accessed=24 * tables.size, transcendentals=tables.size
        ),
        name="table_update",
    )(tables, moments, row_grad, hits)


def fast_body(
    gene_ids,
    levels,
    study_of_cell,
    cotangent,
    tables,
    table_moments,
    level_table,
    level_moments,
    qkv_weight,
    qkv_moments,
    out_weight,
    out_moments,
    in_weight,
    in_moments,
    back_weight,
    back_moments,
    norm_params,
    norm_moments,
):
    low = jnp.bfloat16
    groups = lax.axis_size("dp")
    members = lax.axis_size("mp")
    member = lax.axis_index("mp")
    rows_here, width = cotangent.shape
    layers = qkv_weight.shape[0]
    local_cells = study_of_cell.shape[0]
    capacity = 2 * rows_here // groups
    own_rows = tables.shape[1]
    block_size = own_rows * members
    depth = qkv_weight.shape[2]
    share = width // members
    units = in_weight.shape[2]

    assert groups == 2 * members and layers == 2 and local_cells == 1
    f32 = jnp.float32
    qkv_mine = lax.dynamic_slice_in_dim(qkv_weight, member * share, share, axis=3).astype(low)
    qkv_mine = qkv_mine.transpose(0, 2, 1, 3).reshape(layers, depth, 3 * share)
    out_mine = out_weight.astype(low)
    in_mine = in_weight.astype(low)
    back_mine = back_weight.astype(low).transpose(0, 2, 1)
    level_rows = level_table.shape[0]
    study_onehot = (study_of_cell[:, None] == jnp.arange(width)[None, :]).astype(f32)
    small = jnp.concatenate(
        [
            level_table.astype(low).astype(f32),
            norm_params.reshape(1, width),
            study_onehot,
            jnp.zeros((16 - level_rows - 2, width), f32),
        ]
    )
    row_owner = gene_ids // block_size
    slot_index = slots_of(row_owner)
    sent_ids = slotted_ids(gene_ids, row_owner, slot_index, groups, capacity)
    codes = (row_owner * capacity + slot_index)[:, None]
    level_column = levels[:, None]
    summed_tables = jnp.sum(tables, axis=0).astype(low)

    slots = groups * capacity
    copies = 2 * (groups // 2) - 1
    dma = pltpu.SemaphoreType.DMA
    hidden, asked, scale, *more = run_kernel(
        start_kernel,
        5,
        "start",
        [
            sent_ids[:, None, :],
            codes,
            level_column,
            summed_tables,
            small,
            qkv_mine[0],
            out_mine[0],
            out_mine[1],
        ],
        [
            ((rows_here, width), f32),
            ((members, groups, 1, capacity), jnp.int32),
            ((1, 1), f32),
            ((4, width), f32),
            ((4, width), f32),
            ((groups, depth, 3 * share), low),
            ((2, depth, width), low),
            ((2, depth, width), low),
        ],
        [
            pltpu.VMEM((groups, 16, width), f32),
            pltpu.VMEM((groups, capacity, width), low),
            pltpu.VMEM((groups, capacity, width), low),
            pltpu.VMEM((3, slots, width), low),
            pltpu.VMEM((3, slots, width), low),
        ]
        + dma_sems(1, 3 * 2)
        + [dma((1, copies))] * 2
        + [dma((1, copies))] * 2
        + [dma((2, groups // 2 + 1))] * 2
        + [dma((groups - 1,))] * 2
        + [dma((3,))] * 2
        + [dma((groups,))] * 2,
    )
    norms, qkv_w, out_w = more[0:2], more[2], more[3:5]
    hidden, gradient, norm_zero, norm_one, qkv_pair, out_pair, *more = run_layers(
        hidden,
        cotangent,
        scale,
        norms,
        qkv_w,
        out_w,
        [in_mine[0], back_mine[0], qkv_mine[1], in_mine[1], back_mine[1]],
    )
    in_zero, in_one, back_zero, back_one, qkv_one, out_one = more
    row_grad, hits, qkv_sum, out_sum, small_sum = run_kernel(
        end_kernel,
        6,
        "finish",
        [
            gradient,
            codes,
            level_column,
            asked,
            qkv_pair,
            out_pair,
            norm_zero,
            norm_one,
            qkv_one,
            out_one,
        ],
        [
            ((own_rows, width), f32),
            ((own_rows, 1), f32),
            ((layers, 3, depth, width), f32),
            ((layers, depth, width), f32),
            ((16, width), f32),
        ],
        [
            pltpu.VMEM((groups, capacity, width), low),
            pltpu.VMEM((4 * slots, width), low),
            pltpu.VMEM((groups // 2, 2, 16, width), f32),
            pltpu.VMEM((members, 16, width), f32),
            pltpu.VMEM((2, depth, 3 * share), low),
            pltpu.VMEM((members, 2, depth, 3 * share), low),
            pltpu.VMEM((2, depth, width), low),
            pltpu.VMEM((2, depth, width), low),
        ]
        + reduce_scratch(depth, 3 * share, low)[1:]
        + reduce_scratch(16, width, f32)
        + [pltpu.VMEM((groups // 2 - 1, depth, width), low)]
        + dma_sems(1, groups // 2) * 3
        + dma_sems(1, 3 * 2)
        + [dma((groups,))] * 2
        + [dma((3 * members,))] * 2,
    )

    table_new, table_state = update_tables(tables, table_moments, row_grad, hits)
    level_sum = small_sum[:level_rows]
    norm_sum = small_sum[level_rows].reshape(layers, -1)
    in_sum = jnp.stack([in_zero, in_one])
    back_sum = jnp.stack([back_zero, back_one])
    level_new, level_state = adam_step(
        level_table, level_moments, level_sum, rate_table, decay_rate
    )
    qkv_new, qkv_state = adam_step(qkv_weight, qkv_moments, qkv_sum, rate_dense, decay_rate)
    out_new, out_state = adam_step(out_weight, out_moments, out_sum, rate_mixing, decay_rate)
    in_new, in_state = adam_step(in_weight, in_moments, in_sum, rate_dense, decay_rate)
    back_new, back_state = adam_step(back_weight, back_moments, back_sum, rate_dense, decay_rate)
    norm_new, norm_state = adam_step(norm_params, norm_moments, norm_sum, rate_norm, 0.0)
    return (
        hidden,
        table_new,
        table_state,
        level_new,
        level_state,
        qkv_new,
        qkv_state,
        out_new,
        out_state,
        in_new,
        in_state,
        back_new,
        back_state,
        norm_new,
        norm_state,
    )


def solution(mesh):
    return jax.shard_map(
        fast_body if (mesh.shape["dp"], mesh.shape["mp"]) == (8, 4) else general_body,
        mesh=mesh,
        in_specs=(
            P(("dp", "mp")),
            P(("dp", "mp")),
            P("dp"),
            P(("dp", "mp"), None),
            P(None, ("dp", "mp"), None),
            P(None, None, ("dp", "mp"), None),
            P("dp", None),
            P(None, "dp", None),
            P(None, None, "dp", None),
            P(None, None, None, "dp", None),
            P(None, "dp", None),
            P(None, None, "dp", None),
            P(None, "dp", "mp"),
            P(None, None, "dp", "mp"),
            P(None, "mp", "dp"),
            P(None, None, "mp", "dp"),
            P(None, "dp"),
            P(None, None, "dp"),
        ),
        out_specs=(
            P(("dp", "mp"), None),
            P(None, ("dp", "mp"), None),
            P(None, None, ("dp", "mp"), None),
            P("dp", None),
            P(None, "dp", None),
            P(None, None, "dp", None),
            P(None, None, None, "dp", None),
            P(None, "dp", None),
            P(None, None, "dp", None),
            P(None, "dp", "mp"),
            P(None, None, "dp", "mp"),
            P(None, "mp", "dp"),
            P(None, None, "mp", "dp"),
            P(None, "dp"),
            P(None, None, "dp"),
        ),
        check_vma=False,
    )
```

```python
import math
from functools import partial

import jax
import jax.numpy as jnp
from jax import lax
from jax.experimental import pallas as pl
from jax.experimental.pallas import tpu as pltpu
from jax.sharding import PartitionSpec as P

HEADS = 12
HD = 64
STUDY_TOTAL = 16
STEP = 10


largest_value = lax.Precision.HIGHEST
beta_one = 0.9
beta_two = 0.999
adam_eps = 1e-08
norm_eps = 1e-05
rate_dense = 0.08
rate_mixing = 0.3
rate_table = 0.6
rate_norm = 0.4
decay_rate = 0.01


def spread_rows(rows):
    return lax.all_gather(rows, "mp", axis=0, tiled=True)


def summed_rows(term, count):
    return lax.psum_scatter(
        term(jnp.int32(0), count * lax.axis_size("mp")).astype(jnp.bfloat16),
        "mp",
        scatter_dimension=0,
        tiled=True,
    ).astype(jnp.float32)


def norm_forward(rows, gain, bias):
    centered = rows - jnp.mean(rows, axis=-1, keepdims=True)
    inverse = lax.rsqrt(jnp.mean(centered * centered, axis=-1, keepdims=True) + norm_eps)
    normal = centered * inverse
    return (normal * gain + bias, normal, inverse)


def norm_backward(gradient, normal, inverse, gain):
    scaled = gradient * gain
    inner_part = (
        scaled
        - jnp.mean(scaled, axis=-1, keepdims=True)
        - normal * jnp.mean(scaled * normal, axis=-1, keepdims=True)
    )
    return (inner_part * inverse, jnp.sum(gradient * normal, axis=0), jnp.sum(gradient, axis=0))


def gelu_grad(inner, gradient):
    return jax.vjp(partial(jax.nn.gelu, approximate=False), inner)[1](gradient)[0]


def head_major(rows):
    return rows.reshape(rows.shape[0], HEADS, HD).transpose(1, 0, 2)


def row_major(heads):
    return heads.transpose(1, 0, 2).reshape(heads.shape[1], HEADS * HD)


def attend_forward(query, keys, values):
    scale = HD ** (-0.5)

    def one_head(pieces):
        head_query, head_keys, head_values = pieces
        scores = (
            jnp.einsum("qd,kd->qk", head_query, head_keys, preferred_element_type=jnp.float32)
            * scale
        )
        peak = jnp.max(scores, axis=-1, keepdims=True)
        raised = jnp.exp(scores - peak)
        total = jnp.sum(raised, axis=-1, keepdims=True)
        probs = (raised / total).astype(jnp.bfloat16)
        mixed = jnp.dot(probs, head_values, preferred_element_type=jnp.float32).astype(jnp.bfloat16)
        return (mixed, (peak + jnp.log(total))[:, 0])

    mixed, log_total = lax.map(one_head, (head_major(query), head_major(keys), head_major(values)))
    return (row_major(mixed), log_total)


def attend_backward(query, keys, values, mixed_grad, log_total):
    scale = HD ** (-0.5)

    def one_head(pieces):
        head_query, head_keys, head_values, head_grad, head_total = pieces
        scores = (
            jnp.einsum("qd,kd->qk", head_query, head_keys, preferred_element_type=jnp.float32)
            * scale
        )
        probs = jnp.exp(scores - head_total[:, None])
        product = jnp.einsum(
            "qd,kd->qk", head_grad, head_values, preferred_element_type=jnp.float32
        )
        center = jnp.sum(probs * product, axis=-1, keepdims=True)
        score_grad = (probs * (product - center)).astype(jnp.bfloat16)
        query_grad = (
            jnp.dot(score_grad, head_keys, preferred_element_type=jnp.float32) * scale
        ).astype(jnp.bfloat16)
        key_grad = (
            jnp.einsum("qk,qd->kd", score_grad, head_query, preferred_element_type=jnp.float32)
            * scale
        )
        value_grad = jnp.einsum(
            "qk,qd->kd", probs.astype(jnp.bfloat16), head_grad, preferred_element_type=jnp.float32
        )
        return (query_grad, key_grad, value_grad)

    query_grad, key_grad, value_grad = lax.map(
        one_head,
        (
            head_major(query),
            head_major(keys),
            head_major(values),
            head_major(mixed_grad),
            log_total,
        ),
    )
    return (row_major(query_grad), jnp.stack([row_major(key_grad), row_major(value_grad)], axis=1))


def slots_of(row_owner):
    place = jnp.arange(row_owner.shape[0])
    earlier = (row_owner[:, None] == row_owner[None, :]) & (place[None, :] < place[:, None])
    return jnp.sum(earlier.astype(jnp.int32), axis=1)


def slotted_ids(gene_ids, row_owner, slot_index, cell_groups, capacity):
    code = row_owner * capacity + slot_index
    hot = code[None, :] == jnp.arange(cell_groups * capacity)[:, None]
    found = jnp.sum(jnp.where(hot, gene_ids[None, :] + 1, 0), axis=1) - 1
    return found.reshape(cell_groups, capacity)


def adam_step(weight, moments, gradient, rate, decay):
    first = beta_one * moments[0] + (1.0 - beta_one) * gradient
    second = beta_two * moments[1] + (1.0 - beta_two) * gradient * gradient
    first_hat = first / (1.0 - beta_one**STEP)
    second_hat = second / (1.0 - beta_two**STEP)
    new_weight = weight - rate * (first_hat / (jnp.sqrt(second_hat) + adam_eps) + decay * weight)
    return (new_weight, jnp.stack([first, second]))


def general_body(
    gene_ids,
    levels,
    study_of_cell,
    cotangent,
    tables,
    table_moments,
    level_table,
    level_moments,
    qkv_weight,
    qkv_moments,
    out_weight,
    out_moments,
    in_weight,
    in_moments,
    back_weight,
    back_moments,
    norm_params,
    norm_moments,
):
    cell_groups = lax.axis_size("dp")
    rows_here = cotangent.shape[0]
    model_width = cotangent.shape[1]
    layers = qkv_weight.shape[0]
    local_cells = study_of_cell.shape[0]
    capacity = 2 * rows_here // cell_groups
    own_rows = tables.shape[1]
    block_size = own_rows * lax.axis_size("mp")
    qkv_full, out_full, in_part, back_part, level_full = (
        lax.all_gather(qkv_weight.astype(jnp.bfloat16), "dp", axis=2, tiled=True),
        lax.all_gather(out_weight.astype(jnp.bfloat16), "dp", axis=1, tiled=True),
        lax.all_gather(in_weight.astype(jnp.bfloat16), "dp", axis=1, tiled=True),
        lax.all_gather(back_weight.astype(jnp.bfloat16), "dp", axis=2, tiled=True),
        lax.all_gather(level_table.astype(jnp.bfloat16), "dp", axis=0, tiled=True),
    )
    study_onehot = (study_of_cell[:, None] == jnp.arange(STUDY_TOTAL)[None, :]).astype(jnp.float32)
    norm_full, study_all = (
        lax.all_gather(norm_params, "dp", axis=1, tiled=True),
        lax.all_gather(study_onehot, "dp", axis=0, tiled=True),
    )
    cells_per_study = jnp.sum(study_all, axis=0)
    cell_balance_weight = (
        cell_groups
        * local_cells
        / (STUDY_TOTAL * jnp.dot(study_onehot, cells_per_study, precision=largest_value))
    )
    out_grad = cotangent * cell_balance_weight[0]
    summed_tables = jnp.sum(tables, axis=0).astype(jnp.bfloat16)
    table_rows = lax.all_gather(summed_tables, "mp", axis=0, tiled=True)
    row_owner = gene_ids // block_size
    slot_index = slots_of(row_owner)
    sent_ids = slotted_ids(gene_ids, row_owner, slot_index, cell_groups, capacity)
    asked_ids = lax.all_to_all(sent_ids, "dp", split_axis=0, concat_axis=0, tiled=True)
    present = asked_ids >= 0
    safe_row = jnp.where(present, asked_ids - lax.axis_index("dp") * block_size, 0)
    found_rows = jnp.where(present[..., None], jnp.take(table_rows, safe_row, axis=0), 0)
    returned = lax.all_to_all(found_rows, "dp", split_axis=0, concat_axis=0, tiled=True)
    gene_part = returned[row_owner, slot_index].astype(jnp.float32)
    level_hot = (levels[:, None] == jnp.arange(level_full.shape[0])[None, :]).astype(jnp.bfloat16)
    hidden = gene_part + jnp.dot(level_hot, level_full, preferred_element_type=jnp.float32)
    kept = []
    for layer in range(layers):
        norm_row = norm_full[layer]
        tokens_low = hidden.astype(jnp.bfloat16)
        projected = jnp.einsum(
            "td,cdh->tch", tokens_low, qkv_full[layer], preferred_element_type=jnp.float32
        ).astype(jnp.bfloat16)
        query = projected[:, 0]
        cell_rows = spread_rows(projected[:, 1:])
        keys, values = (cell_rows[:, 0], cell_rows[:, 1])
        mixed, log_total = attend_forward(query, keys, values)
        attention = jnp.dot(mixed, out_full[layer], preferred_element_type=jnp.float32)
        first, first_normal, first_inverse = norm_forward(
            hidden + attention, norm_row[:model_width], norm_row[model_width : 2 * model_width]
        )
        first_low = first.astype(jnp.bfloat16)
        in_layer, back_layer = (in_part[layer], back_part[layer])
        first_spread = spread_rows(first_low)
        inner = jnp.dot(first_spread, in_layer, preferred_element_type=jnp.float32)
        active = jax.nn.gelu(inner, approximate=False).astype(jnp.bfloat16)

        def feed_term(start, count):
            return jnp.dot(active, back_layer, preferred_element_type=jnp.float32)

        feed = summed_rows(feed_term, rows_here)
        second, second_normal, second_inverse = norm_forward(
            first + feed, norm_row[2 * model_width : 3 * model_width], norm_row[3 * model_width :]
        )
        kept.append(
            (
                tokens_low,
                query,
                keys,
                values,
                mixed,
                log_total,
                first_normal,
                first_inverse,
                first_spread,
                inner,
                active,
                in_layer,
                back_layer,
                second_normal,
                second_inverse,
            )
        )
        hidden = second
    gradient = out_grad
    qkv_grads = [None] * layers
    out_grads = [None] * layers
    in_grads = [None] * layers
    back_grads = [None] * layers
    norm_grads = [None] * layers
    for layer in reversed(range(layers)):
        (
            tokens_low,
            query,
            keys,
            values,
            mixed,
            log_total,
            first_normal,
            first_inverse,
            first_spread,
            inner,
            active,
            in_layer,
            back_layer,
            second_normal,
            second_inverse,
        ) = kept[layer]
        norm_row = norm_full[layer]
        grad_second, gain_two, bias_two = norm_backward(
            gradient, second_normal, second_inverse, norm_row[2 * model_width : 3 * model_width]
        )
        feed_low = grad_second.astype(jnp.bfloat16)
        feed_spread = spread_rows(feed_low)
        back_grads[layer] = jnp.einsum(
            "tf,td->fd", active, feed_spread, preferred_element_type=jnp.float32
        )
        active_grad = jnp.einsum(
            "td,fd->tf", feed_spread, back_layer, preferred_element_type=jnp.float32
        )
        inner_grad = gelu_grad(inner, active_grad).astype(jnp.bfloat16)
        in_grads[layer] = jnp.einsum(
            "td,tf->df", first_spread, inner_grad, preferred_element_type=jnp.float32
        )

        def first_term(start, count):
            return jnp.einsum("tf,df->td", inner_grad, in_layer, preferred_element_type=jnp.float32)

        first_grad = summed_rows(first_term, rows_here)
        grad_first, gain_one, bias_one = norm_backward(
            grad_second + first_grad, first_normal, first_inverse, norm_row[:model_width]
        )
        norm_grads[layer] = jnp.concatenate([gain_one, bias_one, gain_two, bias_two])
        attention_low = grad_first.astype(jnp.bfloat16)
        out_grads[layer] = jnp.einsum(
            "th,td->hd", mixed, attention_low, preferred_element_type=jnp.float32
        )
        mixed_grad = jnp.einsum(
            "td,hd->th", attention_low, out_full[layer], preferred_element_type=jnp.float32
        ).astype(jnp.bfloat16)
        query_grad, pair_partial = attend_backward(query, keys, values, mixed_grad, log_total)
        pair_grad = lax.psum_scatter(
            pair_partial.astype(jnp.bfloat16), "mp", scatter_dimension=0, tiled=True
        )
        stacked = jnp.concatenate([query_grad[:, None, :], pair_grad], axis=1)
        qkv_grads[layer] = jnp.einsum(
            "td,tch->cdh", tokens_low, stacked, preferred_element_type=jnp.float32
        )
        gradient = grad_first + jnp.einsum(
            "tch,cdh->td", stacked, qkv_full[layer], preferred_element_type=jnp.float32
        )
    level_grad = jnp.dot(level_hot.astype(jnp.float32).T, gradient, precision=largest_value)
    grad_slots = (
        jnp.zeros((cell_groups, capacity, model_width), jnp.float32)
        .at[row_owner, slot_index]
        .set(gradient)
    )
    arrived = lax.all_to_all(
        grad_slots.astype(jnp.bfloat16), "dp", split_axis=0, concat_axis=0, tiled=True
    ).astype(grad_slots.dtype)
    arrived = jnp.where(present[..., None], arrived, 0.0)
    flat_rows = safe_row.reshape(-1)
    block_grad = jax.ops.segment_sum(
        arrived.reshape(-1, model_width), flat_rows, num_segments=block_size
    )
    block_hits = jax.ops.segment_sum(
        present.reshape(-1).astype(jnp.float32), flat_rows, num_segments=block_size
    )
    row_grad, hits = (
        lax.psum_scatter(
            block_grad.astype(jnp.bfloat16), "mp", scatter_dimension=0, tiled=True
        ).astype(jnp.float32),
        lax.psum_scatter(
            block_hits.astype(jnp.bfloat16), "mp", scatter_dimension=0, tiled=True
        ).astype(jnp.float32),
    )
    qkv_sum, out_sum, in_sum, back_sum, level_sum, norm_sum = (
        lax.psum_scatter(
            jnp.stack(qkv_grads).astype(jnp.bfloat16), "dp", scatter_dimension=2, tiled=True
        ).astype(jnp.float32),
        lax.psum_scatter(
            jnp.stack(out_grads).astype(jnp.bfloat16), "dp", scatter_dimension=1, tiled=True
        ).astype(jnp.float32),
        lax.psum_scatter(
            jnp.stack(in_grads).astype(jnp.bfloat16), "dp", scatter_dimension=1, tiled=True
        ).astype(jnp.float32),
        lax.psum_scatter(
            jnp.stack(back_grads).astype(jnp.bfloat16), "dp", scatter_dimension=2, tiled=True
        ).astype(jnp.float32),
        lax.psum_scatter(
            level_grad.astype(jnp.bfloat16), "dp", scatter_dimension=0, tiled=True
        ).astype(jnp.float32),
        lax.psum_scatter(
            jnp.stack(norm_grads).astype(jnp.bfloat16), "dp", scatter_dimension=1, tiled=True
        ).astype(jnp.float32),
    )
    qkv_sum, out_sum, level_sum, norm_sum = (
        lax.psum(qkv_sum.astype(jnp.bfloat16), "mp").astype(jnp.float32),
        lax.psum(out_sum.astype(jnp.bfloat16), "mp").astype(jnp.float32),
        lax.psum(level_sum.astype(jnp.bfloat16), "mp").astype(jnp.float32),
        lax.psum(norm_sum.astype(jnp.bfloat16), "mp").astype(jnp.float32),
    )
    touched = (hits > 0)[None, :, None]
    table_grad = jnp.broadcast_to(row_grad[None], tables.shape)
    table_new, table_state = adam_step(tables, table_moments, table_grad, rate_table, decay_rate)
    table_new = jnp.where(touched, table_new, tables)
    table_state = jnp.where(touched[None], table_state, table_moments)
    level_new, level_state = adam_step(
        level_table, level_moments, level_sum, rate_table, decay_rate
    )
    qkv_new, qkv_state = adam_step(qkv_weight, qkv_moments, qkv_sum, rate_dense, decay_rate)
    out_new, out_state = adam_step(out_weight, out_moments, out_sum, rate_mixing, decay_rate)
    in_new, in_state = adam_step(in_weight, in_moments, in_sum, rate_dense, decay_rate)
    back_new, back_state = adam_step(back_weight, back_moments, back_sum, rate_dense, decay_rate)
    norm_new, norm_state = adam_step(norm_params, norm_moments, norm_sum, rate_norm, 0.0)
    return (
        hidden,
        table_new,
        table_state,
        level_new,
        level_state,
        qkv_new,
        qkv_state,
        out_new,
        out_state,
        in_new,
        in_state,
        back_new,
        back_state,
        norm_new,
        norm_state,
    )


MESH = pl.DeviceIdType.MESH
SIB, FACE = 0, 1
TILE = 128


def nn(a, b):
    return lax.dot_general(a, b, (((1,), (0,)), ((), ())), preferred_element_type=jnp.float32)


def nt(a, b):
    return lax.dot_general(a, b, (((1,), (1,)), ((), ())), preferred_element_type=jnp.float32)


def tn(a, b):
    return lax.dot_general(a, b, (((0,), (0,)), ((), ())), preferred_element_type=jnp.float32)


def near_devices():
    group, member = lax.axis_index("dp"), lax.axis_index("mp")
    core = member % 2
    return (group, member + 1 - 2 * core), (group, (member + 2) % 4)


def greet(peers):
    barrier = pltpu.get_barrier_semaphore()
    for peer in peers:
        pl.semaphore_signal(barrier, inc=1, device_id=peer, device_id_type=MESH)
    pl.semaphore_wait(barrier, len(peers))


def send(source, target, sems, index, peer):
    copy = pltpu.make_async_remote_copy(
        src_ref=source,
        dst_ref=target,
        send_sem=sems[0].at[index],
        recv_sem=sems[1].at[index],
        device_id=peer,
        device_id_type=MESH,
    )
    copy.start()
    return copy


PIECES = 2


def columns_of(group):
    return group // 2, group % 2


def group_peers():
    group, member = lax.axis_index("dp"), lax.axis_index("mp")
    count = lax.axis_size("dp")
    return [((group + k) % count, member) for k in range(1, count)]


def mates():
    group, member = lax.axis_index("dp"), lax.axis_index("mp")
    count = lax.axis_size("mp")
    return [(group, (member + k) % count) for k in range(1, count)]


class Spread:
    def __init__(self, mine, whole, sems, part):
        group, member = lax.axis_index("dp"), lax.axis_index("mp")
        depth = lax.axis_size("dp") // 2
        z, x = columns_of(group)
        self.beside = (group + 1 - 2 * x, member)
        self.whole, self.sems, self.part, self.depth = whole, sems, part, depth
        self.came = [((z + depth - k) % depth) * 2 + x for k in range(1, depth)]
        self.along = [
            send(mine, whole.at[group], sems, (part, k - 1), (((z + k) % depth) * 2 + x, member))
            for k in range(1, depth)
        ]
        self.across = [send(mine, whole.at[group], sems, (part, depth - 1), self.beside)]
        whole[group] = mine[...]

    def hand_on(self):
        for k in range(1, self.depth):
            self.along[k - 1].wait_recv()
            block = self.whole.at[self.came[k - 1]]
            self.across.append(
                send(block, block, self.sems, (self.part, self.depth - 1 + k), self.beside)
            )

    def arrive(self):
        for copy in self.across:
            copy.wait_recv()

    def finish(self):
        for copy in [*self.along, *self.across]:
            copy.wait_send()


class Reduce:
    def __init__(self, source, near, come, sems, line):
        group, self.member = lax.axis_index("dp"), lax.axis_index("mp")
        self.depth = lax.axis_size("dp") // 2
        self.z, self.x = columns_of(group)
        self.source, self.near, self.come = source, near, come
        self.sems, self.line, self.copies = sems, line, []
        if source is not None:
            beside = (group + 1 - 2 * self.x, self.member)
            self.first = send(source.at[:, 1 - self.x], near, sems, (line, 0), beside)

    def pair(self, z):
        term = self.near[z].astype(jnp.float32)
        return term if self.source is None else term + self.source[z, self.x].astype(jnp.float32)

    def add_up(self):
        self.first.wait_recv()
        for z in range(self.depth):
            self.near[z] = self.pair(z).astype(self.near.dtype)
        self.first.wait_send()

    def middle(self):
        if self.source is not None:
            self.first.wait_recv()
        for k in range(1, self.depth):
            z = (self.z + k) % self.depth
            if self.source is not None:
                self.near[z] = self.pair(z).astype(self.near.dtype)
            self.copies.append(
                send(
                    self.near.at[z],
                    self.come.at[k - 1],
                    self.sems,
                    (self.line, k),
                    (z * 2 + self.x, self.member),
                )
            )

    def finish(self):
        term = self.pair(self.z)
        for k, copy in enumerate(self.copies):
            copy.wait_recv()
            term = term + self.come[k].astype(jnp.float32)
        for copy in self.copies:
            copy.wait_send()
        if self.source is not None:
            self.first.wait_send()
        return term


def reduce_scratch(rows, columns, dtype):
    depth = lax.axis_size("dp") // 2
    return [pltpu.VMEM((depth, rows, columns), dtype), pltpu.VMEM((depth - 1, rows, columns), dtype)]


def dma_sems(*shape):
    return [pltpu.SemaphoreType.DMA(shape)] * 2


class MixReduce:
    def __init__(self, source, near, come, sems, line):
        group, self.member = lax.axis_index("dp"), lax.axis_index("mp")
        self.depth = lax.axis_size("dp") // 2
        self.z, self.x = columns_of(group)
        self.sems, self.line = sems, line
        self.source, self.near, self.come = source, near, come
        if source is not None:
            beside = (group + 1 - 2 * self.x, self.member)
            self.first = send(source.at[1 - self.x], near, sems, (line, 0), beside)

    def copy(self, slot, there):
        return pltpu.make_async_remote_copy(
            src_ref=self.near,
            dst_ref=self.come.at[slot],
            send_sem=self.sems[0].at[self.line, 1 + slot],
            recv_sem=self.sems[1].at[self.line, 1 + slot],
            device_id=(there, self.member),
            device_id_type=MESH,
        )

    def to_root(self):
        slot = (self.member + 2 * self.depth - self.z - 1) % self.depth
        return self.copy(slot, self.member * 2 + self.x)

    def add_up(self):
        self.first.wait_recv()
        term = self.source[self.x].astype(jnp.float32) + self.near[...].astype(jnp.float32)
        self.near[...] = term.astype(self.near.dtype)
        self.first.wait_send()

    def middle(self):
        if self.source is not None:
            self.add_up()

        @pl.when(self.z != self.member)
        def _():
            self.to_root().start()

    def finish(self):
        @pl.when(self.z == self.member)
        def _():
            for slot in range(self.depth - 1):
                self.copy(slot, (self.member * 2 + self.x + 2) % (2 * self.depth)).wait_recv()

        @pl.when(self.z != self.member)
        def _():
            self.to_root().wait_send()

        term = self.near[...].astype(jnp.float32)
        for slot in range(self.depth - 1):
            term = term + self.come[slot].astype(jnp.float32)
        return term


class Gather:
    def __init__(self, buf, sems, line, pieces=PIECES):
        self.buf, self.sems, self.line, self.pieces = buf, sems, line, pieces
        self.sib, self.face = near_devices()
        self.rows = buf.shape[0] // 4
        self.size = self.rows // pieces
        self.across, self.beside, self.handed = [], [], []

    def piece(self, b, i):
        return self.buf.at[pl.ds(b * self.rows + i * self.size, self.size)]

    def start(self, i):
        mine = self.piece(0, i)
        self.across.append(send(mine, self.piece(2, i), self.sems, (self.line, i), self.face))
        self.beside.append(
            send(mine, self.piece(1, i), self.sems, (self.line, self.pieces + i), self.sib)
        )

    def wait_beside(self):
        for copy in self.beside:
            copy.wait_recv()

    def hand_on(self, i):
        self.across[i].wait_recv()
        self.handed.append(
            send(
                self.piece(2, i),
                self.piece(3, i),
                self.sems,
                (self.line, 2 * self.pieces + i),
                self.sib,
            )
        )

    def wait_handed(self, i):
        self.handed[i].wait_recv()

    def finish(self):
        for copy in [*self.across, *self.beside, *self.handed]:
            copy.wait_send()


class Share:
    def __init__(self, buf, sems, line):
        self.buf, self.sems, self.line = buf, sems, line
        member = lax.axis_index("mp")
        self.sib, self.face = near_devices()
        self.copies = [
            send(buf.at[member], buf.at[member], sems, (line, k), peer)
            for k, peer in enumerate((self.face, self.sib))
        ]

    def hand_on(self):
        self.copies[0].wait_recv()
        block = self.buf.at[self.face[1]]
        self.copies.append(send(block, block, self.sems, (self.line, 2), self.sib))

    def arrive(self):
        for copy in self.copies[1:]:
            copy.wait_recv()

    def finish(self):
        for copy in self.copies:
            copy.wait_send()


class RootShare:
    def __init__(self, value, buf, sems, line):
        self.buf, self.sems, self.line = buf, sems, line
        self.member = lax.axis_index("mp")
        self.root, _ = columns_of(lax.axis_index("dp"))
        self.sib, self.face = near_devices()

        @pl.when(self.member == self.root)
        def _():
            buf[...] = value.astype(buf.dtype)
            for k, peer in enumerate((self.face, self.sib)):
                self.copy(k, peer).start()

    def copy(self, k, peer):
        return pltpu.make_async_remote_copy(
            src_ref=self.buf,
            dst_ref=self.buf,
            send_sem=self.sems[0].at[self.line, k],
            recv_sem=self.sems[1].at[self.line, 0],
            device_id=peer,
            device_id_type=MESH,
        )

    def hand_on(self):
        @pl.when(self.member != self.root)
        def _():
            self.copy(0, self.sib).wait_recv()

        @pl.when(self.face[1] == self.root)
        def _():
            self.copy(2, self.sib).start()

    def finish(self):
        @pl.when(self.member == self.root)
        def _():
            for k, peer in enumerate((self.face, self.sib)):
                self.copy(k, peer).wait_send()

        @pl.when(self.face[1] == self.root)
        def _():
            self.copy(2, self.sib).wait_send()


class Total:
    def __init__(self, out, into, sems, line, pieces=PIECES):
        self.out, self.into, self.sems, self.line, self.pieces = out, into, sems, line, pieces
        self.sib, self.face = near_devices()
        self.size = out.shape[1] // pieces
        self.far, self.facing, self.beside = [], [], []

    def give(self, b, i, term, peer):
        piece = pl.ds(i * self.size, self.size)
        self.out[b, piece, :] = term.astype(jnp.bfloat16)
        return send(
            self.out.at[b, piece],
            self.into.at[b, piece],
            self.sems,
            (self.line, b * self.pieces + i),
            peer,
        )

    def came(self, b, i):
        return self.into[b, pl.ds(i * self.size, self.size), :].astype(jnp.float32)

    def part(self, term, i):
        return term[i * self.size : (i + 1) * self.size]

    def give_far(self, i, term):
        self.far.append(self.give(0, i, term, self.sib))

    def give_facing(self, i, term):
        self.far[i].wait_recv()
        self.facing.append(self.give(1, i, term + self.came(0, i), self.face))

    def give_beside(self, i, term):
        self.beside.append(self.give(2, i, term, self.sib))

    def take(self, i, term):
        self.beside[i].wait_recv()
        self.facing[i].wait_recv()
        return term + self.came(2, i) + self.came(1, i)

    def finish(self):
        for copy in [*self.far, *self.facing, *self.beside]:
            copy.wait_send()


def gelu_pair(x):
    t = 1.0 / (1.0 + (0.3275911 * 0.7071067811865476) * jnp.abs(x))
    raised = jnp.exp(-0.5 * x * x)
    series = t * (
        0.254829592
        + t * (-0.284496736 + t * (1.421413741 + t * (-1.453152027 + t * 1.061405429)))
    )
    upper = 0.5 * series * raised
    share = jnp.where(x >= 0, 1.0 - upper, upper)
    return x * share, share + x * raised * 0.3989422804014327


def rows_joined(ref):
    blocks = ref[...]
    return blocks.reshape(blocks.shape[0] * blocks.shape[1], blocks.shape[2])


def around(peers):
    group, member = lax.axis_index("dp"), lax.axis_index("mp")
    depth = lax.axis_size("dp") // 2
    z, x = columns_of(group)
    along = [(((z + k) % depth) * 2 + x, member) for k in range(1, depth)]
    return [*peers, *along, (group + 1 - 2 * x, member)]


def layers_kernel(*refs):
    refs = iter(refs)
    take = lambda count: [next(refs) for _ in range(count)]
    hidden, cotangent, scale = take(3)
    norms = take(2)
    qkv_zero, out_zero, out_one = take(3)
    mine = take(5)
    encoded, gradient_out = take(2)
    norm_grads = take(2)
    qkv_pair, out_pair = take(2)
    in_sums, back_sums = take(2), take(2)
    qkv_shared, out_shared = take(2)
    in_zero, back_zero, qkv_one, in_one, back_one = whole = take(5)
    saved = [take(11), take(11)]
    mixed_t, held, out, into = take(4)
    feeds, inner, lows, mixed_grad, key_grad, value_grad, query_grad, head_grads = take(8)
    in_g, back_g, qkv_g, out_g = take(4)
    in_near, in_come, back_near, back_come = take(2), take(1), take(2), take(1)
    qkv_parts, out_parts = take(2), take(2)
    gather_sems, total_sems, spread_sem = take(2), take(2), take(2)
    in_sems, back_sems, qkv_sems, out_sems = take(2), take(2), take(2), take(2)
    share_sems = take(2)
    weights = [(qkv_zero, out_zero, in_zero, back_zero), (qkv_one, out_one, in_one, back_one)]
    greet(around(near_devices()))
    rows = hidden.shape[0]
    size = rows // PIECES
    share = mixed_t.shape[0]
    per_device = share // HD
    pieces = range(PIECES)

    def block(b):
        return pl.ds(b * rows, rows)

    def piece(b, i):
        return pl.ds(b * rows + i * size, size)

    def spread_of(part):
        return Spread(mine[part], whole[part], spread_sem, part)

    def send_tokens(layer, i, value):
        saved[layer][4][piece(0, i), :] = value.astype(jnp.bfloat16)
        gathers[layer].start(i)

    gathers = [Gather(saved[layer][4], gather_sems, layer) for layer in range(2)]
    for i in pieces:
        send_tokens(0, i, hidden[piece(0, i), :])
    spreads = [spread_of(part) for part in range(5)]
    held[...] = hidden[...]

    def forward(layer, after_projection, after_far, after_attention, before_feed, after_feed, close):
        second_normal, second_inverse, first_normal, first_inverse = saved[layer][:4]
        tokens, heads, mixed, logs, firsts, active, slope = saved[layer][4:]
        qkv_w, out_w, in_w, back_w = weights[layer]
        gather, norm = gathers[layer], norms[layer]

        def project(place):
            parts = nn(tokens[place, :], rows_joined(qkv_w))
            for j in range(3 * per_device):
                part = parts[:, j * HD : (j + 1) * HD]
                if j < per_device:
                    part = part * HD ** (-0.5)
                heads[j, place, :] = part.astype(jnp.bfloat16)

        project(block(0))
        gather.wait_beside()
        project(block(1))
        for i in pieces:
            gather.hand_on(i)
            project(piece(2, i))
        for i in pieces:
            gather.wait_handed(i)
        project(block(3))
        gather.finish()
        after_projection()

        def attend(b):
            def one_head(h, carry):
                scores = nt(heads[per_device + h], heads[h, block(b), :])
                peak = jnp.max(scores, axis=0, keepdims=True)
                raised = jnp.exp(scores - peak)
                total = jnp.sum(raised, axis=0, keepdims=True)
                result = tn(heads[2 * per_device + h], raised.astype(jnp.bfloat16)) / total
                mixed_t[pl.ds(pl.multiple_of(h * HD, HD), HD), :] = result
                logs[b * per_device + h] = peak + jnp.log(total)
                return carry

            lax.fori_loop(0, per_device, one_head, 0)
            rows_mixed = mixed_t[...].T.astype(jnp.bfloat16)
            mixed[block(b), :] = rows_mixed
            return nn(rows_mixed, rows_joined(out_w))

        total = Total(out, into, total_sems, layer)
        term = attend(3)
        for i in pieces:
            total.give_far(i, total.part(term, i))
        term = attend(2)
        for i in pieces:
            total.give_facing(i, total.part(term, i))
        after_far()
        term = attend(1)
        for i in pieces:
            total.give_beside(i, total.part(term, i))
        held[...] += attend(0)
        after_attention()
        gather_two = Gather(firsts, gather_sems, 2 + layer)
        for i in pieces:
            place = piece(0, i)
            first, normal, inverse = norm_forward(
                total.take(i, held[place, :]), norm[0:1, :], norm[1:2, :]
            )
            firsts[place, :] = first.astype(jnp.bfloat16)
            gather_two.start(i)
            first_normal[place, :] = normal
            first_inverse[place, :] = inverse
            held[place, :] = first
        total.finish()
        before_feed()

        def feed(place):
            value, gradient = gelu_pair(nn(firsts[place, :], rows_joined(in_w)))
            value = value.astype(jnp.bfloat16)
            active[place, :] = value
            slope[place, :] = gradient.astype(jnp.bfloat16)
            return nt(value, rows_joined(back_w))

        total = Total(out, into, total_sems, 2 + layer)
        held[...] += feed(block(0))
        gather_two.wait_beside()
        term = feed(block(1))
        for i in pieces:
            total.give_beside(i, total.part(term, i))
        for i in pieces:
            gather_two.hand_on(i)
            term = feed(piece(2, i))
            gather_two.wait_handed(i)
            total.give_far(i, feed(piece(3, i)))
            total.give_facing(i, term)
        after_feed()
        for i in pieces:
            place = piece(0, i)
            result, normal, inverse = norm_forward(
                total.take(i, held[place, :]), norm[2:3, :], norm[3:4, :]
            )
            second_normal[place, :] = normal
            second_inverse[place, :] = inverse
            close(i, result)
        gather_two.finish()
        total.finish()

    def note(layer, row, i, gain, bias):
        target = norm_grads[layer]
        if i:
            gain, bias = gain + target[row, :], bias + target[row + 1, :]
        target[row : row + 1, :] = gain[None]
        target[row + 1 : row + 2, :] = bias[None]

    feed_gathers = [Gather(feeds, gather_sems, 4 + layer) for layer in range(2)]

    def send_feed_grad(layer, i, gradient):
        place = piece(0, i)
        grad_second, gain, bias = norm_backward(
            gradient, saved[layer][0][place, :], saved[layer][1][place, :], norms[layer][2:3, :]
        )
        feeds[place, :] = grad_second.astype(jnp.bfloat16)
        feed_gathers[layer].start(i)
        note(layer, 2, i, gain, bias)
        held[place, :] = grad_second

    def backward(layer, before_in, after_back, after_score, close_in, close):
        _, _, first_normal, first_inverse = saved[layer][:4]
        tokens, heads, mixed, logs, firsts, active, slope = saved[layer][4:]
        qkv_w, out_w, in_w, back_w = weights[layer]
        gather = feed_gathers[layer]

        def feed(place):
            part = nn(feeds[place, :], rows_joined(back_w)) * slope[place, :].astype(jnp.float32)
            part = part.astype(jnp.bfloat16)
            inner[place, :] = part
            return nt(part, rows_joined(in_w))

        total = Total(out, into, total_sems, 4 + layer)
        held[...] += feed(block(0))
        gather.wait_beside()
        term = feed(block(1))
        for i in pieces:
            total.give_beside(i, total.part(term, i))
        for i in pieces:
            gather.hand_on(i)
            term = feed(piece(2, i))
            gather.wait_handed(i)
            total.give_far(i, feed(piece(3, i)))
            total.give_facing(i, term)
        gather.finish()
        before_in()
        in_g[...] = tn(firsts[...], inner[...]).astype(jnp.bfloat16).reshape(in_g.shape)
        in_reduce = Reduce(in_g, in_near[layer], in_come[0], in_sems, layer)
        gather_two = Gather(lows, gather_sems, 6 + layer)
        for i in pieces:
            place = piece(0, i)
            grad_first, gain, bias = norm_backward(
                total.take(i, held[place, :]),
                first_normal[place, :],
                first_inverse[place, :],
                norms[layer][0:1, :],
            )
            lows[place, :] = grad_first.astype(jnp.bfloat16)
            gather_two.start(i)
            note(layer, 0, i, gain, bias)
            held[place, :] = grad_first
        total.finish()
        back_g[...] = tn(feeds[...], active[...]).astype(jnp.bfloat16).reshape(back_g.shape)
        back_reduce = Reduce(back_g, back_near[layer], back_come[0], back_sems, layer)
        after_back()

        def spread(place):
            parts = nt(lows[place, :], rows_joined(out_w))
            for j in range(per_device):
                mixed_grad[j, place, :] = parts[:, j * HD : (j + 1) * HD].astype(jnp.bfloat16)

        def score(b):
            def one_head(h, carry):
                query, key = heads[h, block(b), :], heads[per_device + h]
                upper = mixed_grad[h, block(b), :]
                prob = jnp.exp(nt(key, query) - logs[b * per_device + h])
                product = nt(heads[2 * per_device + h], upper)
                center = jnp.sum(prob * product, axis=0, keepdims=True)
                score_grad = (prob * (product - center)).astype(jnp.bfloat16)
                key_term = nn(score_grad, query)
                value_term = nn(prob.astype(jnp.bfloat16), upper)
                if b:
                    key_term, value_term = key_term + key_grad[h], value_term + value_grad[h]
                key_grad[h] = key_term
                value_grad[h] = value_term
                turned = tn(key, score_grad) * HD ** (-0.5)
                query_grad[h, block(b), :] = turned.T.astype(jnp.bfloat16)
                return carry

            lax.fori_loop(0, per_device, one_head, 0)

        spread(block(0))
        score(0)
        for i in pieces:
            gather_two.hand_on(i)
        gather_two.wait_beside()
        spread(block(1))
        score(1)
        after_score()
        in_reduce.middle()
        spread(block(2))
        score(2)
        for i in pieces:
            gather_two.wait_handed(i)
        spread(block(3))
        score(3)
        gather_two.finish()
        back_reduce.middle()
        for h in range(per_device):
            for c, grad in enumerate((query_grad, key_grad, value_grad)):
                start = c * share + h * HD
                head_grads[:, start : start + HD] = grad[h].astype(jnp.bfloat16)

        total = Total(out, into, total_sems, 6 + layer)
        weight = rows_joined(qkv_w)
        term = nt(head_grads[block(3), :], weight)
        for i in pieces:
            total.give_far(i, total.part(term, i))
        term = nt(head_grads[block(2), :], weight)
        for i in pieces:
            total.give_facing(i, total.part(term, i))
        term = nt(head_grads[block(1), :], weight)
        for i in pieces:
            total.give_beside(i, total.part(term, i))
        held[...] += nt(head_grads[block(0), :], weight)
        qkv_g[...] = tn(tokens[...], head_grads[...]).astype(jnp.bfloat16).reshape(qkv_g.shape)
        out_g[...] = tn(mixed[...], lows[...]).astype(jnp.bfloat16).reshape(out_g.shape)
        close_in()
        for i in pieces:
            close(i, total.take(i, held[piece(0, i), :]))
        total.finish()
        return in_reduce, back_reduce

    def between(i, result):
        held[piece(0, i), :] = result
        send_tokens(1, i, result)

    def before_feed_zero():
        spreads[0].arrive()
        spreads[1].arrive()

    def after_attention_zero():
        spreads[1].hand_on()

    forward(
        0,
        spreads[0].hand_on,
        lambda: None,
        after_attention_zero,
        before_feed_zero,
        spreads[2].hand_on,
        between,
    )
    spreads[2].arrive()

    def turn(i, result):
        encoded[piece(0, i), :] = result
        send_feed_grad(1, i, cotangent[piece(0, i), :] * scale[...])

    def before_feed_one():
        spreads[3].arrive()
        spreads[4].arrive()

    forward(
        1,
        spreads[3].hand_on,
        spreads[4].hand_on,
        lambda: None,
        before_feed_one,
        lambda: None,
        turn,
    )
    for spread in spreads:
        spread.finish()

    reduces, shares = [], []
    none = lambda: None

    def start_prior():
        reduces.append(Reduce(qkv_g, *qkv_parts, qkv_sems, 0))
        reduces.append(MixReduce(out_g, *out_parts, out_sems, 0))

    in_reduce, back_reduce = backward(
        1,
        none,
        none,
        none,
        start_prior,
        lambda i, value: send_feed_grad(0, i, value),
    )
    in_sums[1][...] = in_reduce.finish()
    back_sums[1][...] = back_reduce.finish()

    def prior_middle():
        for reduce in reduces:
            reduce.middle()

    def prior_finish():
        qkv_shared[lax.axis_index("mp")] = reduces[0].finish().astype(qkv_shared.dtype)
        shares.append(Share(qkv_shared, share_sems, 0))
        shares.append(RootShare(reduces[1].finish(), out_shared, share_sems, 1))

    def start_pair():
        for share in shares:
            share.hand_on()
        reduces.append(Reduce(qkv_g, qkv_pair, None, qkv_sems, 1))
        reduces.append(MixReduce(out_g, out_pair, None, out_sems, 1))

    def last(i, value):
        gradient_out[piece(0, i), :] = value

    in_reduce, back_reduce = backward(0, prior_middle, none, prior_finish, start_pair, last)
    in_sums[0][...] = in_reduce.finish()
    back_sums[0][...] = back_reduce.finish()
    shares[0].arrive()
    for share in shares:
        share.finish()
    for reduce in reduces[2:]:
        reduce.add_up()


def halves():
    depth = lax.axis_size("dp") // 2
    steps = [*range(1, depth), 0]
    return [[(k, (k + 1 + half) % 2) for k in steps] for half in range(2)]


def group_at(step, back=False):
    group = lax.axis_index("dp")
    depth = lax.axis_size("dp") // 2
    z, x = columns_of(group)
    along = depth - step[0] if back else step[0]
    return ((z + along) % depth) * 2 + (x + step[1]) % 2


def start_kernel(*refs):
    refs = iter(refs)
    take = lambda count: [next(refs) for _ in range(count)]
    sent_ids, codes, levels, tables, small = take(5)
    mine, out_mine = take(1), take(2)
    hidden, asked, scale = take(3)
    norms = take(2)
    whole, out_whole = take(1), take(2)
    small_all, found, returned, out_a, into_a, table_rows, stream = take(7)
    total_a, small_sems, spread_sem, out_sems, id_sems, near_sems, row_sems = [take(2) for _ in range(7)]
    (stream_sems,) = take(1)
    group, member = lax.axis_index("dp"), lax.axis_index("mp")
    groups, members = lax.axis_size("dp"), lax.axis_size("mp")
    depth = groups // 2
    z, x = columns_of(group)
    beside = (group + 1 - 2 * x, member)
    peers = group_peers()
    sib, face = near_devices()
    far = (group, (sib[1] + 2) % members)
    own_rows = table_rows.shape[0]
    part = own_rows // 3
    streams = [
        pltpu.make_async_copy(
            tables.at[:, pl.ds(n * part, part)], stream.at[n % 2], stream_sems.at[n % 2]
        )
        for n in range(3)
    ]
    streams[0].start()
    streams[1].start()

    def add_tables(n):
        streams[n].wait()
        total = stream[n % 2, 0]
        for t in range(1, stream.shape[1]):
            total = total + stream[n % 2, t]
        table_rows[n * part : (n + 1) * part, :] = total.astype(table_rows.dtype)

    greet([*peers, *mates()])

    id_copies = [
        send(sent_ids.at[peer[0]], asked.at[0, group], id_sems, k, peer)
        for k, peer in enumerate(peers)
    ]
    asked[0, group] = sent_ids[group]
    small_spread = Spread(small, small_all, small_sems, 0)
    add_tables(0)
    streams[2].start()
    for copy in id_copies:
        copy.wait_recv()
    near_copies = [
        send(asked.at[0], asked.at[k + 1], near_sems, k, peer)
        for k, peer in enumerate((sib, face, far))
    ]
    spreads = [Spread(a, b, spread_sem, p) for p, (a, b) in enumerate(zip(mine, whole))]

    def root_copies():
        return [
            pltpu.make_async_remote_copy(
                src_ref=mine_out,
                dst_ref=target.at[x],
                send_sem=out_sems[0].at[p, k],
                recv_sem=out_sems[1].at[p, 0],
                device_id=(((z + k) % depth) * 2 + x, member),
                device_id_type=MESH,
            )
            for p, (mine_out, target) in enumerate(zip(out_mine, out_whole))
            for k in range(1, depth)
        ]

    @pl.when(z == member)
    def _():
        for copy in root_copies():
            copy.start()
        for mine_out, target in zip(out_mine, out_whole):
            target[x] = mine_out[...]

    add_tables(1)
    add_tables(2)
    for copy in near_copies:
        copy.wait_recv()
    first_row = ((group * members + member) * own_rows).astype(jnp.float32)
    capacity = asked.shape[3]
    half_slots = depth * capacity

    def lookup(r, half):
        line = jnp.concatenate([asked[r, group_at(step)] for step in halves()[half]], axis=1)
        line = line.astype(jnp.float32) - first_row
        line = jnp.broadcast_to(line, (8, half_slots)).T[:, 0:1]
        place = lax.broadcasted_iota(jnp.int32, (half_slots, own_rows), 1)
        hot = (line == place.astype(jnp.float32)).astype(jnp.bfloat16)
        return nn(hot, table_rows[...])

    total = Total(out_a, into_a, total_a, 0, 2)
    for half in range(2):
        total.give_far(half, lookup(3, half))
        total.give_facing(half, lookup(2, half))
    for half in range(2):
        total.give_beside(half, lookup(1, half))
    own = [lookup(0, half) for half in range(2)]
    small_spread.hand_on()

    @pl.when(z != member)
    def _():
        for p in range(2):
            pltpu.make_async_remote_copy(
                src_ref=out_mine[p],
                dst_ref=out_whole[p].at[x],
                send_sem=out_sems[0].at[p, 0],
                recv_sem=out_sems[1].at[p, 0],
                device_id=beside,
                device_id_type=MESH,
            ).wait_recv()

    out_copies = [
        pltpu.make_async_remote_copy(
            src_ref=target.at[x],
            dst_ref=target.at[x],
            send_sem=out_sems[0].at[p, depth],
            recv_sem=out_sems[1].at[p, 1],
            device_id=beside,
            device_id_type=MESH,
        )
        for p, target in enumerate(out_whole)
    ]
    for copy in out_copies:
        copy.start()
    row_copies = []
    for half, steps in enumerate(halves()):
        rows_found = total.take(half, own[half]).astype(jnp.bfloat16)
        found[half * depth : (half + 1) * depth] = rows_found.reshape(depth, capacity, -1)
        for n, step in enumerate(steps):
            slot = half * depth + n
            if step == (0, 0):
                returned[group] = found[slot]
            else:
                row_copies.append(
                    send(
                        found.at[slot],
                        returned.at[group],
                        row_sems,
                        slot,
                        (group_at(step), member),
                    )
                )
        if half == 0:
            spreads[0].hand_on()
    small_spread.arrive()
    for layer, target in enumerate(norms):
        half = target.shape[1] // 2
        for c in range(groups):
            start = (c % 2) * half
            target[c // 2 : c // 2 + 1, start : start + half] = small_all[
                c, 8:9, layer * half : (layer + 1) * half
            ]
    counts = small_all[0, 9:10, :]
    for c in range(1, groups):
        counts = counts + small_all[c, 9:10, :]
    same = jnp.sum(counts * small[9:10, :], axis=1, keepdims=True)
    scale[...] = groups / (STUDY_TOTAL * same)
    level_rows = 8 * groups
    level_full = jnp.concatenate([small_all[c, 0:8, :] for c in range(groups)], axis=0)
    rows = hidden.shape[0]
    level_place = lax.broadcasted_iota(jnp.int32, (rows, level_rows), 1)
    level_hot = (levels[...] == level_place).astype(jnp.bfloat16)
    level_part = nn(level_hot, level_full.astype(jnp.bfloat16))
    slot_place = lax.broadcasted_iota(jnp.int32, (rows, groups * capacity), 1)
    slot_hot = (codes[...] == slot_place).astype(jnp.bfloat16)
    for copy in row_copies:
        copy.wait_recv()
    hidden[...] = nn(slot_hot, rows_joined(returned)) + level_part

    for copy in [*id_copies, *near_copies, *row_copies]:
        copy.wait_send()
    total.finish()
    for spread in spreads:
        spread.arrive()
    for spread in (small_spread, *spreads):
        spread.finish()
    for copy in out_copies:
        copy.wait()

    @pl.when(z == member)
    def _():
        for copy in root_copies():
            copy.wait_send()


def end_kernel(*refs):
    refs = iter(refs)
    take = lambda count: [next(refs) for _ in range(count)]
    gradient, codes, levels, asked, qkv_pair, out_pair = take(6)
    norm_zero, norm_one = take(2)
    row_grad, hits, qkv_shared, out_shared, small_sum = take(5)
    slots, arrived, small_g, small_in = take(4)
    qkv_come, small_near, small_come, mix_come = take(4)
    mix_sems, qkv_sems, small_sems, gather_sems, row_sems, mate_sems = [take(2) for _ in range(6)]
    group, member = lax.axis_index("dp"), lax.axis_index("mp")
    groups, members = lax.axis_size("dp"), lax.axis_size("mp")
    depth = groups // 2
    z, x = columns_of(group)
    peers, near = group_peers(), mates()
    greet([*peers, *near])
    rows, width = gradient.shape
    capacity = slots.shape[1]
    count = groups * capacity
    half_count = depth * capacity

    slot_place = lax.broadcasted_iota(jnp.int32, (rows, count), 1)
    slot_hot = (codes[...] == slot_place).astype(jnp.bfloat16)
    high = gradient[...].astype(jnp.bfloat16)
    slots[...] = tn(slot_hot, high).astype(jnp.bfloat16).reshape(slots.shape)
    row_copies = []
    for half, steps in enumerate(halves()):
        copies = []
        for n, step in enumerate(steps):
            slot = half * depth + n
            target = arrived.at[pl.ds(slot * capacity, capacity)]
            if step == (0, 0):
                arrived[slot * capacity : (slot + 1) * capacity, :] = slots[group]
            else:
                there = group_at(step)
                copies.append(send(slots.at[there], target, row_sems, slot, (there, member)))
        row_copies.append(copies)
    qkv_reduce = Reduce(None, qkv_pair, qkv_come, qkv_sems, 0)
    qkv_reduce.middle()
    mix = MixReduce(None, out_pair, mix_come, mix_sems, 0)
    mix.middle()

    level_place = lax.broadcasted_iota(jnp.int32, (rows, 8 * groups), 1)
    level_hot = (levels[...] == level_place).astype(jnp.bfloat16)
    rest = (gradient[...] - high.astype(jnp.float32)).astype(jnp.bfloat16)
    level_grad = tn(level_hot, high) + tn(level_hot, rest)
    half_width = width // 2
    for c in range(groups):
        small_g[c // 2, c % 2, 0:8, :] = level_grad[c * 8 : (c + 1) * 8, :]
        start = (c % 2) * half_width
        for layer, source in enumerate((norm_zero, norm_one)):
            small_g[c // 2, c % 2, 8:9, layer * half_width : (layer + 1) * half_width] = source[
                c // 2 : c // 2 + 1, start : start + half_width
            ]
        small_g[c // 2, c % 2, 9:16, :] = jnp.zeros((7, width), jnp.float32)
    small_reduce = Reduce(small_g, small_near, small_come, small_sems, 0)

    gather = Gather(arrived, gather_sems, 0, 2)
    for half in range(2):
        for copy in row_copies[half]:
            copy.wait_recv()
        gather.start(half)
        if half == 0:
            small_reduce.middle()

    own_rows = row_grad.shape[0]
    first_row = (group * members + member) * own_rows

    def collect(blocks, which):
        line = jnp.concatenate(
            [
                asked[r, group_at(step, back=True)]
                for r in blocks
                for half in which
                for step in halves()[half]
            ],
            axis=1,
        )
        line = line - first_row
        slots_here = line.shape[1]
        place = lax.broadcasted_iota(jnp.int32, (own_rows, slots_here), 0)
        hot = (line == place).astype(jnp.float32)
        source = jnp.concatenate(
            [
                arrived[pl.ds(r * count + half * half_count, half_count), :]
                for r in blocks
                for half in which
            ],
            axis=0,
        )
        part = nn(hot.astype(jnp.bfloat16), source)
        found = jnp.sum(hot, axis=1, keepdims=True)
        if blocks[0]:
            row_grad[...] += part
            hits[...] += found
        else:
            row_grad[...] = part
            hits[...] = found

    gather.wait_beside()
    collect([0, 1], [0, 1])
    gather.hand_on(0)

    small_in[member] = small_reduce.finish()
    small_share = Share(small_in, mate_sems, 0)
    out_share = RootShare(mix.finish(), out_shared, mate_sems, 1)
    qkv_shared[member] = qkv_reduce.finish().astype(qkv_shared.dtype)
    qkv_share = Share(qkv_shared, mate_sems, 2)
    gather.hand_on(1)
    small_share.hand_on()
    out_share.hand_on()
    gather.wait_handed(0)
    collect([2, 3], [0])
    gather.wait_handed(1)
    collect([2, 3], [1])

    qkv_share.hand_on()
    small_share.arrive()
    total = small_in[0]
    for m in range(1, members):
        total = total + small_in[m]
    small_sum[...] = total
    qkv_share.arrive()
    for copy in sum(row_copies, []):
        copy.wait_send()
    for each in (gather, small_share, out_share, qkv_share):
        each.finish()


def run_kernel(kernel, collective_id, name, inputs, outputs, scratch, flops=0, exps=0, left=()):
    moved = sum(math.prod(a.shape) * a.dtype.itemsize for a in inputs)
    return pl.pallas_call(
        kernel,
        out_shape=[jax.ShapeDtypeStruct(*o) for o in outputs],
        in_specs=[
            pl.BlockSpec(memory_space=pl.ANY if n in left else pltpu.VMEM)
            for n in range(len(inputs))
        ],
        out_specs=[pl.BlockSpec(memory_space=pltpu.VMEM)] * len(outputs),
        scratch_shapes=scratch,
        compiler_params=pltpu.CompilerParams(
            collective_id=collective_id, has_side_effects=True, vmem_limit_bytes=60 * 2**20
        ),
        cost_estimate=pl.CostEstimate(flops=flops, bytes_accessed=moved, transcendentals=exps),
        name=name,
    )(*inputs)


def run_layers(hidden, cotangent, scale, norms, qkv_zero, out_w, mine):
    rows, width = hidden.shape
    cell = 4 * rows
    groups, part, columns = qkv_zero.shape
    depth = groups // 2
    share = columns // 3
    per_device = share // HD
    units = mine[0].shape[1]
    f32, low = jnp.float32, jnp.bfloat16
    outputs = [
        ((rows, width), f32),
        ((rows, width), f32),
        ((4, width), f32),
        ((4, width), f32),
        ((depth, part, columns), low),
        ((part, width), low),
        ((part, units), f32),
        ((part, units), f32),
        ((part, units), f32),
        ((part, units), f32),
        ((4, part, columns), low),
        ((part, width), low),
    ]
    kept = [
        pltpu.VMEM((rows, width), f32),
        pltpu.VMEM((rows, 1), f32),
        pltpu.VMEM((rows, width), f32),
        pltpu.VMEM((rows, 1), f32),
        pltpu.VMEM((cell, width), low),
        pltpu.VMEM((3 * per_device, cell, HD), low),
        pltpu.VMEM((cell, share), low),
        pltpu.VMEM((4 * per_device, 1, rows), f32),
        pltpu.VMEM((cell, width), low),
        pltpu.VMEM((cell, units), low),
        pltpu.VMEM((cell, units), low),
    ]
    scratch = [pltpu.VMEM((groups, *piece.shape), low) for piece in mine] + kept * 2
    scratch += [
        pltpu.VMEM((share, rows), f32),
        pltpu.VMEM((rows, width), f32),
        pltpu.VMEM((3, rows, width), low),
        pltpu.VMEM((3, rows, width), low),
        pltpu.VMEM((cell, width), low),
        pltpu.VMEM((cell, units), low),
        pltpu.VMEM((cell, width), low),
        pltpu.VMEM((per_device, cell, HD), low),
        pltpu.VMEM((per_device, cell, HD), f32),
        pltpu.VMEM((per_device, cell, HD), f32),
        pltpu.VMEM((per_device, cell, HD), low),
        pltpu.VMEM((cell, columns), low),
        pltpu.VMEM((depth, 2, part, units), low),
        pltpu.VMEM((depth, 2, part, units), low),
        pltpu.VMEM((depth, 2, part, columns), low),
        pltpu.VMEM((2, part, width), low),
    ]
    near, come = reduce_scratch(part, units, low)
    scratch += [near, near, come] * 2 + reduce_scratch(part, columns, low)
    scratch += [pltpu.VMEM((part, width), low), pltpu.VMEM((depth - 1, part, width), low)]
    scratch += dma_sems(8, 3 * PIECES) + dma_sems(8, 3 * PIECES) + dma_sems(5, 2 * depth - 1)
    scratch += dma_sems(2, depth) * 4 + dma_sems(2, 3)
    flops = 12 * cell * width * (4 * share + 2 * units) + 28 * cell * cell * share
    return run_kernel(
        layers_kernel,
        1,
        "layers",
        [hidden, cotangent, scale, *norms, qkv_zero, *out_w, *mine],
        outputs,
        scratch,
        flops,
        4 * cell * cell * per_device,
    )


def updated(weight, first, second, grad, rate, decay):
    first = beta_one * first + (1.0 - beta_one) * grad
    second = beta_two * second + (1.0 - beta_two) * grad * grad
    first_hat = first * (1.0 / (1.0 - beta_one**STEP))
    second_hat = second * (1.0 / (1.0 - beta_two**STEP))
    new = weight - rate * (first_hat / (jnp.sqrt(second_hat) + adam_eps) + decay * weight)
    return new, first, second


def update_kernel(*refs):
    refs = iter(refs)
    take = lambda count: [next(refs) for _ in range(count)]
    weight, moments, row_grad, hits = take(4)
    qkv_grads, out_grads, in_grads, back_grads = take(2), take(2), take(2), take(2)
    small_grad, level, level_moments, norm, norm_moments = take(5)
    given = take(8)
    new_weight, new_moments = take(2)
    new_level, new_level_moments, new_norm, new_norm_moments = take(4)
    made = take(8)
    held = take(8)
    load_sems, store_sems = take(2)
    step = pl.program_id(0) * pl.num_programs(1) + pl.program_id(1)
    last = pl.num_programs(0) * pl.num_programs(1) - 1
    layers = norm.shape[0]
    loads = [pltpu.make_async_copy(a, b, load_sems.at[n]) for n, (a, b) in enumerate(zip(given, held))]
    stores = [pltpu.make_async_copy(b, a, store_sems.at[n]) for n, (a, b) in enumerate(zip(made, held))]

    @pl.when(step == 0)
    def _():
        for load in loads:
            load.start()
        level_rows = level.shape[0]
        result = updated(
            level[...],
            level_moments[0],
            level_moments[1],
            small_grad[0:level_rows, :],
            rate_table,
            decay_rate,
        )
        new_level[...], new_level_moments[0], new_level_moments[1] = result
        columns = norm.shape[1]
        for n in range(layers):
            line = slice(n, n + 1)
            result = updated(
                norm[line, :],
                norm_moments[0, line, :],
                norm_moments[1, line, :],
                small_grad[level_rows : level_rows + 1, n * columns : (n + 1) * columns],
                rate_norm,
                0.0,
            )
            new_norm[line, :], new_norm_moments[0, line, :], new_norm_moments[1, line, :] = result

    def dense(which, place, grad, rate):
        value, kept = held[2 * which], held[2 * which + 1]
        result = updated(value[place], kept[(0, *place)], kept[(1, *place)], grad, rate, decay_rate)
        value[place], kept[(0, *place)], kept[(1, *place)] = result

    def qkv(n):
        members, _, columns = qkv_grads[n].shape
        share = columns // 3
        for c in range(3):
            grad = jnp.concatenate(
                [qkv_grads[n][m, :, c * share : (c + 1) * share] for m in range(members)], axis=1
            )
            dense(0, (n, c), grad.astype(jnp.float32), rate_dense)

    def plain(which, grads, rate):
        for n in range(layers):
            dense(which, (n,), grads[n][...].astype(jnp.float32), rate)

    jobs = [
        (2, 0, lambda: [qkv(n) for n in range(layers)]),
        (4, 1, lambda: plain(1, out_grads, rate_mixing)),
        (5, 2, lambda: plain(2, in_grads, rate_dense)),
        (6, 3, lambda: plain(3, back_grads, rate_dense)),
    ]
    for when, which, job in jobs:

        @pl.when(step == when)
        def _():
            for n in (2 * which, 2 * which + 1):
                loads[n].wait()
            job()
            for n in (2 * which, 2 * which + 1):
                stores[n].start()

    touched = hits[...] > 0
    old, old_first, old_second = weight[0], moments[0, 0], moments[1, 0]
    new, first, second = updated(old, old_first, old_second, row_grad[...], rate_table, decay_rate)
    new_weight[0] = jnp.where(touched, new, old)
    new_moments[0, 0] = jnp.where(touched, first, old_first)
    new_moments[1, 0] = jnp.where(touched, second, old_second)

    @pl.when(step == last)
    def _():
        for store in stores:
            store.wait()


def update_all(tables, table_moments, row_grad, hits, grads, small, small_state, state):
    count, own_rows, width = tables.shape
    step = own_rows // 3
    table_block = pl.BlockSpec((1, step, width), lambda i, t: (t, i, 0))
    moment_block = pl.BlockSpec((2, 1, step, width), lambda i, t: (0, t, i, 0))

    def whole(array):
        zeros = (0,) * array.ndim
        return pl.BlockSpec(array.shape, lambda i, t: zeros, pipeline_mode=pl.Buffered(1))

    left = pl.BlockSpec(memory_space=pl.ANY)
    kept = [*grads, small, *small_state]
    shape_of = lambda array: jax.ShapeDtypeStruct(array.shape, array.dtype)
    return pl.pallas_call(
        update_kernel,
        grid=(own_rows // step, count),
        in_specs=[
            table_block,
            moment_block,
            pl.BlockSpec((step, width), lambda i, t: (i, 0)),
            pl.BlockSpec((step, 1), lambda i, t: (i, 0)),
            *[whole(array) for array in kept],
            *[left] * len(state),
        ],
        out_specs=[
            table_block,
            moment_block,
            *[whole(array) for array in small_state],
            *[left] * len(state),
        ],
        out_shape=[shape_of(a) for a in (tables, table_moments, *small_state, *state)],
        scratch_shapes=[pltpu.VMEM(a.shape, a.dtype) for a in state]
        + [pltpu.SemaphoreType.DMA((len(state),))] * 2,
        compiler_params=pltpu.CompilerParams(vmem_limit_bytes=56 * 2**20),
        cost_estimate=pl.CostEstimate(
            flops=20 * tables.size, bytes_accessed=28 * tables.size, transcendentals=tables.size
        ),
        name="update",
    )(tables, table_moments, row_grad, hits, *kept, *state)


def fast_body(
    gene_ids,
    levels,
    study_of_cell,
    cotangent,
    tables,
    table_moments,
    level_table,
    level_moments,
    qkv_weight,
    qkv_moments,
    out_weight,
    out_moments,
    in_weight,
    in_moments,
    back_weight,
    back_moments,
    norm_params,
    norm_moments,
):
    low = jnp.bfloat16
    groups = lax.axis_size("dp")
    members = lax.axis_size("mp")
    member = lax.axis_index("mp")
    rows_here, width = cotangent.shape
    layers = qkv_weight.shape[0]
    local_cells = study_of_cell.shape[0]
    capacity = 2 * rows_here // groups
    own_rows = tables.shape[1]
    block_size = own_rows * members
    depth = qkv_weight.shape[2]
    share = width // members
    units = in_weight.shape[2]

    assert groups == 2 * members and layers == 2 and local_cells == 1
    f32 = jnp.float32
    qkv_mine = lax.dynamic_slice_in_dim(qkv_weight, member * share, share, axis=3).astype(low)
    qkv_mine = qkv_mine.transpose(0, 2, 1, 3).reshape(layers, depth, 3 * share)
    out_mine = out_weight.astype(low)
    in_mine = in_weight.astype(low)
    back_mine = back_weight.astype(low).transpose(0, 2, 1)
    level_rows = level_table.shape[0]
    study_onehot = (study_of_cell[:, None] == jnp.arange(width)[None, :]).astype(f32)
    small = jnp.concatenate(
        [
            level_table.astype(low).astype(f32),
            norm_params.reshape(1, width),
            study_onehot,
            jnp.zeros((16 - level_rows - 2, width), f32),
        ]
    )
    row_owner = gene_ids // block_size
    slot_index = slots_of(row_owner)
    sent_ids = slotted_ids(gene_ids, row_owner, slot_index, groups, capacity)
    codes = (row_owner * capacity + slot_index)[:, None]
    level_column = levels[:, None]

    slots = groups * capacity
    copies = 2 * (groups // 2) - 1
    dma = pltpu.SemaphoreType.DMA
    hidden, asked, scale, *more = run_kernel(
        start_kernel,
        5,
        "start",
        [
            sent_ids[:, None, :],
            codes,
            level_column,
            tables,
            small,
            qkv_mine[0],
            out_mine[0],
            out_mine[1],
        ],
        [
            ((rows_here, width), f32),
            ((members, groups, 1, capacity), jnp.int32),
            ((1, 1), f32),
            ((4, width), f32),
            ((4, width), f32),
            ((groups, depth, 3 * share), low),
            ((2, depth, width), low),
            ((2, depth, width), low),
        ],
        [
            pltpu.VMEM((groups, 16, width), f32),
            pltpu.VMEM((groups, capacity, width), low),
            pltpu.VMEM((groups, capacity, width), low),
            pltpu.VMEM((3, slots, width), low),
            pltpu.VMEM((3, slots, width), low),
            pltpu.VMEM((own_rows, width), low),
            pltpu.VMEM((2, tables.shape[0], own_rows // 3, width), f32),
        ]
        + dma_sems(1, 3 * 2)
        + [dma((1, copies))] * 2
        + [dma((1, copies))] * 2
        + [dma((2, groups // 2 + 1))] * 2
        + [dma((groups - 1,))] * 2
        + [dma((3,))] * 2
        + [dma((groups,))] * 2
        + [dma((2,))],
        left=(3,),
    )
    norms, qkv_w, out_w = more[0:2], more[2], more[3:5]
    hidden, gradient, norm_zero, norm_one, qkv_pair, out_pair, *more = run_layers(
        hidden,
        cotangent,
        scale,
        norms,
        qkv_w,
        out_w,
        [in_mine[0], back_mine[0], qkv_mine[1], in_mine[1], back_mine[1]],
    )
    in_zero, in_one, back_zero, back_one, qkv_one, out_one = more
    row_grad, hits, qkv_zero, out_zero, small_sum = run_kernel(
        end_kernel,
        6,
        "finish",
        [
            gradient,
            codes,
            level_column,
            asked,
            qkv_pair,
            out_pair,
            norm_zero,
            norm_one,
        ],
        [
            ((own_rows, width), f32),
            ((own_rows, 1), f32),
            ((members, depth, 3 * share), low),
            ((depth, width), low),
            ((16, width), f32),
        ],
        [
            pltpu.VMEM((groups, capacity, width), low),
            pltpu.VMEM((4 * slots, width), low),
            pltpu.VMEM((groups // 2, 2, 16, width), f32),
            pltpu.VMEM((members, 16, width), f32),
        ]
        + reduce_scratch(depth, 3 * share, low)[1:]
        + reduce_scratch(16, width, f32)
        + [pltpu.VMEM((groups // 2 - 1, depth, width), low)]
        + dma_sems(1, groups // 2) * 3
        + dma_sems(1, 3 * 2)
        + [dma((groups,))] * 2
        + dma_sems(3, 3),
    )

    table_new, table_state, level_new, level_state, norm_new, norm_state, *more = update_all(
        tables,
        table_moments,
        row_grad,
        hits,
        [qkv_zero, qkv_one, out_zero, out_one, in_zero, in_one, back_zero, back_one],
        small_sum,
        [level_table, level_moments, norm_params, norm_moments],
        [
            qkv_weight,
            qkv_moments,
            out_weight,
            out_moments,
            in_weight,
            in_moments,
            back_weight.transpose(0, 2, 1),
            back_moments.transpose(0, 1, 3, 2),
        ],
    )
    qkv_new, qkv_state, out_new, out_state, in_new, in_state, back_new, back_state = more
    back_new, back_state = back_new.transpose(0, 2, 1), back_state.transpose(0, 1, 3, 2)
    return (
        hidden,
        table_new,
        table_state,
        level_new,
        level_state,
        qkv_new,
        qkv_state,
        out_new,
        out_state,
        in_new,
        in_state,
        back_new,
        back_state,
        norm_new,
        norm_state,
    )


def solution(mesh):
    return jax.shard_map(
        fast_body if (mesh.shape["dp"], mesh.shape["mp"]) == (8, 4) else general_body,
        mesh=mesh,
        in_specs=(
            P(("dp", "mp")),
            P(("dp", "mp")),
            P("dp"),
            P(("dp", "mp"), None),
            P(None, ("dp", "mp"), None),
            P(None, None, ("dp", "mp"), None),
            P("dp", None),
            P(None, "dp", None),
            P(None, None, "dp", None),
            P(None, None, None, "dp", None),
            P(None, "dp", None),
            P(None, None, "dp", None),
            P(None, "dp", "mp"),
            P(None, None, "dp", "mp"),
            P(None, "mp", "dp"),
            P(None, None, "mp", "dp"),
            P(None, "dp"),
            P(None, None, "dp"),
        ),
        out_specs=(
            P(("dp", "mp"), None),
            P(None, ("dp", "mp"), None),
            P(None, None, ("dp", "mp"), None),
            P("dp", None),
            P(None, "dp", None),
            P(None, None, "dp", None),
            P(None, None, None, "dp", None),
            P(None, "dp", None),
            P(None, None, "dp", None),
            P(None, "dp", "mp"),
            P(None, None, "dp", "mp"),
            P(None, "mp", "dp"),
            P(None, None, "mp", "dp"),
            P(None, "dp"),
            P(None, None, "dp"),
        ),
        check_vma=False,
    )
```

```python
import math
from functools import partial

import jax
import jax.numpy as jnp
from jax import lax
from jax.experimental import pallas as pl
from jax.experimental.pallas import tpu as pltpu
from jax.sharding import PartitionSpec as P

HEADS = 12
HD = 64
STUDY_TOTAL = 16
STEP = 10


largest_value = lax.Precision.HIGHEST
beta_one = 0.9
beta_two = 0.999
adam_eps = 1e-08
norm_eps = 1e-05
rate_dense = 0.08
rate_mixing = 0.3
rate_table = 0.6
rate_norm = 0.4
decay_rate = 0.01


def spread_rows(rows):
    return lax.all_gather(rows, "mp", axis=0, tiled=True)


def summed_rows(term, count):
    return lax.psum_scatter(
        term(jnp.int32(0), count * lax.axis_size("mp")).astype(jnp.bfloat16),
        "mp",
        scatter_dimension=0,
        tiled=True,
    ).astype(jnp.float32)


def norm_forward(rows, gain, bias):
    centered = rows - jnp.mean(rows, axis=-1, keepdims=True)
    inverse = lax.rsqrt(jnp.mean(centered * centered, axis=-1, keepdims=True) + norm_eps)
    normal = centered * inverse
    return (normal * gain + bias, normal, inverse)


def norm_backward(gradient, normal, inverse, gain):
    scaled = gradient * gain
    inner_part = (
        scaled
        - jnp.mean(scaled, axis=-1, keepdims=True)
        - normal * jnp.mean(scaled * normal, axis=-1, keepdims=True)
    )
    return (inner_part * inverse, jnp.sum(gradient * normal, axis=0), jnp.sum(gradient, axis=0))


def gelu_grad(inner, gradient):
    return jax.vjp(partial(jax.nn.gelu, approximate=False), inner)[1](gradient)[0]


def head_major(rows):
    return rows.reshape(rows.shape[0], HEADS, HD).transpose(1, 0, 2)


def row_major(heads):
    return heads.transpose(1, 0, 2).reshape(heads.shape[1], HEADS * HD)


def attend_forward(query, keys, values):
    scale = HD ** (-0.5)

    def one_head(pieces):
        head_query, head_keys, head_values = pieces
        scores = (
            jnp.einsum("qd,kd->qk", head_query, head_keys, preferred_element_type=jnp.float32)
            * scale
        )
        peak = jnp.max(scores, axis=-1, keepdims=True)
        raised = jnp.exp(scores - peak)
        total = jnp.sum(raised, axis=-1, keepdims=True)
        probs = (raised / total).astype(jnp.bfloat16)
        mixed = jnp.dot(probs, head_values, preferred_element_type=jnp.float32).astype(jnp.bfloat16)
        return (mixed, (peak + jnp.log(total))[:, 0])

    mixed, log_total = lax.map(one_head, (head_major(query), head_major(keys), head_major(values)))
    return (row_major(mixed), log_total)


def attend_backward(query, keys, values, mixed_grad, log_total):
    scale = HD ** (-0.5)

    def one_head(pieces):
        head_query, head_keys, head_values, head_grad, head_total = pieces
        scores = (
            jnp.einsum("qd,kd->qk", head_query, head_keys, preferred_element_type=jnp.float32)
            * scale
        )
        probs = jnp.exp(scores - head_total[:, None])
        product = jnp.einsum(
            "qd,kd->qk", head_grad, head_values, preferred_element_type=jnp.float32
        )
        center = jnp.sum(probs * product, axis=-1, keepdims=True)
        score_grad = (probs * (product - center)).astype(jnp.bfloat16)
        query_grad = (
            jnp.dot(score_grad, head_keys, preferred_element_type=jnp.float32) * scale
        ).astype(jnp.bfloat16)
        key_grad = (
            jnp.einsum("qk,qd->kd", score_grad, head_query, preferred_element_type=jnp.float32)
            * scale
        )
        value_grad = jnp.einsum(
            "qk,qd->kd", probs.astype(jnp.bfloat16), head_grad, preferred_element_type=jnp.float32
        )
        return (query_grad, key_grad, value_grad)

    query_grad, key_grad, value_grad = lax.map(
        one_head,
        (
            head_major(query),
            head_major(keys),
            head_major(values),
            head_major(mixed_grad),
            log_total,
        ),
    )
    return (row_major(query_grad), jnp.stack([row_major(key_grad), row_major(value_grad)], axis=1))


def slots_of(row_owner):
    place = jnp.arange(row_owner.shape[0])
    earlier = (row_owner[:, None] == row_owner[None, :]) & (place[None, :] < place[:, None])
    return jnp.sum(earlier.astype(jnp.int32), axis=1)


def slotted_ids(gene_ids, row_owner, slot_index, cell_groups, capacity):
    code = row_owner * capacity + slot_index
    hot = code[None, :] == jnp.arange(cell_groups * capacity)[:, None]
    found = jnp.sum(jnp.where(hot, gene_ids[None, :] + 1, 0), axis=1) - 1
    return found.reshape(cell_groups, capacity)


def adam_step(weight, moments, gradient, rate, decay):
    first = beta_one * moments[0] + (1.0 - beta_one) * gradient
    second = beta_two * moments[1] + (1.0 - beta_two) * gradient * gradient
    first_hat = first / (1.0 - beta_one**STEP)
    second_hat = second / (1.0 - beta_two**STEP)
    new_weight = weight - rate * (first_hat / (jnp.sqrt(second_hat) + adam_eps) + decay * weight)
    return (new_weight, jnp.stack([first, second]))


def general_body(
    gene_ids,
    levels,
    study_of_cell,
    cotangent,
    tables,
    table_moments,
    level_table,
    level_moments,
    qkv_weight,
    qkv_moments,
    out_weight,
    out_moments,
    in_weight,
    in_moments,
    back_weight,
    back_moments,
    norm_params,
    norm_moments,
):
    cell_groups = lax.axis_size("dp")
    rows_here = cotangent.shape[0]
    model_width = cotangent.shape[1]
    layers = qkv_weight.shape[0]
    local_cells = study_of_cell.shape[0]
    capacity = 2 * rows_here // cell_groups
    own_rows = tables.shape[1]
    block_size = own_rows * lax.axis_size("mp")
    qkv_full, out_full, in_part, back_part, level_full = (
        lax.all_gather(qkv_weight.astype(jnp.bfloat16), "dp", axis=2, tiled=True),
        lax.all_gather(out_weight.astype(jnp.bfloat16), "dp", axis=1, tiled=True),
        lax.all_gather(in_weight.astype(jnp.bfloat16), "dp", axis=1, tiled=True),
        lax.all_gather(back_weight.astype(jnp.bfloat16), "dp", axis=2, tiled=True),
        lax.all_gather(level_table.astype(jnp.bfloat16), "dp", axis=0, tiled=True),
    )
    study_onehot = (study_of_cell[:, None] == jnp.arange(STUDY_TOTAL)[None, :]).astype(jnp.float32)
    norm_full, study_all = (
        lax.all_gather(norm_params, "dp", axis=1, tiled=True),
        lax.all_gather(study_onehot, "dp", axis=0, tiled=True),
    )
    cells_per_study = jnp.sum(study_all, axis=0)
    cell_balance_weight = (
        cell_groups
        * local_cells
        / (STUDY_TOTAL * jnp.dot(study_onehot, cells_per_study, precision=largest_value))
    )
    out_grad = cotangent * cell_balance_weight[0]
    summed_tables = jnp.sum(tables, axis=0).astype(jnp.bfloat16)
    table_rows = lax.all_gather(summed_tables, "mp", axis=0, tiled=True)
    row_owner = gene_ids // block_size
    slot_index = slots_of(row_owner)
    sent_ids = slotted_ids(gene_ids, row_owner, slot_index, cell_groups, capacity)
    asked_ids = lax.all_to_all(sent_ids, "dp", split_axis=0, concat_axis=0, tiled=True)
    present = asked_ids >= 0
    safe_row = jnp.where(present, asked_ids - lax.axis_index("dp") * block_size, 0)
    found_rows = jnp.where(present[..., None], jnp.take(table_rows, safe_row, axis=0), 0)
    returned = lax.all_to_all(found_rows, "dp", split_axis=0, concat_axis=0, tiled=True)
    gene_part = returned[row_owner, slot_index].astype(jnp.float32)
    level_hot = (levels[:, None] == jnp.arange(level_full.shape[0])[None, :]).astype(jnp.bfloat16)
    hidden = gene_part + jnp.dot(level_hot, level_full, preferred_element_type=jnp.float32)
    kept = []
    for layer in range(layers):
        norm_row = norm_full[layer]
        tokens_low = hidden.astype(jnp.bfloat16)
        projected = jnp.einsum(
            "td,cdh->tch", tokens_low, qkv_full[layer], preferred_element_type=jnp.float32
        ).astype(jnp.bfloat16)
        query = projected[:, 0]
        cell_rows = spread_rows(projected[:, 1:])
        keys, values = (cell_rows[:, 0], cell_rows[:, 1])
        mixed, log_total = attend_forward(query, keys, values)
        attention = jnp.dot(mixed, out_full[layer], preferred_element_type=jnp.float32)
        first, first_normal, first_inverse = norm_forward(
            hidden + attention, norm_row[:model_width], norm_row[model_width : 2 * model_width]
        )
        first_low = first.astype(jnp.bfloat16)
        in_layer, back_layer = (in_part[layer], back_part[layer])
        first_spread = spread_rows(first_low)
        inner = jnp.dot(first_spread, in_layer, preferred_element_type=jnp.float32)
        active = jax.nn.gelu(inner, approximate=False).astype(jnp.bfloat16)

        def feed_term(start, count):
            return jnp.dot(active, back_layer, preferred_element_type=jnp.float32)

        feed = summed_rows(feed_term, rows_here)
        second, second_normal, second_inverse = norm_forward(
            first + feed, norm_row[2 * model_width : 3 * model_width], norm_row[3 * model_width :]
        )
        kept.append(
            (
                tokens_low,
                query,
                keys,
                values,
                mixed,
                log_total,
                first_normal,
                first_inverse,
                first_spread,
                inner,
                active,
                in_layer,
                back_layer,
                second_normal,
                second_inverse,
            )
        )
        hidden = second
    gradient = out_grad
    qkv_grads = [None] * layers
    out_grads = [None] * layers
    in_grads = [None] * layers
    back_grads = [None] * layers
    norm_grads = [None] * layers
    for layer in reversed(range(layers)):
        (
            tokens_low,
            query,
            keys,
            values,
            mixed,
            log_total,
            first_normal,
            first_inverse,
            first_spread,
            inner,
            active,
            in_layer,
            back_layer,
            second_normal,
            second_inverse,
        ) = kept[layer]
        norm_row = norm_full[layer]
        grad_second, gain_two, bias_two = norm_backward(
            gradient, second_normal, second_inverse, norm_row[2 * model_width : 3 * model_width]
        )
        feed_low = grad_second.astype(jnp.bfloat16)
        feed_spread = spread_rows(feed_low)
        back_grads[layer] = jnp.einsum(
            "tf,td->fd", active, feed_spread, preferred_element_type=jnp.float32
        )
        active_grad = jnp.einsum(
            "td,fd->tf", feed_spread, back_layer, preferred_element_type=jnp.float32
        )
        inner_grad = gelu_grad(inner, active_grad).astype(jnp.bfloat16)
        in_grads[layer] = jnp.einsum(
            "td,tf->df", first_spread, inner_grad, preferred_element_type=jnp.float32
        )

        def first_term(start, count):
            return jnp.einsum("tf,df->td", inner_grad, in_layer, preferred_element_type=jnp.float32)

        first_grad = summed_rows(first_term, rows_here)
        grad_first, gain_one, bias_one = norm_backward(
            grad_second + first_grad, first_normal, first_inverse, norm_row[:model_width]
        )
        norm_grads[layer] = jnp.concatenate([gain_one, bias_one, gain_two, bias_two])
        attention_low = grad_first.astype(jnp.bfloat16)
        out_grads[layer] = jnp.einsum(
            "th,td->hd", mixed, attention_low, preferred_element_type=jnp.float32
        )
        mixed_grad = jnp.einsum(
            "td,hd->th", attention_low, out_full[layer], preferred_element_type=jnp.float32
        ).astype(jnp.bfloat16)
        query_grad, pair_partial = attend_backward(query, keys, values, mixed_grad, log_total)
        pair_grad = lax.psum_scatter(
            pair_partial.astype(jnp.bfloat16), "mp", scatter_dimension=0, tiled=True
        )
        stacked = jnp.concatenate([query_grad[:, None, :], pair_grad], axis=1)
        qkv_grads[layer] = jnp.einsum(
            "td,tch->cdh", tokens_low, stacked, preferred_element_type=jnp.float32
        )
        gradient = grad_first + jnp.einsum(
            "tch,cdh->td", stacked, qkv_full[layer], preferred_element_type=jnp.float32
        )
    level_grad = jnp.dot(level_hot.astype(jnp.float32).T, gradient, precision=largest_value)
    grad_slots = (
        jnp.zeros((cell_groups, capacity, model_width), jnp.float32)
        .at[row_owner, slot_index]
        .set(gradient)
    )
    arrived = lax.all_to_all(
        grad_slots.astype(jnp.bfloat16), "dp", split_axis=0, concat_axis=0, tiled=True
    ).astype(grad_slots.dtype)
    arrived = jnp.where(present[..., None], arrived, 0.0)
    flat_rows = safe_row.reshape(-1)
    block_grad = jax.ops.segment_sum(
        arrived.reshape(-1, model_width), flat_rows, num_segments=block_size
    )
    block_hits = jax.ops.segment_sum(
        present.reshape(-1).astype(jnp.float32), flat_rows, num_segments=block_size
    )
    row_grad, hits = (
        lax.psum_scatter(
            block_grad.astype(jnp.bfloat16), "mp", scatter_dimension=0, tiled=True
        ).astype(jnp.float32),
        lax.psum_scatter(
            block_hits.astype(jnp.bfloat16), "mp", scatter_dimension=0, tiled=True
        ).astype(jnp.float32),
    )
    qkv_sum, out_sum, in_sum, back_sum, level_sum, norm_sum = (
        lax.psum_scatter(
            jnp.stack(qkv_grads).astype(jnp.bfloat16), "dp", scatter_dimension=2, tiled=True
        ).astype(jnp.float32),
        lax.psum_scatter(
            jnp.stack(out_grads).astype(jnp.bfloat16), "dp", scatter_dimension=1, tiled=True
        ).astype(jnp.float32),
        lax.psum_scatter(
            jnp.stack(in_grads).astype(jnp.bfloat16), "dp", scatter_dimension=1, tiled=True
        ).astype(jnp.float32),
        lax.psum_scatter(
            jnp.stack(back_grads).astype(jnp.bfloat16), "dp", scatter_dimension=2, tiled=True
        ).astype(jnp.float32),
        lax.psum_scatter(
            level_grad.astype(jnp.bfloat16), "dp", scatter_dimension=0, tiled=True
        ).astype(jnp.float32),
        lax.psum_scatter(
            jnp.stack(norm_grads).astype(jnp.bfloat16), "dp", scatter_dimension=1, tiled=True
        ).astype(jnp.float32),
    )
    qkv_sum, out_sum, level_sum, norm_sum = (
        lax.psum(qkv_sum.astype(jnp.bfloat16), "mp").astype(jnp.float32),
        lax.psum(out_sum.astype(jnp.bfloat16), "mp").astype(jnp.float32),
        lax.psum(level_sum.astype(jnp.bfloat16), "mp").astype(jnp.float32),
        lax.psum(norm_sum.astype(jnp.bfloat16), "mp").astype(jnp.float32),
    )
    touched = (hits > 0)[None, :, None]
    table_grad = jnp.broadcast_to(row_grad[None], tables.shape)
    table_new, table_state = adam_step(tables, table_moments, table_grad, rate_table, decay_rate)
    table_new = jnp.where(touched, table_new, tables)
    table_state = jnp.where(touched[None], table_state, table_moments)
    level_new, level_state = adam_step(
        level_table, level_moments, level_sum, rate_table, decay_rate
    )
    qkv_new, qkv_state = adam_step(qkv_weight, qkv_moments, qkv_sum, rate_dense, decay_rate)
    out_new, out_state = adam_step(out_weight, out_moments, out_sum, rate_mixing, decay_rate)
    in_new, in_state = adam_step(in_weight, in_moments, in_sum, rate_dense, decay_rate)
    back_new, back_state = adam_step(back_weight, back_moments, back_sum, rate_dense, decay_rate)
    norm_new, norm_state = adam_step(norm_params, norm_moments, norm_sum, rate_norm, 0.0)
    return (
        hidden,
        table_new,
        table_state,
        level_new,
        level_state,
        qkv_new,
        qkv_state,
        out_new,
        out_state,
        in_new,
        in_state,
        back_new,
        back_state,
        norm_new,
        norm_state,
    )


MESH = pl.DeviceIdType.MESH
SIB, FACE = 0, 1
TILE = 128


def nn(a, b):
    return lax.dot_general(a, b, (((1,), (0,)), ((), ())), preferred_element_type=jnp.float32)


def nt(a, b):
    return lax.dot_general(a, b, (((1,), (1,)), ((), ())), preferred_element_type=jnp.float32)


def tn(a, b):
    return lax.dot_general(a, b, (((0,), (0,)), ((), ())), preferred_element_type=jnp.float32)


def near_devices():
    group, member = lax.axis_index("dp"), lax.axis_index("mp")
    core = member % 2
    return (group, member + 1 - 2 * core), (group, (member + 2) % 4)


def greet(peers):
    barrier = pltpu.get_barrier_semaphore()
    for peer in peers:
        pl.semaphore_signal(barrier, inc=1, device_id=peer, device_id_type=MESH)
    pl.semaphore_wait(barrier, len(peers))


def send(source, target, sems, index, peer):
    copy = pltpu.make_async_remote_copy(
        src_ref=source,
        dst_ref=target,
        send_sem=sems[0].at[index],
        recv_sem=sems[1].at[index],
        device_id=peer,
        device_id_type=MESH,
    )
    copy.start()
    return copy


PIECES = 2


def columns_of(group):
    return group // 2, group % 2


def group_peers():
    group, member = lax.axis_index("dp"), lax.axis_index("mp")
    count = lax.axis_size("dp")
    return [((group + k) % count, member) for k in range(1, count)]


def mates():
    group, member = lax.axis_index("dp"), lax.axis_index("mp")
    count = lax.axis_size("mp")
    return [(group, (member + k) % count) for k in range(1, count)]


class Spread:
    def __init__(self, mine, whole, sems, part):
        group, member = lax.axis_index("dp"), lax.axis_index("mp")
        depth = lax.axis_size("dp") // 2
        z, x = columns_of(group)
        self.beside = (group + 1 - 2 * x, member)
        self.whole, self.sems, self.part, self.depth = whole, sems, part, depth
        self.came = [((z + depth - k) % depth) * 2 + x for k in range(1, depth)]
        self.along = [
            send(mine, whole.at[group], sems, (part, k - 1), (((z + k) % depth) * 2 + x, member))
            for k in range(1, depth)
        ]
        self.across = [send(mine, whole.at[group], sems, (part, depth - 1), self.beside)]
        whole[group] = mine[...]

    def hand_on(self):
        for k in range(1, self.depth):
            self.along[k - 1].wait_recv()
            block = self.whole.at[self.came[k - 1]]
            self.across.append(
                send(block, block, self.sems, (self.part, self.depth - 1 + k), self.beside)
            )

    def arrive(self):
        for copy in self.across:
            copy.wait_recv()

    def finish(self):
        for copy in [*self.along, *self.across]:
            copy.wait_send()


class Reduce:
    def __init__(self, source, near, come, sems, line):
        group, self.member = lax.axis_index("dp"), lax.axis_index("mp")
        self.depth = lax.axis_size("dp") // 2
        self.z, self.x = columns_of(group)
        self.source, self.near, self.come = source, near, come
        self.sems, self.line, self.copies = sems, line, []
        if source is not None:
            beside = (group + 1 - 2 * self.x, self.member)
            self.first = send(source.at[:, 1 - self.x], near, sems, (line, 0), beside)

    def pair(self, z):
        term = self.near[z].astype(jnp.float32)
        return term if self.source is None else term + self.source[z, self.x].astype(jnp.float32)

    def add_up(self):
        self.first.wait_recv()
        for z in range(self.depth):
            self.near[z] = self.pair(z).astype(self.near.dtype)
        self.first.wait_send()

    def middle(self):
        if self.source is not None:
            self.first.wait_recv()
        for k in range(1, self.depth):
            z = (self.z + k) % self.depth
            if self.source is not None:
                self.near[z] = self.pair(z).astype(self.near.dtype)
            self.copies.append(
                send(
                    self.near.at[z],
                    self.come.at[k - 1],
                    self.sems,
                    (self.line, k),
                    (z * 2 + self.x, self.member),
                )
            )

    def finish(self):
        term = self.pair(self.z)
        for k, copy in enumerate(self.copies):
            copy.wait_recv()
            term = term + self.come[k].astype(jnp.float32)
        for copy in self.copies:
            copy.wait_send()
        if self.source is not None:
            self.first.wait_send()
        return term


def reduce_scratch(rows, columns, dtype):
    depth = lax.axis_size("dp") // 2
    return [pltpu.VMEM((depth, rows, columns), dtype), pltpu.VMEM((depth - 1, rows, columns), dtype)]


def dma_sems(*shape):
    return [pltpu.SemaphoreType.DMA(shape)] * 2


class MixReduce:
    def __init__(self, source, near, come, sems, line):
        group, self.member = lax.axis_index("dp"), lax.axis_index("mp")
        self.depth = lax.axis_size("dp") // 2
        self.z, self.x = columns_of(group)
        self.sems, self.line = sems, line
        self.source, self.near, self.come = source, near, come
        if source is not None:
            beside = (group + 1 - 2 * self.x, self.member)
            self.first = send(source.at[1 - self.x], near, sems, (line, 0), beside)

    def copy(self, slot, there):
        return pltpu.make_async_remote_copy(
            src_ref=self.near,
            dst_ref=self.come.at[slot],
            send_sem=self.sems[0].at[self.line, 1 + slot],
            recv_sem=self.sems[1].at[self.line, 1 + slot],
            device_id=(there, self.member),
            device_id_type=MESH,
        )

    def to_root(self):
        slot = (self.member + 2 * self.depth - self.z - 1) % self.depth
        return self.copy(slot, self.member * 2 + self.x)

    def add_up(self):
        self.first.wait_recv()
        term = self.source[self.x].astype(jnp.float32) + self.near[...].astype(jnp.float32)
        self.near[...] = term.astype(self.near.dtype)
        self.first.wait_send()

    def middle(self):
        if self.source is not None:
            self.add_up()

        @pl.when(self.z != self.member)
        def _():
            self.to_root().start()

    def finish(self):
        @pl.when(self.z == self.member)
        def _():
            for slot in range(self.depth - 1):
                self.copy(slot, (self.member * 2 + self.x + 2) % (2 * self.depth)).wait_recv()

        @pl.when(self.z != self.member)
        def _():
            self.to_root().wait_send()

        term = self.near[...].astype(jnp.float32)
        for slot in range(self.depth - 1):
            term = term + self.come[slot].astype(jnp.float32)
        return term


class Gather:
    def __init__(self, buf, sems, line, pieces=PIECES):
        self.buf, self.sems, self.line, self.pieces = buf, sems, line, pieces
        self.sib, self.face = near_devices()
        self.rows = buf.shape[0] // 4
        self.size = self.rows // pieces
        self.across, self.beside, self.handed = [], [], []

    def piece(self, b, i):
        return self.buf.at[pl.ds(b * self.rows + i * self.size, self.size)]

    def start(self, i):
        mine = self.piece(0, i)
        self.across.append(send(mine, self.piece(2, i), self.sems, (self.line, i), self.face))
        self.beside.append(
            send(mine, self.piece(1, i), self.sems, (self.line, self.pieces + i), self.sib)
        )

    def wait_beside(self):
        for copy in self.beside:
            copy.wait_recv()

    def hand_on(self, i):
        self.across[i].wait_recv()
        self.handed.append(
            send(
                self.piece(2, i),
                self.piece(3, i),
                self.sems,
                (self.line, 2 * self.pieces + i),
                self.sib,
            )
        )

    def wait_handed(self, i):
        self.handed[i].wait_recv()

    def finish(self):
        for copy in [*self.across, *self.beside, *self.handed]:
            copy.wait_send()


class Share:
    def __init__(self, buf, sems, line):
        self.buf, self.sems, self.line = buf, sems, line
        member = lax.axis_index("mp")
        self.sib, self.face = near_devices()
        self.copies = [
            send(buf.at[member], buf.at[member], sems, (line, k), peer)
            for k, peer in enumerate((self.face, self.sib))
        ]

    def hand_on(self):
        self.copies[0].wait_recv()
        block = self.buf.at[self.face[1]]
        self.copies.append(send(block, block, self.sems, (self.line, 2), self.sib))

    def arrive(self):
        for copy in self.copies[1:]:
            copy.wait_recv()

    def finish(self):
        for copy in self.copies:
            copy.wait_send()


class RootShare:
    def __init__(self, value, buf, sems, line):
        self.buf, self.sems, self.line = buf, sems, line
        self.member = lax.axis_index("mp")
        self.root, _ = columns_of(lax.axis_index("dp"))
        self.sib, self.face = near_devices()

        @pl.when(self.member == self.root)
        def _():
            buf[...] = value.astype(buf.dtype)
            for k, peer in enumerate((self.face, self.sib)):
                self.copy(k, peer).start()

    def copy(self, k, peer):
        return pltpu.make_async_remote_copy(
            src_ref=self.buf,
            dst_ref=self.buf,
            send_sem=self.sems[0].at[self.line, k],
            recv_sem=self.sems[1].at[self.line, 0],
            device_id=peer,
            device_id_type=MESH,
        )

    def hand_on(self):
        @pl.when(self.member != self.root)
        def _():
            self.copy(0, self.sib).wait_recv()

        @pl.when(self.face[1] == self.root)
        def _():
            self.copy(2, self.sib).start()

    def finish(self):
        @pl.when(self.member == self.root)
        def _():
            for k, peer in enumerate((self.face, self.sib)):
                self.copy(k, peer).wait_send()

        @pl.when(self.face[1] == self.root)
        def _():
            self.copy(2, self.sib).wait_send()


class Total:
    def __init__(self, out, into, sems, line, pieces=PIECES):
        self.out, self.into, self.sems, self.line, self.pieces = out, into, sems, line, pieces
        self.sib, self.face = near_devices()
        self.size = out.shape[1] // pieces
        self.far, self.facing, self.beside = [], [], []

    def give(self, b, i, term, peer):
        piece = pl.ds(i * self.size, self.size)
        self.out[b, piece, :] = term.astype(jnp.bfloat16)
        return send(
            self.out.at[b, piece],
            self.into.at[b, piece],
            self.sems,
            (self.line, b * self.pieces + i),
            peer,
        )

    def came(self, b, i):
        return self.into[b, pl.ds(i * self.size, self.size), :].astype(jnp.float32)

    def part(self, term, i):
        return term[i * self.size : (i + 1) * self.size]

    def give_far(self, i, term):
        self.far.append(self.give(0, i, term, self.sib))

    def give_facing(self, i, term):
        self.far[i].wait_recv()
        self.facing.append(self.give(1, i, term + self.came(0, i), self.face))

    def give_beside(self, i, term):
        self.beside.append(self.give(2, i, term, self.sib))

    def take(self, i, term):
        self.beside[i].wait_recv()
        self.facing[i].wait_recv()
        return term + self.came(2, i) + self.came(1, i)

    def finish(self):
        for copy in [*self.far, *self.facing, *self.beside]:
            copy.wait_send()


def gelu_pair(x):
    t = 1.0 / (1.0 + (0.3275911 * 0.7071067811865476) * jnp.abs(x))
    raised = jnp.exp(-0.5 * x * x)
    series = t * (
        0.254829592
        + t * (-0.284496736 + t * (1.421413741 + t * (-1.453152027 + t * 1.061405429)))
    )
    upper = 0.5 * series * raised
    share = jnp.where(x >= 0, 1.0 - upper, upper)
    return x * share, share + x * raised * 0.3989422804014327


def column(ref):
    line = ref[...].astype(jnp.float32)
    return jnp.broadcast_to(line, (8, line.shape[1])).T[:, 0:1]


def hot_places(ref, count):
    place = lax.broadcasted_iota(jnp.int32, (ref.shape[1], count), 1)
    return (column(ref) == place.astype(jnp.float32)).astype(jnp.bfloat16)


def rows_joined(ref):
    blocks = ref[...]
    return blocks.reshape(blocks.shape[0] * blocks.shape[1], blocks.shape[2])


def around(peers):
    group, member = lax.axis_index("dp"), lax.axis_index("mp")
    depth = lax.axis_size("dp") // 2
    z, x = columns_of(group)
    along = [(((z + k) % depth) * 2 + x, member) for k in range(1, depth)]
    return [*peers, *along, (group + 1 - 2 * x, member)]


def layers_kernel(*refs):
    refs = iter(refs)
    take = lambda count: [next(refs) for _ in range(count)]
    hidden, cotangent, scale = take(3)
    norms = take(2)
    qkv_zero, out_zero, out_one = take(3)
    qkv_mine, in_mine, back_mine = take(3)
    mine = [in_mine.at[0], back_mine.at[0], qkv_mine.at[1], in_mine.at[1], back_mine.at[1]]
    encoded, gradient_out = take(2)
    norm_grads = take(2)
    qkv_pair, out_pair = take(2)
    in_sums, back_sums = take(2), take(2)
    qkv_shared, out_shared = take(2)
    in_zero, back_zero, qkv_one, in_one, back_one = whole = take(5)
    saved = [take(11), take(11)]
    mixed_t, held, out, into = take(4)
    feeds, inner, lows, mixed_grad, key_grad, value_grad, query_grad, head_grads = take(8)
    in_g, back_g, qkv_g, out_g = take(4)
    in_near, in_come, back_near, back_come = take(2), take(1), take(2), take(1)
    qkv_parts, out_parts = take(2), take(2)
    gather_sems, total_sems, spread_sem = take(2), take(2), take(2)
    in_sems, back_sems, qkv_sems, out_sems = take(2), take(2), take(2), take(2)
    share_sems = take(2)
    weights = [(qkv_zero, out_zero, in_zero, back_zero), (qkv_one, out_one, in_one, back_one)]
    greet(around(near_devices()))
    rows = hidden.shape[0]
    size = rows // PIECES
    share = mixed_t.shape[0]
    per_device = share // HD
    pieces = range(PIECES)

    def block(b):
        return pl.ds(b * rows, rows)

    def piece(b, i):
        return pl.ds(b * rows + i * size, size)

    def spread_of(part):
        return Spread(mine[part], whole[part], spread_sem, part)

    def send_tokens(layer, i, value):
        saved[layer][4][piece(0, i), :] = value.astype(jnp.bfloat16)
        gathers[layer].start(i)

    gathers = [Gather(saved[layer][4], gather_sems, layer) for layer in range(2)]
    for i in pieces:
        send_tokens(0, i, hidden[piece(0, i), :])
    spreads = [spread_of(part) for part in range(2)]
    held[...] = hidden[...]

    def forward(layer, after_projection, after_far, after_attention, before_feed, after_feed, close):
        second_normal, second_inverse, first_normal, first_inverse = saved[layer][:4]
        tokens, heads, mixed, logs, firsts, active, slope = saved[layer][4:]
        qkv_w, out_w, in_w, back_w = weights[layer]
        gather, norm = gathers[layer], norms[layer]

        def project(place):
            parts = nn(tokens[place, :], rows_joined(qkv_w))
            for j in range(3 * per_device):
                part = parts[:, j * HD : (j + 1) * HD]
                if j < per_device:
                    part = part * HD ** (-0.5)
                heads[j, place, :] = part.astype(jnp.bfloat16)

        project(block(0))
        gather.wait_beside()
        project(block(1))
        for i in pieces:
            gather.hand_on(i)
            project(piece(2, i))
        for i in pieces:
            gather.wait_handed(i)
        project(block(3))
        gather.finish()
        after_projection()

        def attend(b):
            def one_head(h, carry):
                scores = nt(heads[per_device + h], heads[h, block(b), :])
                peak = jnp.max(scores, axis=0, keepdims=True)
                raised = jnp.exp(scores - peak)
                total = jnp.sum(raised, axis=0, keepdims=True)
                result = tn(heads[2 * per_device + h], raised.astype(jnp.bfloat16)) / total
                mixed_t[pl.ds(pl.multiple_of(h * HD, HD), HD), :] = result
                logs[b * per_device + h] = peak + jnp.log(total)
                return carry

            lax.fori_loop(0, per_device, one_head, 0)
            rows_mixed = mixed_t[...].T.astype(jnp.bfloat16)
            mixed[block(b), :] = rows_mixed
            return nn(rows_mixed, rows_joined(out_w))

        total = Total(out, into, total_sems, layer)
        term = attend(3)
        for i in pieces:
            total.give_far(i, total.part(term, i))
        term = attend(2)
        for i in pieces:
            total.give_facing(i, total.part(term, i))
        after_far()
        term = attend(1)
        for i in pieces:
            total.give_beside(i, total.part(term, i))
        held[...] += attend(0)
        after_attention()
        gather_two = Gather(firsts, gather_sems, 2 + layer)
        for i in pieces:
            place = piece(0, i)
            first, normal, inverse = norm_forward(
                total.take(i, held[place, :]), norm[0:1, :], norm[1:2, :]
            )
            firsts[place, :] = first.astype(jnp.bfloat16)
            gather_two.start(i)
            first_normal[place, :] = normal
            first_inverse[place, :] = inverse
            held[place, :] = first
        total.finish()
        before_feed()

        def feed(place):
            value, gradient = gelu_pair(nn(firsts[place, :], rows_joined(in_w)))
            value = value.astype(jnp.bfloat16)
            active[place, :] = value
            slope[place, :] = gradient.astype(jnp.bfloat16)
            return nt(value, rows_joined(back_w))

        total = Total(out, into, total_sems, 2 + layer)
        held[...] += feed(block(0))
        gather_two.wait_beside()
        term = feed(block(1))
        for i in pieces:
            total.give_beside(i, total.part(term, i))
        for i in pieces:
            gather_two.hand_on(i)
            term = feed(piece(2, i))
            gather_two.wait_handed(i)
            total.give_far(i, feed(piece(3, i)))
            total.give_facing(i, term)
        after_feed()
        for i in pieces:
            place = piece(0, i)
            result, normal, inverse = norm_forward(
                total.take(i, held[place, :]), norm[2:3, :], norm[3:4, :]
            )
            second_normal[place, :] = normal
            second_inverse[place, :] = inverse
            close(i, result)
        gather_two.finish()
        total.finish()

    def note(layer, row, i, gain, bias):
        target = norm_grads[layer]
        if i:
            gain, bias = gain + target[row, :], bias + target[row + 1, :]
        target[row : row + 1, :] = gain[None]
        target[row + 1 : row + 2, :] = bias[None]

    feed_gathers = [Gather(feeds, gather_sems, 4 + layer) for layer in range(2)]

    def send_feed_grad(layer, i, gradient):
        place = piece(0, i)
        grad_second, gain, bias = norm_backward(
            gradient, saved[layer][0][place, :], saved[layer][1][place, :], norms[layer][2:3, :]
        )
        feeds[place, :] = grad_second.astype(jnp.bfloat16)
        feed_gathers[layer].start(i)
        note(layer, 2, i, gain, bias)
        held[place, :] = grad_second

    def backward(layer, before_in, after_back, after_score, close_in, close):
        _, _, first_normal, first_inverse = saved[layer][:4]
        tokens, heads, mixed, logs, firsts, active, slope = saved[layer][4:]
        qkv_w, out_w, in_w, back_w = weights[layer]
        gather = feed_gathers[layer]

        def feed(place):
            part = nn(feeds[place, :], rows_joined(back_w)) * slope[place, :].astype(jnp.float32)
            part = part.astype(jnp.bfloat16)
            inner[place, :] = part
            return nt(part, rows_joined(in_w))

        total = Total(out, into, total_sems, 4 + layer)
        held[...] += feed(block(0))
        gather.wait_beside()
        term = feed(block(1))
        for i in pieces:
            total.give_beside(i, total.part(term, i))
        for i in pieces:
            gather.hand_on(i)
            term = feed(piece(2, i))
            gather.wait_handed(i)
            total.give_far(i, feed(piece(3, i)))
            total.give_facing(i, term)
        gather.finish()
        before_in()
        in_g[...] = tn(firsts[...], inner[...]).astype(jnp.bfloat16).reshape(in_g.shape)
        in_reduce = Reduce(in_g, in_near[layer], in_come[0], in_sems, layer)
        gather_two = Gather(lows, gather_sems, 6 + layer)
        for i in pieces:
            place = piece(0, i)
            grad_first, gain, bias = norm_backward(
                total.take(i, held[place, :]),
                first_normal[place, :],
                first_inverse[place, :],
                norms[layer][0:1, :],
            )
            lows[place, :] = grad_first.astype(jnp.bfloat16)
            gather_two.start(i)
            note(layer, 0, i, gain, bias)
            held[place, :] = grad_first
        total.finish()
        back_g[...] = tn(feeds[...], active[...]).astype(jnp.bfloat16).reshape(back_g.shape)
        back_reduce = Reduce(back_g, back_near[layer], back_come[0], back_sems, layer)
        after_back()

        def spread(place):
            parts = nt(lows[place, :], rows_joined(out_w))
            for j in range(per_device):
                mixed_grad[j, place, :] = parts[:, j * HD : (j + 1) * HD].astype(jnp.bfloat16)

        def score(b):
            def one_head(h, carry):
                query, key = heads[h, block(b), :], heads[per_device + h]
                upper = mixed_grad[h, block(b), :]
                prob = jnp.exp(nt(key, query) - logs[b * per_device + h])
                product = nt(heads[2 * per_device + h], upper)
                center = jnp.sum(prob * product, axis=0, keepdims=True)
                score_grad = (prob * (product - center)).astype(jnp.bfloat16)
                key_term = nn(score_grad, query)
                value_term = nn(prob.astype(jnp.bfloat16), upper)
                if b:
                    key_term, value_term = key_term + key_grad[h], value_term + value_grad[h]
                key_grad[h] = key_term
                value_grad[h] = value_term
                turned = tn(key, score_grad) * HD ** (-0.5)
                query_grad[h, block(b), :] = turned.T.astype(jnp.bfloat16)
                return carry

            lax.fori_loop(0, per_device, one_head, 0)

        spread(block(0))
        score(0)
        for i in pieces:
            gather_two.hand_on(i)
        gather_two.wait_beside()
        spread(block(1))
        score(1)
        after_score()
        in_reduce.middle()
        spread(block(2))
        score(2)
        for i in pieces:
            gather_two.wait_handed(i)
        spread(block(3))
        back_reduce.middle()
        score(3)
        gather_two.finish()
        for h in range(per_device):
            for c, grad in enumerate((query_grad, key_grad, value_grad)):
                start = c * share + h * HD
                head_grads[:, start : start + HD] = grad[h].astype(jnp.bfloat16)

        total = Total(out, into, total_sems, 6 + layer)
        weight = rows_joined(qkv_w)
        term = nt(head_grads[block(3), :], weight)
        for i in pieces:
            total.give_far(i, total.part(term, i))
        term = nt(head_grads[block(2), :], weight)
        for i in pieces:
            total.give_facing(i, total.part(term, i))
        term = nt(head_grads[block(1), :], weight)
        for i in pieces:
            total.give_beside(i, total.part(term, i))
        held[...] += nt(head_grads[block(0), :], weight)
        qkv_g[...] = tn(tokens[...], head_grads[...]).astype(jnp.bfloat16).reshape(qkv_g.shape)
        out_g[...] = tn(mixed[...], lows[...]).astype(jnp.bfloat16).reshape(out_g.shape)
        close_in()
        for i in pieces:
            close(i, total.take(i, held[piece(0, i), :]))
        total.finish()
        return in_reduce, back_reduce

    def between(i, result):
        held[piece(0, i), :] = result
        send_tokens(1, i, result)

    def after_attention_zero():
        spreads[1].hand_on()
        spreads.append(spread_of(2))

    def before_feed_zero():
        spreads[0].arrive()
        spreads[1].arrive()
        spreads.append(spread_of(3))

    def after_feed_zero():
        spreads[2].hand_on()
        spreads.append(spread_of(4))

    forward(
        0,
        lambda: None,
        spreads[0].hand_on,
        after_attention_zero,
        before_feed_zero,
        after_feed_zero,
        between,
    )
    spreads[2].arrive()

    def turn(i, result):
        encoded[piece(0, i), :] = result
        send_feed_grad(1, i, cotangent[piece(0, i), :] * scale[...])

    def before_feed_one():
        spreads[3].arrive()
        spreads[4].arrive()

    forward(
        1,
        spreads[3].hand_on,
        spreads[4].hand_on,
        lambda: None,
        before_feed_one,
        lambda: None,
        turn,
    )
    for spread in spreads:
        spread.finish()

    reduces, shares = [], []
    none = lambda: None

    def start_prior():
        reduces.append(Reduce(qkv_g, *qkv_parts, qkv_sems, 0))
        reduces.append(MixReduce(out_g, *out_parts, out_sems, 0))

    in_reduce, back_reduce = backward(
        1,
        none,
        none,
        none,
        start_prior,
        lambda i, value: send_feed_grad(0, i, value),
    )
    in_prior, back_prior = in_reduce, back_reduce

    def prior_middle():
        in_sums[1][...] = in_prior.finish()
        back_sums[1][...] = back_prior.finish()
        for reduce in reduces:
            reduce.middle()

    def prior_finish():
        qkv_shared[lax.axis_index("mp")] = reduces[0].finish().astype(qkv_shared.dtype)
        shares.append(Share(qkv_shared, share_sems, 0))
        shares.append(RootShare(reduces[1].finish(), out_shared, share_sems, 1))

    def start_pair():
        for share in shares:
            share.hand_on()
        reduces.append(Reduce(qkv_g, qkv_pair, None, qkv_sems, 1))
        reduces.append(MixReduce(out_g, out_pair, None, out_sems, 1))

    def last(i, value):
        gradient_out[piece(0, i), :] = value

    in_reduce, back_reduce = backward(0, prior_middle, none, prior_finish, start_pair, last)
    in_sums[0][...] = in_reduce.finish()
    back_sums[0][...] = back_reduce.finish()
    shares[0].arrive()
    for share in shares:
        share.finish()
    for reduce in reduces[2:]:
        reduce.add_up()


def halves():
    depth = lax.axis_size("dp") // 2
    steps = [*range(1, depth), 0]
    return [[(k, (k + 1 + half) % 2) for k in steps] for half in range(2)]


def group_at(step, back=False):
    group = lax.axis_index("dp")
    depth = lax.axis_size("dp") // 2
    z, x = columns_of(group)
    along = depth - step[0] if back else step[0]
    return ((z + along) % depth) * 2 + (x + step[1]) % 2


def start_kernel(*refs):
    refs = iter(refs)
    take = lambda count: [next(refs) for _ in range(count)]
    sent_ids, codes, levels, tables, small = take(5)
    qkv_mine, out_pair = take(2)
    mine, out_mine = [qkv_mine.at[0]], [out_pair.at[0], out_pair.at[1]]
    hidden, asked, scale = take(3)
    norms = take(2)
    whole, out_whole = take(1), take(2)
    small_all, found, returned, out_a, into_a, table_rows, stream = take(7)
    total_a, small_sems, spread_sem, out_sems, id_sems, near_sems, row_sems = [take(2) for _ in range(7)]
    (stream_sems,) = take(1)
    group, member = lax.axis_index("dp"), lax.axis_index("mp")
    groups, members = lax.axis_size("dp"), lax.axis_size("mp")
    depth = groups // 2
    z, x = columns_of(group)
    beside = (group + 1 - 2 * x, member)
    peers = group_peers()
    sib, face = near_devices()
    far = (group, (sib[1] + 2) % members)
    own_rows = table_rows.shape[0]
    part = own_rows // 3
    streams = [
        pltpu.make_async_copy(
            tables.at[:, pl.ds(n * part, part)], stream.at[n % 2], stream_sems.at[n % 2]
        )
        for n in range(3)
    ]
    streams[0].start()
    streams[1].start()

    def add_tables(n):
        streams[n].wait()
        total = stream[n % 2, 0]
        for t in range(1, stream.shape[1]):
            total = total + stream[n % 2, t]
        table_rows[n * part : (n + 1) * part, :] = total.astype(table_rows.dtype)

    greet([*peers, *mates()])

    id_copies = [
        send(sent_ids.at[peer[0]], asked.at[0, group], id_sems, k, peer)
        for k, peer in enumerate(peers)
    ]
    asked[0, group] = sent_ids[group]
    small_spread = Spread(small, small_all, small_sems, 0)
    spreads = [Spread(a, b, spread_sem, p) for p, (a, b) in enumerate(zip(mine, whole))]
    add_tables(0)
    streams[2].start()
    for copy in id_copies:
        copy.wait_recv()
    near_copies = [
        send(asked.at[0], asked.at[k + 1], near_sems, k, peer)
        for k, peer in enumerate((sib, face, far))
    ]
    def root_copies():
        return [
            pltpu.make_async_remote_copy(
                src_ref=mine_out,
                dst_ref=target.at[x],
                send_sem=out_sems[0].at[p, k],
                recv_sem=out_sems[1].at[p, 0],
                device_id=(((z + k) % depth) * 2 + x, member),
                device_id_type=MESH,
            )
            for p, (mine_out, target) in enumerate(zip(out_mine, out_whole))
            for k in range(1, depth)
        ]

    @pl.when(z == member)
    def _():
        for copy in root_copies():
            copy.start()
        for mine_out, target in zip(out_mine, out_whole):
            target[x] = mine_out[...]

    add_tables(1)
    add_tables(2)
    for copy in near_copies:
        copy.wait_recv()
    first_row = ((group * members + member) * own_rows).astype(jnp.float32)
    capacity = asked.shape[3]
    half_slots = depth * capacity

    def lookup(r, half):
        line = jnp.concatenate([asked[r, group_at(step)] for step in halves()[half]], axis=1)
        line = line.astype(jnp.float32) - first_row
        line = jnp.broadcast_to(line, (8, half_slots)).T[:, 0:1]
        place = lax.broadcasted_iota(jnp.int32, (half_slots, own_rows), 1)
        hot = (line == place.astype(jnp.float32)).astype(jnp.bfloat16)
        return nn(hot, table_rows[...])

    total = Total(out_a, into_a, total_a, 0, 2)
    for half in range(2):
        total.give_far(half, lookup(3, half))
        total.give_facing(half, lookup(2, half))
    for half in range(2):
        total.give_beside(half, lookup(1, half))
    own = [lookup(0, half) for half in range(2)]
    small_spread.hand_on()
    spreads[0].hand_on()

    @pl.when(z != member)
    def _():
        for p in range(2):
            pltpu.make_async_remote_copy(
                src_ref=out_mine[p],
                dst_ref=out_whole[p].at[x],
                send_sem=out_sems[0].at[p, 0],
                recv_sem=out_sems[1].at[p, 0],
                device_id=beside,
                device_id_type=MESH,
            ).wait_recv()

    out_copies = [
        pltpu.make_async_remote_copy(
            src_ref=target.at[x],
            dst_ref=target.at[x],
            send_sem=out_sems[0].at[p, depth],
            recv_sem=out_sems[1].at[p, 1],
            device_id=beside,
            device_id_type=MESH,
        )
        for p, target in enumerate(out_whole)
    ]
    for copy in out_copies:
        copy.start()
    row_copies = []
    for half, steps in enumerate(halves()):
        rows_found = total.take(half, own[half]).astype(jnp.bfloat16)
        found[half * depth : (half + 1) * depth] = rows_found.reshape(depth, capacity, -1)
        for n, step in enumerate(steps):
            slot = half * depth + n
            if step == (0, 0):
                returned[group] = found[slot]
            else:
                row_copies.append(
                    send(
                        found.at[slot],
                        returned.at[group],
                        row_sems,
                        slot,
                        (group_at(step), member),
                    )
                )
    small_spread.arrive()
    for layer, target in enumerate(norms):
        half = target.shape[1] // 2
        for c in range(groups):
            start = (c % 2) * half
            target[c // 2 : c // 2 + 1, start : start + half] = small_all[
                c, 8:9, layer * half : (layer + 1) * half
            ]
    counts = small_all[0, 9:10, :]
    for c in range(1, groups):
        counts = counts + small_all[c, 9:10, :]
    same = jnp.sum(counts * small[9:10, :], axis=1, keepdims=True)
    scale[...] = groups / (STUDY_TOTAL * same)
    level_rows = 8 * groups
    level_full = jnp.concatenate([small_all[c, 0:8, :] for c in range(groups)], axis=0)
    rows = hidden.shape[0]
    level_hot = hot_places(levels, level_rows)
    level_part = nn(level_hot, level_full.astype(jnp.bfloat16))
    slot_hot = hot_places(codes, groups * capacity)
    for copy in row_copies:
        copy.wait_recv()
    hidden[...] = nn(slot_hot, rows_joined(returned)) + level_part

    for copy in [*id_copies, *near_copies, *row_copies]:
        copy.wait_send()
    total.finish()
    for spread in spreads:
        spread.arrive()
    for spread in (small_spread, *spreads):
        spread.finish()
    for copy in out_copies:
        copy.wait()

    @pl.when(z == member)
    def _():
        for copy in root_copies():
            copy.wait_send()


def end_kernel(*refs):
    refs = iter(refs)
    take = lambda count: [next(refs) for _ in range(count)]
    gradient, codes, levels, asked, qkv_pair, out_pair = take(6)
    norm_zero, norm_one = take(2)
    row_grad, hits, qkv_shared, out_shared, small_sum = take(5)
    slots, arrived, small_g, small_in = take(4)
    qkv_come, small_near, small_come, mix_come = take(4)
    mix_sems, qkv_sems, small_sems, gather_sems, row_sems, mate_sems = [take(2) for _ in range(6)]
    group, member = lax.axis_index("dp"), lax.axis_index("mp")
    groups, members = lax.axis_size("dp"), lax.axis_size("mp")
    depth = groups // 2
    z, x = columns_of(group)
    peers, near = group_peers(), mates()
    greet([*peers, *near])
    rows, width = gradient.shape
    capacity = slots.shape[1]
    count = groups * capacity
    half_count = depth * capacity

    slot_hot = hot_places(codes, count)
    high = gradient[...].astype(jnp.bfloat16)
    slots[...] = tn(slot_hot, high).astype(jnp.bfloat16).reshape(slots.shape)
    row_copies = []
    for half, steps in enumerate(halves()):
        copies = []
        for n, step in enumerate(steps):
            slot = half * depth + n
            target = arrived.at[pl.ds(slot * capacity, capacity)]
            if step == (0, 0):
                arrived[slot * capacity : (slot + 1) * capacity, :] = slots[group]
            else:
                there = group_at(step)
                copies.append(send(slots.at[there], target, row_sems, slot, (there, member)))
        row_copies.append(copies)
    qkv_reduce = Reduce(None, qkv_pair, qkv_come, qkv_sems, 0)
    mix = MixReduce(None, out_pair, mix_come, mix_sems, 0)

    level_hot = hot_places(levels, 8 * groups)
    rest = (gradient[...] - high.astype(jnp.float32)).astype(jnp.bfloat16)
    level_grad = tn(level_hot, high) + tn(level_hot, rest)
    half_width = width // 2
    for c in range(groups):
        small_g[c // 2, c % 2, 0:8, :] = level_grad[c * 8 : (c + 1) * 8, :]
        start = (c % 2) * half_width
        for layer, source in enumerate((norm_zero, norm_one)):
            small_g[c // 2, c % 2, 8:9, layer * half_width : (layer + 1) * half_width] = source[
                c // 2 : c // 2 + 1, start : start + half_width
            ]
        small_g[c // 2, c % 2, 9:16, :] = jnp.zeros((7, width), jnp.float32)
    small_reduce = Reduce(small_g, small_near, small_come, small_sems, 0)

    gather = Gather(arrived, gather_sems, 0, 2)
    for half in range(2):
        for copy in row_copies[half]:
            copy.wait_recv()
        gather.start(half)
        if half == 0:
            small_reduce.middle()
            qkv_reduce.middle()
            mix.middle()

    own_rows = row_grad.shape[0]
    first_row = (group * members + member) * own_rows

    def collect(blocks, which):
        line = jnp.concatenate(
            [
                asked[r, group_at(step, back=True)]
                for r in blocks
                for half in which
                for step in halves()[half]
            ],
            axis=1,
        )
        line = line - first_row
        slots_here = line.shape[1]
        place = lax.broadcasted_iota(jnp.int32, (own_rows, slots_here), 0)
        hot = (line == place).astype(jnp.float32)
        source = jnp.concatenate(
            [
                arrived[pl.ds(r * count + half * half_count, half_count), :]
                for r in blocks
                for half in which
            ],
            axis=0,
        )
        part = nn(hot.astype(jnp.bfloat16), source)
        found = jnp.sum(hot, axis=1, keepdims=True)
        if blocks[0]:
            row_grad[...] += part
            hits[...] += found
        else:
            row_grad[...] = part
            hits[...] = found

    gather.wait_beside()
    collect([0, 1], [0, 1])
    gather.hand_on(0)

    small_in[member] = small_reduce.finish()
    small_share = Share(small_in, mate_sems, 0)
    out_share = RootShare(mix.finish(), out_shared, mate_sems, 1)
    qkv_shared[member] = qkv_reduce.finish().astype(qkv_shared.dtype)
    qkv_share = Share(qkv_shared, mate_sems, 2)
    gather.hand_on(1)
    small_share.hand_on()
    out_share.hand_on()
    gather.wait_handed(0)
    collect([2, 3], [0])
    gather.wait_handed(1)
    collect([2, 3], [1])

    qkv_share.hand_on()
    small_share.arrive()
    total = small_in[0]
    for m in range(1, members):
        total = total + small_in[m]
    small_sum[...] = total
    qkv_share.arrive()
    for copy in sum(row_copies, []):
        copy.wait_send()
    for each in (gather, small_share, out_share, qkv_share):
        each.finish()


def run_kernel(kernel, collective_id, name, inputs, outputs, scratch, flops=0, exps=0, left=()):
    moved = sum(math.prod(a.shape) * a.dtype.itemsize for a in inputs)
    return pl.pallas_call(
        kernel,
        out_shape=[jax.ShapeDtypeStruct(*o) for o in outputs],
        in_specs=[
            pl.BlockSpec(memory_space=pl.ANY if n in left else pltpu.VMEM)
            for n in range(len(inputs))
        ],
        out_specs=[pl.BlockSpec(memory_space=pltpu.VMEM)] * len(outputs),
        scratch_shapes=scratch,
        compiler_params=pltpu.CompilerParams(
            collective_id=collective_id, has_side_effects=True, vmem_limit_bytes=60 * 2**20
        ),
        cost_estimate=pl.CostEstimate(flops=flops, bytes_accessed=moved, transcendentals=exps),
        name=name,
    )(*inputs)


def run_layers(hidden, cotangent, scale, norms, qkv_zero, out_w, mine):
    rows, width = hidden.shape
    cell = 4 * rows
    groups, part, columns = qkv_zero.shape
    depth = groups // 2
    share = columns // 3
    per_device = share // HD
    units = mine[1].shape[2]
    f32, low = jnp.float32, jnp.bfloat16
    outputs = [
        ((rows, width), f32),
        ((rows, width), f32),
        ((4, width), f32),
        ((4, width), f32),
        ((depth, part, columns), low),
        ((part, width), low),
        ((part, units), f32),
        ((part, units), f32),
        ((part, units), f32),
        ((part, units), f32),
        ((4, part, columns), low),
        ((part, width), low),
    ]
    kept = [
        pltpu.VMEM((rows, width), f32),
        pltpu.VMEM((rows, 1), f32),
        pltpu.VMEM((rows, width), f32),
        pltpu.VMEM((rows, 1), f32),
        pltpu.VMEM((cell, width), low),
        pltpu.VMEM((3 * per_device, cell, HD), low),
        pltpu.VMEM((cell, share), low),
        pltpu.VMEM((4 * per_device, 1, rows), f32),
        pltpu.VMEM((cell, width), low),
        pltpu.VMEM((cell, units), low),
        pltpu.VMEM((cell, units), low),
    ]
    scratch = [
        pltpu.VMEM((groups, part, wide), low) for wide in (units, units, columns, units, units)
    ] + kept * 2
    scratch += [
        pltpu.VMEM((share, rows), f32),
        pltpu.VMEM((rows, width), f32),
        pltpu.VMEM((3, rows, width), low),
        pltpu.VMEM((3, rows, width), low),
        pltpu.VMEM((cell, width), low),
        pltpu.VMEM((cell, units), low),
        pltpu.VMEM((cell, width), low),
        pltpu.VMEM((per_device, cell, HD), low),
        pltpu.VMEM((per_device, cell, HD), f32),
        pltpu.VMEM((per_device, cell, HD), f32),
        pltpu.VMEM((per_device, cell, HD), low),
        pltpu.VMEM((cell, columns), low),
        pltpu.VMEM((depth, 2, part, units), low),
        pltpu.VMEM((depth, 2, part, units), low),
        pltpu.VMEM((depth, 2, part, columns), low),
        pltpu.VMEM((2, part, width), low),
    ]
    near, come = reduce_scratch(part, units, low)
    scratch += [near, near, come] * 2 + reduce_scratch(part, columns, low)
    scratch += [pltpu.VMEM((part, width), low), pltpu.VMEM((depth - 1, part, width), low)]
    scratch += dma_sems(8, 3 * PIECES) + dma_sems(8, 3 * PIECES) + dma_sems(5, 2 * depth - 1)
    scratch += dma_sems(2, depth) * 4 + dma_sems(2, 3)
    flops = 12 * cell * width * (4 * share + 2 * units) + 28 * cell * cell * share
    return run_kernel(
        layers_kernel,
        1,
        "layers",
        [hidden, cotangent, scale, *norms, qkv_zero, *out_w, *mine],
        outputs,
        scratch,
        flops,
        4 * cell * cell * per_device,
    )


def updated(weight, first, second, grad, rate, decay):
    first = beta_one * first + (1.0 - beta_one) * grad
    second = beta_two * second + (1.0 - beta_two) * grad * grad
    first_hat = first * (1.0 / (1.0 - beta_one**STEP))
    second_hat = second * (1.0 / (1.0 - beta_two**STEP))
    new = weight - rate * (first_hat / (jnp.sqrt(second_hat) + adam_eps) + decay * weight)
    return new, first, second


def update_kernel(*refs):
    refs = iter(refs)
    take = lambda count: [next(refs) for _ in range(count)]
    weight, moments, row_grad, hits = take(4)
    qkv_grads, out_grads, in_grads, back_grads = take(2), take(2), take(2), take(2)
    small_grad, level, level_moments, norm, norm_moments = take(5)
    given = take(8)
    new_weight, new_moments = take(2)
    new_level, new_level_moments, new_norm, new_norm_moments = take(4)
    made = take(8)
    held = take(8)
    load_sems, store_sems = take(2)
    step = pl.program_id(0) * pl.num_programs(1) + pl.program_id(1)
    last = pl.num_programs(0) * pl.num_programs(1) - 1
    layers = norm.shape[0]
    loads = [pltpu.make_async_copy(a, b, load_sems.at[n]) for n, (a, b) in enumerate(zip(given, held))]
    stores = [pltpu.make_async_copy(b, a, store_sems.at[n]) for n, (a, b) in enumerate(zip(made, held))]

    @pl.when(step == 0)
    def _():
        for load in loads:
            load.start()
        level_rows = level.shape[0]
        result = updated(
            level[...],
            level_moments[0],
            level_moments[1],
            small_grad[0:level_rows, :],
            rate_table,
            decay_rate,
        )
        new_level[...], new_level_moments[0], new_level_moments[1] = result
        columns = norm.shape[1]
        for n in range(layers):
            line = slice(n, n + 1)
            result = updated(
                norm[line, :],
                norm_moments[0, line, :],
                norm_moments[1, line, :],
                small_grad[level_rows : level_rows + 1, n * columns : (n + 1) * columns],
                rate_norm,
                0.0,
            )
            new_norm[line, :], new_norm_moments[0, line, :], new_norm_moments[1, line, :] = result

    def dense(which, place, grad, rate):
        value, kept = held[2 * which], held[2 * which + 1]
        result = updated(value[place], kept[(0, *place)], kept[(1, *place)], grad, rate, decay_rate)
        value[place], kept[(0, *place)], kept[(1, *place)] = result

    def qkv(n):
        members, _, columns = qkv_grads[n].shape
        share = columns // 3
        for c in range(3):
            grad = jnp.concatenate(
                [qkv_grads[n][m, :, c * share : (c + 1) * share] for m in range(members)], axis=1
            )
            dense(0, (n, c), grad.astype(jnp.float32), rate_dense)

    def plain(which, grads, rate):
        for n in range(layers):
            dense(which, (n,), grads[n][...].astype(jnp.float32), rate)

    jobs = [
        (2, 0, lambda: [qkv(n) for n in range(layers)]),
        (4, 1, lambda: plain(1, out_grads, rate_mixing)),
        (5, 2, lambda: plain(2, in_grads, rate_dense)),
        (6, 3, lambda: plain(3, back_grads, rate_dense)),
    ]
    for when, which, job in jobs:

        @pl.when(step == when)
        def _():
            for n in (2 * which, 2 * which + 1):
                loads[n].wait()
            job()
            for n in (2 * which, 2 * which + 1):
                stores[n].start()

    touched = hits[...] > 0
    old, old_first, old_second = weight[0], moments[0, 0], moments[1, 0]
    new, first, second = updated(old, old_first, old_second, row_grad[...], rate_table, decay_rate)
    new_weight[0] = jnp.where(touched, new, old)
    new_moments[0, 0] = jnp.where(touched, first, old_first)
    new_moments[1, 0] = jnp.where(touched, second, old_second)

    @pl.when(step == last)
    def _():
        for store in stores:
            store.wait()


def update_all(tables, table_moments, row_grad, hits, grads, small, small_state, state):
    count, own_rows, width = tables.shape
    step = own_rows // 3
    table_block = pl.BlockSpec((1, step, width), lambda i, t: (t, i, 0))
    moment_block = pl.BlockSpec((2, 1, step, width), lambda i, t: (0, t, i, 0))

    def whole(array):
        zeros = (0,) * array.ndim
        return pl.BlockSpec(array.shape, lambda i, t: zeros, pipeline_mode=pl.Buffered(1))

    left = pl.BlockSpec(memory_space=pl.ANY)
    kept = [*grads, small, *small_state]
    shape_of = lambda array: jax.ShapeDtypeStruct(array.shape, array.dtype)
    return pl.pallas_call(
        update_kernel,
        grid=(own_rows // step, count),
        in_specs=[
            table_block,
            moment_block,
            pl.BlockSpec((step, width), lambda i, t: (i, 0)),
            pl.BlockSpec((step, 1), lambda i, t: (i, 0)),
            *[whole(array) for array in kept],
            *[left] * len(state),
        ],
        out_specs=[
            table_block,
            moment_block,
            *[whole(array) for array in small_state],
            *[left] * len(state),
        ],
        out_shape=[shape_of(a) for a in (tables, table_moments, *small_state, *state)],
        scratch_shapes=[pltpu.VMEM(a.shape, a.dtype) for a in state]
        + [pltpu.SemaphoreType.DMA((len(state),))] * 2,
        compiler_params=pltpu.CompilerParams(vmem_limit_bytes=56 * 2**20),
        cost_estimate=pl.CostEstimate(
            flops=20 * tables.size, bytes_accessed=28 * tables.size, transcendentals=tables.size
        ),
        name="update",
    )(tables, table_moments, row_grad, hits, *kept, *state)


def fast_body(
    gene_ids,
    levels,
    study_of_cell,
    cotangent,
    tables,
    table_moments,
    level_table,
    level_moments,
    qkv_weight,
    qkv_moments,
    out_weight,
    out_moments,
    in_weight,
    in_moments,
    back_weight,
    back_moments,
    norm_params,
    norm_moments,
):
    low = jnp.bfloat16
    groups = lax.axis_size("dp")
    members = lax.axis_size("mp")
    member = lax.axis_index("mp")
    rows_here, width = cotangent.shape
    layers = qkv_weight.shape[0]
    local_cells = study_of_cell.shape[0]
    capacity = 2 * rows_here // groups
    own_rows = tables.shape[1]
    block_size = own_rows * members
    depth = qkv_weight.shape[2]
    share = width // members
    units = in_weight.shape[2]

    assert groups == 2 * members and layers == 2 and local_cells == 1
    f32 = jnp.float32
    qkv_mine = lax.dynamic_slice_in_dim(qkv_weight, member * share, share, axis=3).astype(low)
    qkv_mine = qkv_mine.transpose(0, 2, 1, 3).reshape(layers, depth, 3 * share)
    out_mine = out_weight.astype(low)
    in_mine = in_weight.astype(low)
    back_mine = back_weight.astype(low).transpose(0, 2, 1)
    level_rows = level_table.shape[0]
    study_onehot = (study_of_cell[:, None] == jnp.arange(width)[None, :]).astype(f32)
    small = jnp.concatenate(
        [
            level_table.astype(low).astype(f32),
            norm_params.reshape(1, width),
            study_onehot,
            jnp.zeros((16 - level_rows - 2, width), f32),
        ]
    )
    row_owner = gene_ids // block_size
    slot_index = slots_of(row_owner)
    sent_ids = slotted_ids(gene_ids, row_owner, slot_index, groups, capacity)
    codes = (row_owner * capacity + slot_index)[None, :]
    level_line = levels[None, :]

    slots = groups * capacity
    copies = 2 * (groups // 2) - 1
    dma = pltpu.SemaphoreType.DMA
    hidden, asked, scale, *more = run_kernel(
        start_kernel,
        5,
        "start",
        [
            sent_ids[:, None, :],
            codes,
            level_line,
            tables,
            small,
            qkv_mine,
            out_mine,
        ],
        [
            ((rows_here, width), f32),
            ((members, groups, 1, capacity), jnp.int32),
            ((1, 1), f32),
            ((4, width), f32),
            ((4, width), f32),
            ((groups, depth, 3 * share), low),
            ((2, depth, width), low),
            ((2, depth, width), low),
        ],
        [
            pltpu.VMEM((groups, 16, width), f32),
            pltpu.VMEM((groups, capacity, width), low),
            pltpu.VMEM((groups, capacity, width), low),
            pltpu.VMEM((3, slots, width), low),
            pltpu.VMEM((3, slots, width), low),
            pltpu.VMEM((own_rows, width), low),
            pltpu.VMEM((2, tables.shape[0], own_rows // 3, width), f32),
        ]
        + dma_sems(1, 3 * 2)
        + [dma((1, copies))] * 2
        + [dma((1, copies))] * 2
        + [dma((2, groups // 2 + 1))] * 2
        + [dma((groups - 1,))] * 2
        + [dma((3,))] * 2
        + [dma((groups,))] * 2
        + [dma((2,))],
        left=(3,),
    )
    norms, qkv_w, out_w = more[0:2], more[2], more[3:5]
    hidden, gradient, norm_zero, norm_one, qkv_pair, out_pair, *more = run_layers(
        hidden,
        cotangent,
        scale,
        norms,
        qkv_w,
        out_w,
        [qkv_mine, in_mine, back_mine],
    )
    in_zero, in_one, back_zero, back_one, qkv_one, out_one = more
    row_grad, hits, qkv_zero, out_zero, small_sum = run_kernel(
        end_kernel,
        6,
        "finish",
        [
            gradient,
            codes,
            level_line,
            asked,
            qkv_pair,
            out_pair,
            norm_zero,
            norm_one,
        ],
        [
            ((own_rows, width), f32),
            ((own_rows, 1), f32),
            ((members, depth, 3 * share), low),
            ((depth, width), low),
            ((16, width), f32),
        ],
        [
            pltpu.VMEM((groups, capacity, width), low),
            pltpu.VMEM((4 * slots, width), low),
            pltpu.VMEM((groups // 2, 2, 16, width), f32),
            pltpu.VMEM((members, 16, width), f32),
        ]
        + reduce_scratch(depth, 3 * share, low)[1:]
        + reduce_scratch(16, width, f32)
        + [pltpu.VMEM((groups // 2 - 1, depth, width), low)]
        + dma_sems(1, groups // 2) * 3
        + dma_sems(1, 3 * 2)
        + [dma((groups,))] * 2
        + dma_sems(3, 3),
    )

    table_new, table_state, level_new, level_state, norm_new, norm_state, *more = update_all(
        tables,
        table_moments,
        row_grad,
        hits,
        [qkv_zero, qkv_one, out_zero, out_one, in_zero, in_one, back_zero, back_one],
        small_sum,
        [level_table, level_moments, norm_params, norm_moments],
        [
            qkv_weight,
            qkv_moments,
            out_weight,
            out_moments,
            in_weight,
            in_moments,
            back_weight.transpose(0, 2, 1),
            back_moments.transpose(0, 1, 3, 2),
        ],
    )
    qkv_new, qkv_state, out_new, out_state, in_new, in_state, back_new, back_state = more
    back_new, back_state = back_new.transpose(0, 2, 1), back_state.transpose(0, 1, 3, 2)
    return (
        hidden,
        table_new,
        table_state,
        level_new,
        level_state,
        qkv_new,
        qkv_state,
        out_new,
        out_state,
        in_new,
        in_state,
        back_new,
        back_state,
        norm_new,
        norm_state,
    )


def solution(mesh):
    return jax.shard_map(
        fast_body if (mesh.shape["dp"], mesh.shape["mp"]) == (8, 4) else general_body,
        mesh=mesh,
        in_specs=(
            P(("dp", "mp")),
            P(("dp", "mp")),
            P("dp"),
            P(("dp", "mp"), None),
            P(None, ("dp", "mp"), None),
            P(None, None, ("dp", "mp"), None),
            P("dp", None),
            P(None, "dp", None),
            P(None, None, "dp", None),
            P(None, None, None, "dp", None),
            P(None, "dp", None),
            P(None, None, "dp", None),
            P(None, "dp", "mp"),
            P(None, None, "dp", "mp"),
            P(None, "mp", "dp"),
            P(None, None, "mp", "dp"),
            P(None, "dp"),
            P(None, None, "dp"),
        ),
        out_specs=(
            P(("dp", "mp"), None),
            P(None, ("dp", "mp"), None),
            P(None, None, ("dp", "mp"), None),
            P("dp", None),
            P(None, "dp", None),
            P(None, None, "dp", None),
            P(None, None, None, "dp", None),
            P(None, "dp", None),
            P(None, None, "dp", None),
            P(None, "dp", "mp"),
            P(None, None, "dp", "mp"),
            P(None, "mp", "dp"),
            P(None, None, "mp", "dp"),
            P(None, "dp"),
            P(None, None, "dp"),
        ),
        check_vma=False,
    )
```

```python
import math
from functools import partial

import jax
import jax.numpy as jnp
from jax import lax
from jax.experimental import pallas as pl
from jax.experimental.pallas import tpu as pltpu
from jax.sharding import PartitionSpec as P

HEADS = 12
HD = 64
STUDY_TOTAL = 16
STEP = 10


largest_value = lax.Precision.HIGHEST
beta_one = 0.9
beta_two = 0.999
adam_eps = 1e-08
norm_eps = 1e-05
rate_dense = 0.08
rate_mixing = 0.3
rate_table = 0.6
rate_norm = 0.4
decay_rate = 0.01


def spread_rows(rows):
    return lax.all_gather(rows, "mp", axis=0, tiled=True)


def summed_rows(term, count):
    return lax.psum_scatter(
        term(jnp.int32(0), count * lax.axis_size("mp")).astype(jnp.bfloat16),
        "mp",
        scatter_dimension=0,
        tiled=True,
    ).astype(jnp.float32)


def norm_forward(rows, gain, bias):
    centered = rows - jnp.mean(rows, axis=-1, keepdims=True)
    inverse = lax.rsqrt(jnp.mean(centered * centered, axis=-1, keepdims=True) + norm_eps)
    normal = centered * inverse
    return (normal * gain + bias, normal, inverse)


def norm_backward(gradient, normal, inverse, gain):
    scaled = gradient * gain
    inner_part = (
        scaled
        - jnp.mean(scaled, axis=-1, keepdims=True)
        - normal * jnp.mean(scaled * normal, axis=-1, keepdims=True)
    )
    return (inner_part * inverse, jnp.sum(gradient * normal, axis=0), jnp.sum(gradient, axis=0))


def gelu_grad(inner, gradient):
    return jax.vjp(partial(jax.nn.gelu, approximate=False), inner)[1](gradient)[0]


def head_major(rows):
    return rows.reshape(rows.shape[0], HEADS, HD).transpose(1, 0, 2)


def row_major(heads):
    return heads.transpose(1, 0, 2).reshape(heads.shape[1], HEADS * HD)


def attend_forward(query, keys, values):
    scale = HD ** (-0.5)

    def one_head(pieces):
        head_query, head_keys, head_values = pieces
        scores = (
            jnp.einsum("qd,kd->qk", head_query, head_keys, preferred_element_type=jnp.float32)
            * scale
        )
        peak = jnp.max(scores, axis=-1, keepdims=True)
        raised = jnp.exp(scores - peak)
        total = jnp.sum(raised, axis=-1, keepdims=True)
        probs = (raised / total).astype(jnp.bfloat16)
        mixed = jnp.dot(probs, head_values, preferred_element_type=jnp.float32).astype(jnp.bfloat16)
        return (mixed, (peak + jnp.log(total))[:, 0])

    mixed, log_total = lax.map(one_head, (head_major(query), head_major(keys), head_major(values)))
    return (row_major(mixed), log_total)


def attend_backward(query, keys, values, mixed_grad, log_total):
    scale = HD ** (-0.5)

    def one_head(pieces):
        head_query, head_keys, head_values, head_grad, head_total = pieces
        scores = (
            jnp.einsum("qd,kd->qk", head_query, head_keys, preferred_element_type=jnp.float32)
            * scale
        )
        probs = jnp.exp(scores - head_total[:, None])
        product = jnp.einsum(
            "qd,kd->qk", head_grad, head_values, preferred_element_type=jnp.float32
        )
        center = jnp.sum(probs * product, axis=-1, keepdims=True)
        score_grad = (probs * (product - center)).astype(jnp.bfloat16)
        query_grad = (
            jnp.dot(score_grad, head_keys, preferred_element_type=jnp.float32) * scale
        ).astype(jnp.bfloat16)
        key_grad = (
            jnp.einsum("qk,qd->kd", score_grad, head_query, preferred_element_type=jnp.float32)
            * scale
        )
        value_grad = jnp.einsum(
            "qk,qd->kd", probs.astype(jnp.bfloat16), head_grad, preferred_element_type=jnp.float32
        )
        return (query_grad, key_grad, value_grad)

    query_grad, key_grad, value_grad = lax.map(
        one_head,
        (
            head_major(query),
            head_major(keys),
            head_major(values),
            head_major(mixed_grad),
            log_total,
        ),
    )
    return (row_major(query_grad), jnp.stack([row_major(key_grad), row_major(value_grad)], axis=1))


def slots_of(row_owner):
    place = jnp.arange(row_owner.shape[0])
    earlier = (row_owner[:, None] == row_owner[None, :]) & (place[None, :] < place[:, None])
    return jnp.sum(earlier.astype(jnp.int32), axis=1)


def slotted_ids(gene_ids, row_owner, slot_index, cell_groups, capacity):
    code = row_owner * capacity + slot_index
    hot = code[None, :] == jnp.arange(cell_groups * capacity)[:, None]
    found = jnp.sum(jnp.where(hot, gene_ids[None, :] + 1, 0), axis=1) - 1
    return found.reshape(cell_groups, capacity)


def adam_step(weight, moments, gradient, rate, decay):
    first = beta_one * moments[0] + (1.0 - beta_one) * gradient
    second = beta_two * moments[1] + (1.0 - beta_two) * gradient * gradient
    first_hat = first / (1.0 - beta_one**STEP)
    second_hat = second / (1.0 - beta_two**STEP)
    new_weight = weight - rate * (first_hat / (jnp.sqrt(second_hat) + adam_eps) + decay * weight)
    return (new_weight, jnp.stack([first, second]))


def general_body(
    gene_ids,
    levels,
    study_of_cell,
    cotangent,
    tables,
    table_moments,
    level_table,
    level_moments,
    qkv_weight,
    qkv_moments,
    out_weight,
    out_moments,
    in_weight,
    in_moments,
    back_weight,
    back_moments,
    norm_params,
    norm_moments,
):
    cell_groups = lax.axis_size("dp")
    rows_here = cotangent.shape[0]
    model_width = cotangent.shape[1]
    layers = qkv_weight.shape[0]
    local_cells = study_of_cell.shape[0]
    capacity = 2 * rows_here // cell_groups
    own_rows = tables.shape[1]
    block_size = own_rows * lax.axis_size("mp")
    qkv_full, out_full, in_part, back_part, level_full = (
        lax.all_gather(qkv_weight.astype(jnp.bfloat16), "dp", axis=2, tiled=True),
        lax.all_gather(out_weight.astype(jnp.bfloat16), "dp", axis=1, tiled=True),
        lax.all_gather(in_weight.astype(jnp.bfloat16), "dp", axis=1, tiled=True),
        lax.all_gather(back_weight.astype(jnp.bfloat16), "dp", axis=2, tiled=True),
        lax.all_gather(level_table.astype(jnp.bfloat16), "dp", axis=0, tiled=True),
    )
    study_onehot = (study_of_cell[:, None] == jnp.arange(STUDY_TOTAL)[None, :]).astype(jnp.float32)
    norm_full, study_all = (
        lax.all_gather(norm_params, "dp", axis=1, tiled=True),
        lax.all_gather(study_onehot, "dp", axis=0, tiled=True),
    )
    cells_per_study = jnp.sum(study_all, axis=0)
    cell_balance_weight = (
        cell_groups
        * local_cells
        / (STUDY_TOTAL * jnp.dot(study_onehot, cells_per_study, precision=largest_value))
    )
    out_grad = cotangent * cell_balance_weight[0]
    summed_tables = jnp.sum(tables, axis=0).astype(jnp.bfloat16)
    table_rows = lax.all_gather(summed_tables, "mp", axis=0, tiled=True)
    row_owner = gene_ids // block_size
    slot_index = slots_of(row_owner)
    sent_ids = slotted_ids(gene_ids, row_owner, slot_index, cell_groups, capacity)
    asked_ids = lax.all_to_all(sent_ids, "dp", split_axis=0, concat_axis=0, tiled=True)
    present = asked_ids >= 0
    safe_row = jnp.where(present, asked_ids - lax.axis_index("dp") * block_size, 0)
    found_rows = jnp.where(present[..., None], jnp.take(table_rows, safe_row, axis=0), 0)
    returned = lax.all_to_all(found_rows, "dp", split_axis=0, concat_axis=0, tiled=True)
    gene_part = returned[row_owner, slot_index].astype(jnp.float32)
    level_hot = (levels[:, None] == jnp.arange(level_full.shape[0])[None, :]).astype(jnp.bfloat16)
    hidden = gene_part + jnp.dot(level_hot, level_full, preferred_element_type=jnp.float32)
    kept = []
    for layer in range(layers):
        norm_row = norm_full[layer]
        tokens_low = hidden.astype(jnp.bfloat16)
        projected = jnp.einsum(
            "td,cdh->tch", tokens_low, qkv_full[layer], preferred_element_type=jnp.float32
        ).astype(jnp.bfloat16)
        query = projected[:, 0]
        cell_rows = spread_rows(projected[:, 1:])
        keys, values = (cell_rows[:, 0], cell_rows[:, 1])
        mixed, log_total = attend_forward(query, keys, values)
        attention = jnp.dot(mixed, out_full[layer], preferred_element_type=jnp.float32)
        first, first_normal, first_inverse = norm_forward(
            hidden + attention, norm_row[:model_width], norm_row[model_width : 2 * model_width]
        )
        first_low = first.astype(jnp.bfloat16)
        in_layer, back_layer = (in_part[layer], back_part[layer])
        first_spread = spread_rows(first_low)
        inner = jnp.dot(first_spread, in_layer, preferred_element_type=jnp.float32)
        active = jax.nn.gelu(inner, approximate=False).astype(jnp.bfloat16)

        def feed_term(start, count):
            return jnp.dot(active, back_layer, preferred_element_type=jnp.float32)

        feed = summed_rows(feed_term, rows_here)
        second, second_normal, second_inverse = norm_forward(
            first + feed, norm_row[2 * model_width : 3 * model_width], norm_row[3 * model_width :]
        )
        kept.append(
            (
                tokens_low,
                query,
                keys,
                values,
                mixed,
                log_total,
                first_normal,
                first_inverse,
                first_spread,
                inner,
                active,
                in_layer,
                back_layer,
                second_normal,
                second_inverse,
            )
        )
        hidden = second
    gradient = out_grad
    qkv_grads = [None] * layers
    out_grads = [None] * layers
    in_grads = [None] * layers
    back_grads = [None] * layers
    norm_grads = [None] * layers
    for layer in reversed(range(layers)):
        (
            tokens_low,
            query,
            keys,
            values,
            mixed,
            log_total,
            first_normal,
            first_inverse,
            first_spread,
            inner,
            active,
            in_layer,
            back_layer,
            second_normal,
            second_inverse,
        ) = kept[layer]
        norm_row = norm_full[layer]
        grad_second, gain_two, bias_two = norm_backward(
            gradient, second_normal, second_inverse, norm_row[2 * model_width : 3 * model_width]
        )
        feed_low = grad_second.astype(jnp.bfloat16)
        feed_spread = spread_rows(feed_low)
        back_grads[layer] = jnp.einsum(
            "tf,td->fd", active, feed_spread, preferred_element_type=jnp.float32
        )
        active_grad = jnp.einsum(
            "td,fd->tf", feed_spread, back_layer, preferred_element_type=jnp.float32
        )
        inner_grad = gelu_grad(inner, active_grad).astype(jnp.bfloat16)
        in_grads[layer] = jnp.einsum(
            "td,tf->df", first_spread, inner_grad, preferred_element_type=jnp.float32
        )

        def first_term(start, count):
            return jnp.einsum("tf,df->td", inner_grad, in_layer, preferred_element_type=jnp.float32)

        first_grad = summed_rows(first_term, rows_here)
        grad_first, gain_one, bias_one = norm_backward(
            grad_second + first_grad, first_normal, first_inverse, norm_row[:model_width]
        )
        norm_grads[layer] = jnp.concatenate([gain_one, bias_one, gain_two, bias_two])
        attention_low = grad_first.astype(jnp.bfloat16)
        out_grads[layer] = jnp.einsum(
            "th,td->hd", mixed, attention_low, preferred_element_type=jnp.float32
        )
        mixed_grad = jnp.einsum(
            "td,hd->th", attention_low, out_full[layer], preferred_element_type=jnp.float32
        ).astype(jnp.bfloat16)
        query_grad, pair_partial = attend_backward(query, keys, values, mixed_grad, log_total)
        pair_grad = lax.psum_scatter(
            pair_partial.astype(jnp.bfloat16), "mp", scatter_dimension=0, tiled=True
        )
        stacked = jnp.concatenate([query_grad[:, None, :], pair_grad], axis=1)
        qkv_grads[layer] = jnp.einsum(
            "td,tch->cdh", tokens_low, stacked, preferred_element_type=jnp.float32
        )
        gradient = grad_first + jnp.einsum(
            "tch,cdh->td", stacked, qkv_full[layer], preferred_element_type=jnp.float32
        )
    level_grad = jnp.dot(level_hot.astype(jnp.float32).T, gradient, precision=largest_value)
    grad_slots = (
        jnp.zeros((cell_groups, capacity, model_width), jnp.float32)
        .at[row_owner, slot_index]
        .set(gradient)
    )
    arrived = lax.all_to_all(
        grad_slots.astype(jnp.bfloat16), "dp", split_axis=0, concat_axis=0, tiled=True
    ).astype(grad_slots.dtype)
    arrived = jnp.where(present[..., None], arrived, 0.0)
    flat_rows = safe_row.reshape(-1)
    block_grad = jax.ops.segment_sum(
        arrived.reshape(-1, model_width), flat_rows, num_segments=block_size
    )
    block_hits = jax.ops.segment_sum(
        present.reshape(-1).astype(jnp.float32), flat_rows, num_segments=block_size
    )
    row_grad, hits = (
        lax.psum_scatter(
            block_grad.astype(jnp.bfloat16), "mp", scatter_dimension=0, tiled=True
        ).astype(jnp.float32),
        lax.psum_scatter(
            block_hits.astype(jnp.bfloat16), "mp", scatter_dimension=0, tiled=True
        ).astype(jnp.float32),
    )
    qkv_sum, out_sum, in_sum, back_sum, level_sum, norm_sum = (
        lax.psum_scatter(
            jnp.stack(qkv_grads).astype(jnp.bfloat16), "dp", scatter_dimension=2, tiled=True
        ).astype(jnp.float32),
        lax.psum_scatter(
            jnp.stack(out_grads).astype(jnp.bfloat16), "dp", scatter_dimension=1, tiled=True
        ).astype(jnp.float32),
        lax.psum_scatter(
            jnp.stack(in_grads).astype(jnp.bfloat16), "dp", scatter_dimension=1, tiled=True
        ).astype(jnp.float32),
        lax.psum_scatter(
            jnp.stack(back_grads).astype(jnp.bfloat16), "dp", scatter_dimension=2, tiled=True
        ).astype(jnp.float32),
        lax.psum_scatter(
            level_grad.astype(jnp.bfloat16), "dp", scatter_dimension=0, tiled=True
        ).astype(jnp.float32),
        lax.psum_scatter(
            jnp.stack(norm_grads).astype(jnp.bfloat16), "dp", scatter_dimension=1, tiled=True
        ).astype(jnp.float32),
    )
    qkv_sum, out_sum, level_sum, norm_sum = (
        lax.psum(qkv_sum.astype(jnp.bfloat16), "mp").astype(jnp.float32),
        lax.psum(out_sum.astype(jnp.bfloat16), "mp").astype(jnp.float32),
        lax.psum(level_sum.astype(jnp.bfloat16), "mp").astype(jnp.float32),
        lax.psum(norm_sum.astype(jnp.bfloat16), "mp").astype(jnp.float32),
    )
    touched = (hits > 0)[None, :, None]
    table_grad = jnp.broadcast_to(row_grad[None], tables.shape)
    table_new, table_state = adam_step(tables, table_moments, table_grad, rate_table, decay_rate)
    table_new = jnp.where(touched, table_new, tables)
    table_state = jnp.where(touched[None], table_state, table_moments)
    level_new, level_state = adam_step(
        level_table, level_moments, level_sum, rate_table, decay_rate
    )
    qkv_new, qkv_state = adam_step(qkv_weight, qkv_moments, qkv_sum, rate_dense, decay_rate)
    out_new, out_state = adam_step(out_weight, out_moments, out_sum, rate_mixing, decay_rate)
    in_new, in_state = adam_step(in_weight, in_moments, in_sum, rate_dense, decay_rate)
    back_new, back_state = adam_step(back_weight, back_moments, back_sum, rate_dense, decay_rate)
    norm_new, norm_state = adam_step(norm_params, norm_moments, norm_sum, rate_norm, 0.0)
    return (
        hidden,
        table_new,
        table_state,
        level_new,
        level_state,
        qkv_new,
        qkv_state,
        out_new,
        out_state,
        in_new,
        in_state,
        back_new,
        back_state,
        norm_new,
        norm_state,
    )


MESH = pl.DeviceIdType.MESH
SIB, FACE = 0, 1
TILE = 128


def nn(a, b):
    return lax.dot_general(a, b, (((1,), (0,)), ((), ())), preferred_element_type=jnp.float32)


def nt(a, b):
    return lax.dot_general(a, b, (((1,), (1,)), ((), ())), preferred_element_type=jnp.float32)


def tn(a, b):
    return lax.dot_general(a, b, (((0,), (0,)), ((), ())), preferred_element_type=jnp.float32)


def near_devices():
    group, member = lax.axis_index("dp"), lax.axis_index("mp")
    core = member % 2
    return (group, member + 1 - 2 * core), (group, (member + 2) % 4)


def greet(peers):
    barrier = pltpu.get_barrier_semaphore()
    for peer in peers:
        pl.semaphore_signal(barrier, inc=1, device_id=peer, device_id_type=MESH)
    pl.semaphore_wait(barrier, len(peers))


def send(source, target, sems, index, peer):
    copy = pltpu.make_async_remote_copy(
        src_ref=source,
        dst_ref=target,
        send_sem=sems[0].at[index],
        recv_sem=sems[1].at[index],
        device_id=peer,
        device_id_type=MESH,
    )
    copy.start()
    return copy


PIECES = 2


def columns_of(group):
    return group // 2, group % 2


def group_peers():
    group, member = lax.axis_index("dp"), lax.axis_index("mp")
    count = lax.axis_size("dp")
    return [((group + k) % count, member) for k in range(1, count)]


def mates():
    group, member = lax.axis_index("dp"), lax.axis_index("mp")
    count = lax.axis_size("mp")
    return [(group, (member + k) % count) for k in range(1, count)]


class Spread:
    def __init__(self, mine, whole, sems, part):
        group, member = lax.axis_index("dp"), lax.axis_index("mp")
        depth = lax.axis_size("dp") // 2
        z, x = columns_of(group)
        self.beside = (group + 1 - 2 * x, member)
        self.whole, self.sems, self.part, self.depth = whole, sems, part, depth
        self.came = [((z + depth - k) % depth) * 2 + x for k in range(1, depth)]
        self.along = [
            send(mine, whole.at[group], sems, (part, k - 1), (((z + k) % depth) * 2 + x, member))
            for k in range(1, depth)
        ]
        self.across = [send(mine, whole.at[group], sems, (part, depth - 1), self.beside)]
        whole[group] = mine[...]

    def hand_on(self):
        for k in range(1, self.depth):
            self.along[k - 1].wait_recv()
            block = self.whole.at[self.came[k - 1]]
            self.across.append(
                send(block, block, self.sems, (self.part, self.depth - 1 + k), self.beside)
            )

    def arrive(self):
        for copy in self.across:
            copy.wait_recv()

    def finish(self):
        for copy in [*self.along, *self.across]:
            copy.wait_send()


class Reduce:
    def __init__(self, source, near, come, sems, line):
        group, self.member = lax.axis_index("dp"), lax.axis_index("mp")
        self.depth = lax.axis_size("dp") // 2
        self.z, self.x = columns_of(group)
        self.source, self.near, self.come = source, near, come
        self.sems, self.line, self.copies = sems, line, []
        if source is not None:
            beside = (group + 1 - 2 * self.x, self.member)
            self.first = send(source.at[:, 1 - self.x], near, sems, (line, 0), beside)

    def pair(self, z):
        term = self.near[z].astype(jnp.float32)
        return term if self.source is None else term + self.source[z, self.x].astype(jnp.float32)

    def add_up(self):
        self.first.wait_recv()
        for z in range(self.depth):
            self.near[z] = self.pair(z).astype(self.near.dtype)
        self.first.wait_send()

    def middle(self):
        if self.source is not None:
            self.first.wait_recv()
        for k in range(1, self.depth):
            z = (self.z + k) % self.depth
            if self.source is not None:
                self.near[z] = self.pair(z).astype(self.near.dtype)
            self.copies.append(
                send(
                    self.near.at[z],
                    self.come.at[k - 1],
                    self.sems,
                    (self.line, k),
                    (z * 2 + self.x, self.member),
                )
            )

    def finish(self):
        term = self.pair(self.z)
        for k, copy in enumerate(self.copies):
            copy.wait_recv()
            term = term + self.come[k].astype(jnp.float32)
        for copy in self.copies:
            copy.wait_send()
        if self.source is not None:
            self.first.wait_send()
        return term


def reduce_scratch(rows, columns, dtype):
    depth = lax.axis_size("dp") // 2
    return [pltpu.VMEM((depth, rows, columns), dtype), pltpu.VMEM((depth - 1, rows, columns), dtype)]


def dma_sems(*shape):
    return [pltpu.SemaphoreType.DMA(shape)] * 2


class MixReduce:
    def __init__(self, source, near, come, sems, line):
        group, self.member = lax.axis_index("dp"), lax.axis_index("mp")
        self.depth = lax.axis_size("dp") // 2
        self.z, self.x = columns_of(group)
        self.sems, self.line = sems, line
        self.source, self.near, self.come = source, near, come
        if source is not None:
            beside = (group + 1 - 2 * self.x, self.member)
            self.first = send(source.at[1 - self.x], near, sems, (line, 0), beside)

    def copy(self, slot, there):
        return pltpu.make_async_remote_copy(
            src_ref=self.near,
            dst_ref=self.come.at[slot],
            send_sem=self.sems[0].at[self.line, 1 + slot],
            recv_sem=self.sems[1].at[self.line, 1 + slot],
            device_id=(there, self.member),
            device_id_type=MESH,
        )

    def to_root(self):
        slot = (self.member + 2 * self.depth - self.z - 1) % self.depth
        return self.copy(slot, self.member * 2 + self.x)

    def add_up(self):
        self.first.wait_recv()
        term = self.source[self.x].astype(jnp.float32) + self.near[...].astype(jnp.float32)
        self.near[...] = term.astype(self.near.dtype)
        self.first.wait_send()

    def middle(self):
        if self.source is not None:
            self.add_up()

        @pl.when(self.z != self.member)
        def _():
            self.to_root().start()

    def finish(self):
        @pl.when(self.z == self.member)
        def _():
            for slot in range(self.depth - 1):
                self.copy(slot, (self.member * 2 + self.x + 2) % (2 * self.depth)).wait_recv()

        @pl.when(self.z != self.member)
        def _():
            self.to_root().wait_send()

        term = self.near[...].astype(jnp.float32)
        for slot in range(self.depth - 1):
            term = term + self.come[slot].astype(jnp.float32)
        return term


class Gather:
    def __init__(self, buf, sems, line, pieces=PIECES):
        self.buf, self.sems, self.line, self.pieces = buf, sems, line, pieces
        self.sib, self.face = near_devices()
        self.rows = buf.shape[0] // 4
        self.size = self.rows // pieces
        self.across, self.beside, self.handed = [], [], []

    def piece(self, b, i):
        return self.buf.at[pl.ds(b * self.rows + i * self.size, self.size)]

    def start(self, i):
        mine = self.piece(0, i)
        self.across.append(send(mine, self.piece(2, i), self.sems, (self.line, i), self.face))
        self.beside.append(
            send(mine, self.piece(1, i), self.sems, (self.line, self.pieces + i), self.sib)
        )

    def wait_beside(self):
        for copy in self.beside:
            copy.wait_recv()

    def hand_on(self, i):
        self.across[i].wait_recv()
        self.handed.append(
            send(
                self.piece(2, i),
                self.piece(3, i),
                self.sems,
                (self.line, 2 * self.pieces + i),
                self.sib,
            )
        )

    def wait_handed(self, i):
        self.handed[i].wait_recv()

    def finish(self):
        for copy in [*self.across, *self.beside, *self.handed]:
            copy.wait_send()


class Share:
    def __init__(self, buf, sems, line):
        self.buf, self.sems, self.line = buf, sems, line
        member = lax.axis_index("mp")
        self.sib, self.face = near_devices()
        self.copies = [
            send(buf.at[member], buf.at[member], sems, (line, k), peer)
            for k, peer in enumerate((self.face, self.sib))
        ]

    def hand_on(self):
        self.copies[0].wait_recv()
        block = self.buf.at[self.face[1]]
        self.copies.append(send(block, block, self.sems, (self.line, 2), self.sib))

    def arrive(self):
        for copy in self.copies[1:]:
            copy.wait_recv()

    def finish(self):
        for copy in self.copies:
            copy.wait_send()


class RootShare:
    def __init__(self, value, buf, sems, line):
        self.buf, self.sems, self.line = buf, sems, line
        self.member = lax.axis_index("mp")
        self.root, _ = columns_of(lax.axis_index("dp"))
        self.sib, self.face = near_devices()

        @pl.when(self.member == self.root)
        def _():
            buf[...] = value.astype(buf.dtype)
            for k, peer in enumerate((self.face, self.sib)):
                self.copy(k, peer).start()

    def copy(self, k, peer):
        return pltpu.make_async_remote_copy(
            src_ref=self.buf,
            dst_ref=self.buf,
            send_sem=self.sems[0].at[self.line, k],
            recv_sem=self.sems[1].at[self.line, 0],
            device_id=peer,
            device_id_type=MESH,
        )

    def hand_on(self):
        @pl.when(self.member != self.root)
        def _():
            self.copy(0, self.sib).wait_recv()

        @pl.when(self.face[1] == self.root)
        def _():
            self.copy(2, self.sib).start()

    def finish(self):
        @pl.when(self.member == self.root)
        def _():
            for k, peer in enumerate((self.face, self.sib)):
                self.copy(k, peer).wait_send()

        @pl.when(self.face[1] == self.root)
        def _():
            self.copy(2, self.sib).wait_send()


class Total:
    def __init__(self, out, into, sems, line, pieces=PIECES):
        self.out, self.into, self.sems, self.line, self.pieces = out, into, sems, line, pieces
        self.sib, self.face = near_devices()
        self.size = out.shape[1] // pieces
        self.far, self.facing, self.beside = [], [], []

    def give(self, b, i, term, peer):
        piece = pl.ds(i * self.size, self.size)
        self.out[b, piece, :] = term.astype(jnp.bfloat16)
        return send(
            self.out.at[b, piece],
            self.into.at[b, piece],
            self.sems,
            (self.line, b * self.pieces + i),
            peer,
        )

    def came(self, b, i):
        return self.into[b, pl.ds(i * self.size, self.size), :].astype(jnp.float32)

    def part(self, term, i):
        return term[i * self.size : (i + 1) * self.size]

    def give_far(self, i, term):
        self.far.append(self.give(0, i, term, self.sib))

    def give_facing(self, i, term):
        self.far[i].wait_recv()
        self.facing.append(self.give(1, i, term + self.came(0, i), self.face))

    def give_beside(self, i, term):
        self.beside.append(self.give(2, i, term, self.sib))

    def take(self, i, term):
        self.beside[i].wait_recv()
        self.facing[i].wait_recv()
        return term + self.came(2, i) + self.came(1, i)

    def finish(self):
        for copy in [*self.far, *self.facing, *self.beside]:
            copy.wait_send()


def gelu_pair(x):
    t = 1.0 / (1.0 + (0.3275911 * 0.7071067811865476) * jnp.abs(x))
    raised = jnp.exp(-0.5 * x * x)
    series = t * (
        0.254829592
        + t * (-0.284496736 + t * (1.421413741 + t * (-1.453152027 + t * 1.061405429)))
    )
    upper = 0.5 * series * raised
    share = jnp.where(x >= 0, 1.0 - upper, upper)
    return x * share, share + x * raised * 0.3989422804014327


def column(ref):
    line = ref[...].astype(jnp.float32)
    return jnp.broadcast_to(line, (8, line.shape[1])).T[:, 0:1]


def hot_places(ref, count):
    place = lax.broadcasted_iota(jnp.int32, (ref.shape[1], count), 1)
    return (column(ref) == place.astype(jnp.float32)).astype(jnp.bfloat16)


def rows_joined(ref):
    blocks = ref[...]
    return blocks.reshape(blocks.shape[0] * blocks.shape[1], blocks.shape[2])


def around(peers):
    group, member = lax.axis_index("dp"), lax.axis_index("mp")
    depth = lax.axis_size("dp") // 2
    z, x = columns_of(group)
    along = [(((z + k) % depth) * 2 + x, member) for k in range(1, depth)]
    return [*peers, *along, (group + 1 - 2 * x, member)]


def layers_kernel(*refs):
    refs = iter(refs)
    take = lambda count: [next(refs) for _ in range(count)]
    hidden, cotangent, scale = take(3)
    norms = take(2)
    qkv_zero, out_zero, out_one = take(3)
    qkv_mine, in_mine, back_mine = take(3)
    mine = [in_mine.at[0], back_mine.at[0], qkv_mine.at[1], in_mine.at[1], back_mine.at[1]]
    encoded, gradient_out = take(2)
    norm_grads = take(2)
    qkv_pair, out_pair = take(2)
    in_sums, back_sums = take(2), take(2)
    qkv_shared, out_shared = take(2)
    in_zero, back_zero, qkv_one, in_one, back_one = whole = take(5)
    saved = [take(11), take(11)]
    mixed_t, held, out, into = take(4)
    feeds, inner, lows, mixed_grad, key_grad, value_grad, query_grad, head_grads = take(8)
    in_g, back_g, qkv_g, out_g = take(4)
    in_near, in_come, back_near, back_come = take(2), take(1), take(2), take(1)
    qkv_parts, out_parts = take(2), take(2)
    gather_sems, total_sems, spread_sem = take(2), take(2), take(2)
    in_sems, back_sems, qkv_sems, out_sems = take(2), take(2), take(2), take(2)
    share_sems = take(2)
    weights = [(qkv_zero, out_zero, in_zero, back_zero), (qkv_one, out_one, in_one, back_one)]
    greet(around(near_devices()))
    rows = hidden.shape[0]
    size = rows // PIECES
    share = mixed_t.shape[0]
    per_device = share // HD
    pieces = range(PIECES)

    def block(b):
        return pl.ds(b * rows, rows)

    def piece(b, i):
        return pl.ds(b * rows + i * size, size)

    def spread_of(part):
        return Spread(mine[part], whole[part], spread_sem, part)

    def send_tokens(layer, i, value):
        saved[layer][4][piece(0, i), :] = value.astype(jnp.bfloat16)
        gathers[layer].start(i)

    gathers = [Gather(saved[layer][4], gather_sems, layer) for layer in range(2)]
    for i in pieces:
        send_tokens(0, i, hidden[piece(0, i), :])
    spreads = [spread_of(part) for part in range(2)]
    held[...] = hidden[...]

    def forward(
        layer,
        after_projection,
        after_far,
        after_attention,
        before_feed,
        before_back,
        after_feed,
        close,
    ):
        second_normal, second_inverse, first_normal, first_inverse = saved[layer][:4]
        tokens, heads, mixed, logs, firsts, active, slope = saved[layer][4:]
        qkv_w, out_w, in_w, back_w = weights[layer]
        gather, norm = gathers[layer], norms[layer]

        def project(place):
            parts = nn(tokens[place, :], rows_joined(qkv_w))
            for j in range(3 * per_device):
                part = parts[:, j * HD : (j + 1) * HD]
                if j < per_device:
                    part = part * HD ** (-0.5)
                heads[j, place, :] = part.astype(jnp.bfloat16)

        project(block(0))
        gather.wait_beside()
        project(block(1))
        for i in pieces:
            gather.hand_on(i)
            project(piece(2, i))
        for i in pieces:
            gather.wait_handed(i)
        project(block(3))
        gather.finish()
        after_projection()

        def attend(b):
            def one_head(h, carry):
                scores = nt(heads[per_device + h], heads[h, block(b), :])
                peak = jnp.max(scores, axis=0, keepdims=True)
                raised = jnp.exp(scores - peak)
                total = jnp.sum(raised, axis=0, keepdims=True)
                result = tn(heads[2 * per_device + h], raised.astype(jnp.bfloat16)) / total
                mixed_t[pl.ds(pl.multiple_of(h * HD, HD), HD), :] = result
                logs[b * per_device + h] = peak + jnp.log(total)
                return carry

            lax.fori_loop(0, per_device, one_head, 0)
            rows_mixed = mixed_t[...].T.astype(jnp.bfloat16)
            mixed[block(b), :] = rows_mixed
            return nn(rows_mixed, rows_joined(out_w))

        total = Total(out, into, total_sems, layer)
        term = attend(3)
        for i in pieces:
            total.give_far(i, total.part(term, i))
        term = attend(2)
        for i in pieces:
            total.give_facing(i, total.part(term, i))
        after_far()
        term = attend(1)
        for i in pieces:
            total.give_beside(i, total.part(term, i))
        held[...] += attend(0)
        after_attention()
        gather_two = Gather(firsts, gather_sems, 2 + layer)
        for i in pieces:
            place = piece(0, i)
            first, normal, inverse = norm_forward(
                total.take(i, held[place, :]), norm[0:1, :], norm[1:2, :]
            )
            firsts[place, :] = first.astype(jnp.bfloat16)
            gather_two.start(i)
            first_normal[place, :] = normal
            first_inverse[place, :] = inverse
            held[place, :] = first
        total.finish()
        before_feed()

        def feed(place, ready=lambda: None):
            value, gradient = gelu_pair(nn(firsts[place, :], rows_joined(in_w)))
            value = value.astype(jnp.bfloat16)
            active[place, :] = value
            slope[place, :] = gradient.astype(jnp.bfloat16)
            ready()
            return nt(value, rows_joined(back_w))

        total = Total(out, into, total_sems, 2 + layer)
        held[...] += feed(block(0), before_back)
        gather_two.wait_beside()
        term = feed(block(1))
        for i in pieces:
            total.give_beside(i, total.part(term, i))
        for i in pieces:
            gather_two.hand_on(i)
            term = feed(piece(2, i))
            gather_two.wait_handed(i)
            total.give_far(i, feed(piece(3, i)))
            total.give_facing(i, term)
        after_feed()
        for i in pieces:
            place = piece(0, i)
            result, normal, inverse = norm_forward(
                total.take(i, held[place, :]), norm[2:3, :], norm[3:4, :]
            )
            second_normal[place, :] = normal
            second_inverse[place, :] = inverse
            close(i, result)
        gather_two.finish()
        total.finish()

    def note(layer, row, i, gain, bias):
        target = norm_grads[layer]
        if i:
            gain, bias = gain + target[row, :], bias + target[row + 1, :]
        target[row : row + 1, :] = gain[None]
        target[row + 1 : row + 2, :] = bias[None]

    feed_gathers = [Gather(feeds, gather_sems, 4 + layer) for layer in range(2)]

    def send_feed_grad(layer, i, gradient):
        place = piece(0, i)
        grad_second, gain, bias = norm_backward(
            gradient, saved[layer][0][place, :], saved[layer][1][place, :], norms[layer][2:3, :]
        )
        feeds[place, :] = grad_second.astype(jnp.bfloat16)
        feed_gathers[layer].start(i)
        note(layer, 2, i, gain, bias)
        held[place, :] = grad_second

    def backward(layer, before_in, after_back, after_score, close_in, close):
        _, _, first_normal, first_inverse = saved[layer][:4]
        tokens, heads, mixed, logs, firsts, active, slope = saved[layer][4:]
        qkv_w, out_w, in_w, back_w = weights[layer]
        gather = feed_gathers[layer]

        def feed(place):
            part = nn(feeds[place, :], rows_joined(back_w)) * slope[place, :].astype(jnp.float32)
            part = part.astype(jnp.bfloat16)
            inner[place, :] = part
            return nt(part, rows_joined(in_w))

        total = Total(out, into, total_sems, 4 + layer)
        held[...] += feed(block(0))
        gather.wait_beside()
        term = feed(block(1))
        for i in pieces:
            total.give_beside(i, total.part(term, i))
        for i in pieces:
            gather.hand_on(i)
            term = feed(piece(2, i))
            gather.wait_handed(i)
            total.give_far(i, feed(piece(3, i)))
            total.give_facing(i, term)
        gather.finish()
        before_in()
        in_g[...] = tn(firsts[...], inner[...]).astype(jnp.bfloat16).reshape(in_g.shape)
        in_reduce = Reduce(in_g, in_near[layer], in_come[0], in_sems, layer)
        gather_two = Gather(lows, gather_sems, 6 + layer)
        for i in pieces:
            place = piece(0, i)
            grad_first, gain, bias = norm_backward(
                total.take(i, held[place, :]),
                first_normal[place, :],
                first_inverse[place, :],
                norms[layer][0:1, :],
            )
            lows[place, :] = grad_first.astype(jnp.bfloat16)
            gather_two.start(i)
            note(layer, 0, i, gain, bias)
            held[place, :] = grad_first
        total.finish()
        back_g[...] = tn(feeds[...], active[...]).astype(jnp.bfloat16).reshape(back_g.shape)
        back_reduce = Reduce(back_g, back_near[layer], back_come[0], back_sems, layer)
        after_back()

        def spread(place):
            parts = nt(lows[place, :], rows_joined(out_w))
            for j in range(per_device):
                mixed_grad[j, place, :] = parts[:, j * HD : (j + 1) * HD].astype(jnp.bfloat16)

        def score(b):
            def one_head(h, carry):
                query, key = heads[h, block(b), :], heads[per_device + h]
                upper = mixed_grad[h, block(b), :]
                prob = jnp.exp(nt(key, query) - logs[b * per_device + h])
                product = nt(heads[2 * per_device + h], upper)
                center = jnp.sum(prob * product, axis=0, keepdims=True)
                score_grad = (prob * (product - center)).astype(jnp.bfloat16)
                key_term = nn(score_grad, query)
                value_term = nn(prob.astype(jnp.bfloat16), upper)
                if b:
                    key_term, value_term = key_term + key_grad[h], value_term + value_grad[h]
                key_grad[h] = key_term
                value_grad[h] = value_term
                turned = tn(key, score_grad) * HD ** (-0.5)
                query_grad[h, block(b), :] = turned.T.astype(jnp.bfloat16)
                return carry

            lax.fori_loop(0, per_device, one_head, 0)

        spread(block(0))
        score(0)
        for i in pieces:
            gather_two.hand_on(i)
        gather_two.wait_beside()
        spread(block(1))
        score(1)
        after_score()
        in_reduce.middle()
        spread(block(2))
        score(2)
        for i in pieces:
            gather_two.wait_handed(i)
        spread(block(3))
        back_reduce.middle()
        score(3)
        gather_two.finish()
        for h in range(per_device):
            for c, grad in enumerate((query_grad, key_grad, value_grad)):
                start = c * share + h * HD
                head_grads[:, start : start + HD] = grad[h].astype(jnp.bfloat16)

        total = Total(out, into, total_sems, 6 + layer)
        weight = rows_joined(qkv_w)
        term = nt(head_grads[block(3), :], weight)
        for i in pieces:
            total.give_far(i, total.part(term, i))
        term = nt(head_grads[block(2), :], weight)
        for i in pieces:
            total.give_facing(i, total.part(term, i))
        term = nt(head_grads[block(1), :], weight)
        for i in pieces:
            total.give_beside(i, total.part(term, i))
        held[...] += nt(head_grads[block(0), :], weight)
        qkv_g[...] = tn(tokens[...], head_grads[...]).astype(jnp.bfloat16).reshape(qkv_g.shape)
        out_g[...] = tn(mixed[...], lows[...]).astype(jnp.bfloat16).reshape(out_g.shape)
        close_in()
        for i in pieces:
            close(i, total.take(i, held[piece(0, i), :]))
        total.finish()
        return in_reduce, back_reduce

    def between(i, result):
        held[piece(0, i), :] = result
        send_tokens(1, i, result)

    def after_far_zero():
        spreads[0].hand_on()
        spreads[1].hand_on()

    def after_attention_zero():
        spreads.append(spread_of(2))

    def before_feed_zero():
        spreads[0].arrive()
        spreads.append(spread_of(3))

    def after_feed_zero():
        spreads[2].hand_on()
        spreads.append(spread_of(4))

    forward(
        0,
        lambda: None,
        after_far_zero,
        after_attention_zero,
        before_feed_zero,
        spreads[1].arrive,
        after_feed_zero,
        between,
    )
    spreads[2].arrive()

    def turn(i, result):
        encoded[piece(0, i), :] = result
        send_feed_grad(1, i, cotangent[piece(0, i), :] * scale[...])

    def before_feed_one():
        spreads[3].arrive()

    forward(
        1,
        spreads[3].hand_on,
        spreads[4].hand_on,
        lambda: None,
        before_feed_one,
        spreads[4].arrive,
        lambda: None,
        turn,
    )
    for spread in spreads:
        spread.finish()

    reduces, shares = [], []
    none = lambda: None

    def start_prior():
        reduces.append(Reduce(qkv_g, *qkv_parts, qkv_sems, 0))
        reduces.append(MixReduce(out_g, *out_parts, out_sems, 0))

    in_reduce, back_reduce = backward(
        1,
        none,
        none,
        none,
        start_prior,
        lambda i, value: send_feed_grad(0, i, value),
    )
    in_prior, back_prior = in_reduce, back_reduce

    def prior_middle():
        in_sums[1][...] = in_prior.finish()
        back_sums[1][...] = back_prior.finish()
        for reduce in reduces:
            reduce.middle()

    def prior_finish():
        qkv_shared[lax.axis_index("mp")] = reduces[0].finish().astype(qkv_shared.dtype)
        shares.append(Share(qkv_shared, share_sems, 0))
        shares.append(RootShare(reduces[1].finish(), out_shared, share_sems, 1))

    def start_pair():
        for share in shares:
            share.hand_on()
        reduces.append(Reduce(qkv_g, qkv_pair, None, qkv_sems, 1))
        reduces.append(MixReduce(out_g, out_pair, None, out_sems, 1))

    def last(i, value):
        gradient_out[piece(0, i), :] = value

    in_reduce, back_reduce = backward(0, prior_middle, none, prior_finish, start_pair, last)
    in_sums[0][...] = in_reduce.finish()
    back_sums[0][...] = back_reduce.finish()
    shares[0].arrive()
    for share in shares:
        share.finish()
    for reduce in reduces[2:]:
        reduce.add_up()


def halves():
    depth = lax.axis_size("dp") // 2
    steps = [*range(1, depth), 0]
    return [[(k, (k + 1 + half) % 2) for k in steps] for half in range(2)]


def group_at(step, back=False):
    group = lax.axis_index("dp")
    depth = lax.axis_size("dp") // 2
    z, x = columns_of(group)
    along = depth - step[0] if back else step[0]
    return ((z + along) % depth) * 2 + (x + step[1]) % 2


def start_kernel(*refs):
    refs = iter(refs)
    take = lambda count: [next(refs) for _ in range(count)]
    sent_ids, codes, levels, tables, small = take(5)
    qkv_mine, out_pair = take(2)
    mine, out_mine = [qkv_mine.at[0]], [out_pair.at[0], out_pair.at[1]]
    hidden, asked, scale = take(3)
    norms = take(2)
    whole, out_whole = take(1), take(2)
    small_all, found, returned, out_a, into_a, table_rows, stream = take(7)
    total_a, small_sems, spread_sem, out_sems, id_sems, near_sems, row_sems = [take(2) for _ in range(7)]
    (stream_sems,) = take(1)
    group, member = lax.axis_index("dp"), lax.axis_index("mp")
    groups, members = lax.axis_size("dp"), lax.axis_size("mp")
    depth = groups // 2
    z, x = columns_of(group)
    beside = (group + 1 - 2 * x, member)
    peers = group_peers()
    sib, face = near_devices()
    far = (group, (sib[1] + 2) % members)
    own_rows = table_rows.shape[0]
    part = own_rows // 3
    streams = [
        pltpu.make_async_copy(
            tables.at[:, pl.ds(n * part, part)], stream.at[n % 2], stream_sems.at[n % 2]
        )
        for n in range(3)
    ]
    streams[0].start()
    streams[1].start()

    def add_tables(n):
        streams[n].wait()
        total = stream[n % 2, 0]
        for t in range(1, stream.shape[1]):
            total = total + stream[n % 2, t]
        table_rows[n * part : (n + 1) * part, :] = total.astype(table_rows.dtype)

    greet([*peers, *mates()])

    id_copies = [
        send(sent_ids.at[peer[0]], asked.at[0, group], id_sems, k, peer)
        for k, peer in enumerate(peers)
    ]
    asked[0, group] = sent_ids[group]
    small_spread = Spread(small, small_all, small_sems, 0)
    spreads = [Spread(a, b, spread_sem, p) for p, (a, b) in enumerate(zip(mine, whole))]
    add_tables(0)
    streams[2].start()
    for copy in id_copies:
        copy.wait_recv()
    near_copies = [
        send(asked.at[0], asked.at[k + 1], near_sems, k, peer)
        for k, peer in enumerate((sib, face, far))
    ]
    def root_copies():
        return [
            pltpu.make_async_remote_copy(
                src_ref=mine_out,
                dst_ref=target.at[x],
                send_sem=out_sems[0].at[p, k],
                recv_sem=out_sems[1].at[p, 0],
                device_id=(((z + k) % depth) * 2 + x, member),
                device_id_type=MESH,
            )
            for p, (mine_out, target) in enumerate(zip(out_mine, out_whole))
            for k in range(1, depth)
        ]

    @pl.when(z == member)
    def _():
        for copy in root_copies():
            copy.start()
        for mine_out, target in zip(out_mine, out_whole):
            target[x] = mine_out[...]

    add_tables(1)
    add_tables(2)
    for copy in near_copies:
        copy.wait_recv()
    first_row = ((group * members + member) * own_rows).astype(jnp.float32)
    capacity = asked.shape[3]
    half_slots = depth * capacity

    def lookup(r, half):
        line = jnp.concatenate([asked[r, group_at(step)] for step in halves()[half]], axis=1)
        line = line.astype(jnp.float32) - first_row
        line = jnp.broadcast_to(line, (8, half_slots)).T[:, 0:1]
        place = lax.broadcasted_iota(jnp.int32, (half_slots, own_rows), 1)
        hot = (line == place.astype(jnp.float32)).astype(jnp.bfloat16)
        return nn(hot, table_rows[...])

    total = Total(out_a, into_a, total_a, 0, 2)
    for half in range(2):
        total.give_far(half, lookup(3, half))
        total.give_facing(half, lookup(2, half))
    for half in range(2):
        total.give_beside(half, lookup(1, half))
    own = [lookup(0, half) for half in range(2)]
    small_spread.hand_on()
    spreads[0].hand_on()

    @pl.when(z != member)
    def _():
        for p in range(2):
            pltpu.make_async_remote_copy(
                src_ref=out_mine[p],
                dst_ref=out_whole[p].at[x],
                send_sem=out_sems[0].at[p, 0],
                recv_sem=out_sems[1].at[p, 0],
                device_id=beside,
                device_id_type=MESH,
            ).wait_recv()

    out_copies = [
        pltpu.make_async_remote_copy(
            src_ref=target.at[x],
            dst_ref=target.at[x],
            send_sem=out_sems[0].at[p, depth],
            recv_sem=out_sems[1].at[p, 1],
            device_id=beside,
            device_id_type=MESH,
        )
        for p, target in enumerate(out_whole)
    ]
    for copy in out_copies:
        copy.start()
    row_copies = []
    for half, steps in enumerate(halves()):
        rows_found = total.take(half, own[half]).astype(jnp.bfloat16)
        found[half * depth : (half + 1) * depth] = rows_found.reshape(depth, capacity, -1)
        for n, step in enumerate(steps):
            slot = half * depth + n
            if step == (0, 0):
                returned[group] = found[slot]
            else:
                row_copies.append(
                    send(
                        found.at[slot],
                        returned.at[group],
                        row_sems,
                        slot,
                        (group_at(step), member),
                    )
                )
    small_spread.arrive()
    for layer, target in enumerate(norms):
        half = target.shape[1] // 2
        for c in range(groups):
            start = (c % 2) * half
            target[c // 2 : c // 2 + 1, start : start + half] = small_all[
                c, 8:9, layer * half : (layer + 1) * half
            ]
    counts = small_all[0, 9:10, :]
    for c in range(1, groups):
        counts = counts + small_all[c, 9:10, :]
    same = jnp.sum(counts * small[9:10, :], axis=1, keepdims=True)
    scale[...] = groups / (STUDY_TOTAL * same)
    level_rows = 8 * groups
    level_full = jnp.concatenate([small_all[c, 0:8, :] for c in range(groups)], axis=0)
    rows = hidden.shape[0]
    level_hot = hot_places(levels, level_rows)
    level_part = nn(level_hot, level_full.astype(jnp.bfloat16))
    slot_hot = hot_places(codes, groups * capacity)
    for copy in row_copies:
        copy.wait_recv()
    hidden[...] = nn(slot_hot, rows_joined(returned)) + level_part

    for copy in [*id_copies, *near_copies, *row_copies]:
        copy.wait_send()
    total.finish()
    for spread in spreads:
        spread.arrive()
    for spread in (small_spread, *spreads):
        spread.finish()
    for copy in out_copies:
        copy.wait()

    @pl.when(z == member)
    def _():
        for copy in root_copies():
            copy.wait_send()


def end_kernel(*refs):
    refs = iter(refs)
    take = lambda count: [next(refs) for _ in range(count)]
    gradient, codes, levels, asked, qkv_pair, out_pair = take(6)
    norm_zero, norm_one = take(2)
    row_grad, hits, qkv_shared, out_shared, small_sum = take(5)
    slots, arrived, small_g, small_in = take(4)
    qkv_come, small_near, small_come, mix_come = take(4)
    mix_sems, qkv_sems, small_sems, gather_sems, row_sems, mate_sems = [take(2) for _ in range(6)]
    group, member = lax.axis_index("dp"), lax.axis_index("mp")
    groups, members = lax.axis_size("dp"), lax.axis_size("mp")
    depth = groups // 2
    z, x = columns_of(group)
    peers, near = group_peers(), mates()
    greet([*peers, *near])
    rows, width = gradient.shape
    capacity = slots.shape[1]
    count = groups * capacity
    half_count = depth * capacity

    slot_hot = hot_places(codes, count)
    high = gradient[...].astype(jnp.bfloat16)
    slots[...] = tn(slot_hot, high).astype(jnp.bfloat16).reshape(slots.shape)
    row_copies = []
    for half, steps in enumerate(halves()):
        copies = []
        for n, step in enumerate(steps):
            slot = half * depth + n
            target = arrived.at[pl.ds(slot * capacity, capacity)]
            if step == (0, 0):
                arrived[slot * capacity : (slot + 1) * capacity, :] = slots[group]
            else:
                there = group_at(step)
                copies.append(send(slots.at[there], target, row_sems, slot, (there, member)))
        row_copies.append(copies)
    qkv_reduce = Reduce(None, qkv_pair, qkv_come, qkv_sems, 0)
    mix = MixReduce(None, out_pair, mix_come, mix_sems, 0)

    level_hot = hot_places(levels, 8 * groups)
    rest = (gradient[...] - high.astype(jnp.float32)).astype(jnp.bfloat16)
    level_grad = tn(level_hot, high) + tn(level_hot, rest)
    half_width = width // 2
    for c in range(groups):
        small_g[c // 2, c % 2, 0:8, :] = level_grad[c * 8 : (c + 1) * 8, :]
        start = (c % 2) * half_width
        for layer, source in enumerate((norm_zero, norm_one)):
            small_g[c // 2, c % 2, 8:9, layer * half_width : (layer + 1) * half_width] = source[
                c // 2 : c // 2 + 1, start : start + half_width
            ]
        small_g[c // 2, c % 2, 9:16, :] = jnp.zeros((7, width), jnp.float32)
    small_reduce = Reduce(small_g, small_near, small_come, small_sems, 0)

    gather = Gather(arrived, gather_sems, 0, 2)
    for half in range(2):
        for copy in row_copies[half]:
            copy.wait_recv()
        gather.start(half)
        if half == 0:
            small_reduce.middle()
            qkv_reduce.middle()
            mix.middle()

    own_rows = row_grad.shape[0]
    first_row = (group * members + member) * own_rows

    def collect(blocks, which):
        line = jnp.concatenate(
            [
                asked[r, group_at(step, back=True)]
                for r in blocks
                for half in which
                for step in halves()[half]
            ],
            axis=1,
        )
        line = line - first_row
        slots_here = line.shape[1]
        place = lax.broadcasted_iota(jnp.int32, (own_rows, slots_here), 0)
        hot = (line == place).astype(jnp.float32)
        source = jnp.concatenate(
            [
                arrived[pl.ds(r * count + half * half_count, half_count), :]
                for r in blocks
                for half in which
            ],
            axis=0,
        )
        part = nn(hot.astype(jnp.bfloat16), source)
        found = jnp.sum(hot, axis=1, keepdims=True)
        if blocks[0]:
            row_grad[...] += part
            hits[...] += found
        else:
            row_grad[...] = part
            hits[...] = found

    gather.wait_beside()
    collect([0, 1], [0, 1])
    gather.hand_on(0)

    small_in[member] = small_reduce.finish()
    small_share = Share(small_in, mate_sems, 0)
    out_share = RootShare(mix.finish(), out_shared, mate_sems, 1)
    qkv_shared[member] = qkv_reduce.finish().astype(qkv_shared.dtype)
    qkv_share = Share(qkv_shared, mate_sems, 2)
    gather.hand_on(1)
    small_share.hand_on()
    out_share.hand_on()
    gather.wait_handed(0)
    collect([2, 3], [0])
    gather.wait_handed(1)
    collect([2, 3], [1])

    qkv_share.hand_on()
    small_share.arrive()
    total = small_in[0]
    for m in range(1, members):
        total = total + small_in[m]
    small_sum[...] = total
    qkv_share.arrive()
    for copy in sum(row_copies, []):
        copy.wait_send()
    for each in (gather, small_share, out_share, qkv_share):
        each.finish()


def run_kernel(kernel, collective_id, name, inputs, outputs, scratch, flops=0, exps=0, left=()):
    moved = sum(math.prod(a.shape) * a.dtype.itemsize for a in inputs)
    return pl.pallas_call(
        kernel,
        out_shape=[jax.ShapeDtypeStruct(*o) for o in outputs],
        in_specs=[
            pl.BlockSpec(memory_space=pl.ANY if n in left else pltpu.VMEM)
            for n in range(len(inputs))
        ],
        out_specs=[pl.BlockSpec(memory_space=pltpu.VMEM)] * len(outputs),
        scratch_shapes=scratch,
        compiler_params=pltpu.CompilerParams(
            collective_id=collective_id, has_side_effects=True, vmem_limit_bytes=60 * 2**20
        ),
        cost_estimate=pl.CostEstimate(flops=flops, bytes_accessed=moved, transcendentals=exps),
        name=name,
    )(*inputs)


def run_layers(hidden, cotangent, scale, norms, qkv_zero, out_w, mine):
    rows, width = hidden.shape
    cell = 4 * rows
    groups, part, columns = qkv_zero.shape
    depth = groups // 2
    share = columns // 3
    per_device = share // HD
    units = mine[1].shape[2]
    f32, low = jnp.float32, jnp.bfloat16
    outputs = [
        ((rows, width), f32),
        ((rows, width), f32),
        ((4, width), f32),
        ((4, width), f32),
        ((depth, part, columns), low),
        ((part, width), low),
        ((part, units), f32),
        ((part, units), f32),
        ((part, units), f32),
        ((part, units), f32),
        ((4, part, columns), low),
        ((part, width), low),
    ]
    kept = [
        pltpu.VMEM((rows, width), f32),
        pltpu.VMEM((rows, 1), f32),
        pltpu.VMEM((rows, width), f32),
        pltpu.VMEM((rows, 1), f32),
        pltpu.VMEM((cell, width), low),
        pltpu.VMEM((3 * per_device, cell, HD), low),
        pltpu.VMEM((cell, share), low),
        pltpu.VMEM((4 * per_device, 1, rows), f32),
        pltpu.VMEM((cell, width), low),
        pltpu.VMEM((cell, units), low),
        pltpu.VMEM((cell, units), low),
    ]
    scratch = [
        pltpu.VMEM((groups, part, wide), low) for wide in (units, units, columns, units, units)
    ] + kept * 2
    scratch += [
        pltpu.VMEM((share, rows), f32),
        pltpu.VMEM((rows, width), f32),
        pltpu.VMEM((3, rows, width), low),
        pltpu.VMEM((3, rows, width), low),
        pltpu.VMEM((cell, width), low),
        pltpu.VMEM((cell, units), low),
        pltpu.VMEM((cell, width), low),
        pltpu.VMEM((per_device, cell, HD), low),
        pltpu.VMEM((per_device, cell, HD), f32),
        pltpu.VMEM((per_device, cell, HD), f32),
        pltpu.VMEM((per_device, cell, HD), low),
        pltpu.VMEM((cell, columns), low),
        pltpu.VMEM((depth, 2, part, units), low),
        pltpu.VMEM((depth, 2, part, units), low),
        pltpu.VMEM((depth, 2, part, columns), low),
        pltpu.VMEM((2, part, width), low),
    ]
    near, come = reduce_scratch(part, units, low)
    scratch += [near, near, come] * 2 + reduce_scratch(part, columns, low)
    scratch += [pltpu.VMEM((part, width), low), pltpu.VMEM((depth - 1, part, width), low)]
    scratch += dma_sems(8, 3 * PIECES) + dma_sems(8, 3 * PIECES) + dma_sems(5, 2 * depth - 1)
    scratch += dma_sems(2, depth) * 4 + dma_sems(2, 3)
    flops = 12 * cell * width * (4 * share + 2 * units) + 28 * cell * cell * share
    return run_kernel(
        layers_kernel,
        1,
        "layers",
        [hidden, cotangent, scale, *norms, qkv_zero, *out_w, *mine],
        outputs,
        scratch,
        flops,
        4 * cell * cell * per_device,
    )


def updated(weight, first, second, grad, rate, decay):
    first = beta_one * first + (1.0 - beta_one) * grad
    second = beta_two * second + (1.0 - beta_two) * grad * grad
    first_hat = first * (1.0 / (1.0 - beta_one**STEP))
    second_hat = second * (1.0 / (1.0 - beta_two**STEP))
    new = weight - rate * (first_hat / (jnp.sqrt(second_hat) + adam_eps) + decay * weight)
    return new, first, second


def update_kernel(*refs):
    refs = iter(refs)
    take = lambda count: [next(refs) for _ in range(count)]
    weight, moments, row_grad, hits = take(4)
    qkv_grads, out_grads, in_grads, back_grads = take(2), take(2), take(2), take(2)
    small_grad, level, level_moments, norm, norm_moments = take(5)
    given = take(8)
    new_weight, new_moments = take(2)
    new_level, new_level_moments, new_norm, new_norm_moments = take(4)
    made = take(8)
    held = take(8)
    load_sems, store_sems = take(2)
    step = pl.program_id(0) * pl.num_programs(1) + pl.program_id(1)
    last = pl.num_programs(0) * pl.num_programs(1) - 1
    layers = norm.shape[0]
    loads = [pltpu.make_async_copy(a, b, load_sems.at[n]) for n, (a, b) in enumerate(zip(given, held))]
    stores = [pltpu.make_async_copy(b, a, store_sems.at[n]) for n, (a, b) in enumerate(zip(made, held))]

    @pl.when(step == 0)
    def _():
        for load in loads:
            load.start()
        level_rows = level.shape[0]
        result = updated(
            level[...],
            level_moments[0],
            level_moments[1],
            small_grad[0:level_rows, :],
            rate_table,
            decay_rate,
        )
        new_level[...], new_level_moments[0], new_level_moments[1] = result
        columns = norm.shape[1]
        for n in range(layers):
            line = slice(n, n + 1)
            result = updated(
                norm[line, :],
                norm_moments[0, line, :],
                norm_moments[1, line, :],
                small_grad[level_rows : level_rows + 1, n * columns : (n + 1) * columns],
                rate_norm,
                0.0,
            )
            new_norm[line, :], new_norm_moments[0, line, :], new_norm_moments[1, line, :] = result

    def dense(which, place, grad, rate):
        value, kept = held[2 * which], held[2 * which + 1]
        result = updated(value[place], kept[(0, *place)], kept[(1, *place)], grad, rate, decay_rate)
        value[place], kept[(0, *place)], kept[(1, *place)] = result

    def qkv(n):
        members, _, columns = qkv_grads[n].shape
        share = columns // 3
        for c in range(3):
            grad = jnp.concatenate(
                [qkv_grads[n][m, :, c * share : (c + 1) * share] for m in range(members)], axis=1
            )
            dense(0, (n, c), grad.astype(jnp.float32), rate_dense)

    def plain(which, grads, rate):
        for n in range(layers):
            dense(which, (n,), grads[n][...].astype(jnp.float32), rate)

    jobs = [
        (2, 0, lambda: [qkv(n) for n in range(layers)]),
        (4, 1, lambda: plain(1, out_grads, rate_mixing)),
        (5, 2, lambda: plain(2, in_grads, rate_dense)),
        (6, 3, lambda: plain(3, back_grads, rate_dense)),
    ]
    for when, which, job in jobs:

        @pl.when(step == when)
        def _():
            for n in (2 * which, 2 * which + 1):
                loads[n].wait()
            job()
            for n in (2 * which, 2 * which + 1):
                stores[n].start()

    touched = hits[...] > 0
    old, old_first, old_second = weight[0], moments[0, 0], moments[1, 0]
    new, first, second = updated(old, old_first, old_second, row_grad[...], rate_table, decay_rate)
    new_weight[0] = jnp.where(touched, new, old)
    new_moments[0, 0] = jnp.where(touched, first, old_first)
    new_moments[1, 0] = jnp.where(touched, second, old_second)

    @pl.when(step == last)
    def _():
        for store in stores:
            store.wait()


def update_all(tables, table_moments, row_grad, hits, grads, small, small_state, state):
    count, own_rows, width = tables.shape
    step = own_rows // 3
    table_block = pl.BlockSpec((1, step, width), lambda i, t: (t, i, 0))
    moment_block = pl.BlockSpec((2, 1, step, width), lambda i, t: (0, t, i, 0))

    def whole(array):
        zeros = (0,) * array.ndim
        return pl.BlockSpec(array.shape, lambda i, t: zeros, pipeline_mode=pl.Buffered(1))

    left = pl.BlockSpec(memory_space=pl.ANY)
    kept = [*grads, small, *small_state]
    shape_of = lambda array: jax.ShapeDtypeStruct(array.shape, array.dtype)
    return pl.pallas_call(
        update_kernel,
        grid=(own_rows // step, count),
        in_specs=[
            table_block,
            moment_block,
            pl.BlockSpec((step, width), lambda i, t: (i, 0)),
            pl.BlockSpec((step, 1), lambda i, t: (i, 0)),
            *[whole(array) for array in kept],
            *[left] * len(state),
        ],
        out_specs=[
            table_block,
            moment_block,
            *[whole(array) for array in small_state],
            *[left] * len(state),
        ],
        out_shape=[shape_of(a) for a in (tables, table_moments, *small_state, *state)],
        scratch_shapes=[pltpu.VMEM(a.shape, a.dtype) for a in state]
        + [pltpu.SemaphoreType.DMA((len(state),))] * 2,
        compiler_params=pltpu.CompilerParams(vmem_limit_bytes=56 * 2**20),
        cost_estimate=pl.CostEstimate(
            flops=20 * tables.size, bytes_accessed=28 * tables.size, transcendentals=tables.size
        ),
        name="update",
    )(tables, table_moments, row_grad, hits, *kept, *state)


def fast_body(
    gene_ids,
    levels,
    study_of_cell,
    cotangent,
    tables,
    table_moments,
    level_table,
    level_moments,
    qkv_weight,
    qkv_moments,
    out_weight,
    out_moments,
    in_weight,
    in_moments,
    back_weight,
    back_moments,
    norm_params,
    norm_moments,
):
    low = jnp.bfloat16
    groups = lax.axis_size("dp")
    members = lax.axis_size("mp")
    member = lax.axis_index("mp")
    rows_here, width = cotangent.shape
    layers = qkv_weight.shape[0]
    local_cells = study_of_cell.shape[0]
    capacity = 2 * rows_here // groups
    own_rows = tables.shape[1]
    block_size = own_rows * members
    depth = qkv_weight.shape[2]
    share = width // members
    units = in_weight.shape[2]

    assert groups == 2 * members and layers == 2 and local_cells == 1
    f32 = jnp.float32
    qkv_mine = lax.dynamic_slice_in_dim(qkv_weight, member * share, share, axis=3).astype(low)
    qkv_mine = qkv_mine.transpose(0, 2, 1, 3).reshape(layers, depth, 3 * share)
    out_mine = out_weight.astype(low)
    in_mine = in_weight.astype(low)
    back_mine = back_weight.astype(low).transpose(0, 2, 1)
    level_rows = level_table.shape[0]
    study_onehot = (study_of_cell[:, None] == jnp.arange(width)[None, :]).astype(f32)
    small = jnp.concatenate(
        [
            level_table.astype(low).astype(f32),
            norm_params.reshape(1, width),
            study_onehot,
            jnp.zeros((16 - level_rows - 2, width), f32),
        ]
    )
    row_owner = gene_ids // block_size
    slot_index = slots_of(row_owner)
    sent_ids = slotted_ids(gene_ids, row_owner, slot_index, groups, capacity)
    codes = (row_owner * capacity + slot_index)[None, :]
    level_line = levels[None, :]

    slots = groups * capacity
    copies = 2 * (groups // 2) - 1
    dma = pltpu.SemaphoreType.DMA
    hidden, asked, scale, *more = run_kernel(
        start_kernel,
        5,
        "start",
        [
            sent_ids[:, None, :],
            codes,
            level_line,
            tables,
            small,
            qkv_mine,
            out_mine,
        ],
        [
            ((rows_here, width), f32),
            ((members, groups, 1, capacity), jnp.int32),
            ((1, 1), f32),
            ((4, width), f32),
            ((4, width), f32),
            ((groups, depth, 3 * share), low),
            ((2, depth, width), low),
            ((2, depth, width), low),
        ],
        [
            pltpu.VMEM((groups, 16, width), f32),
            pltpu.VMEM((groups, capacity, width), low),
            pltpu.VMEM((groups, capacity, width), low),
            pltpu.VMEM((3, slots, width), low),
            pltpu.VMEM((3, slots, width), low),
            pltpu.VMEM((own_rows, width), low),
            pltpu.VMEM((2, tables.shape[0], own_rows // 3, width), f32),
        ]
        + dma_sems(1, 3 * 2)
        + [dma((1, copies))] * 2
        + [dma((1, copies))] * 2
        + [dma((2, groups // 2 + 1))] * 2
        + [dma((groups - 1,))] * 2
        + [dma((3,))] * 2
        + [dma((groups,))] * 2
        + [dma((2,))],
        left=(3,),
    )
    norms, qkv_w, out_w = more[0:2], more[2], more[3:5]
    hidden, gradient, norm_zero, norm_one, qkv_pair, out_pair, *more = run_layers(
        hidden,
        cotangent,
        scale,
        norms,
        qkv_w,
        out_w,
        [qkv_mine, in_mine, back_mine],
    )
    in_zero, in_one, back_zero, back_one, qkv_one, out_one = more
    row_grad, hits, qkv_zero, out_zero, small_sum = run_kernel(
        end_kernel,
        6,
        "finish",
        [
            gradient,
            codes,
            level_line,
            asked,
            qkv_pair,
            out_pair,
            norm_zero,
            norm_one,
        ],
        [
            ((own_rows, width), f32),
            ((own_rows, 1), f32),
            ((members, depth, 3 * share), low),
            ((depth, width), low),
            ((16, width), f32),
        ],
        [
            pltpu.VMEM((groups, capacity, width), low),
            pltpu.VMEM((4 * slots, width), low),
            pltpu.VMEM((groups // 2, 2, 16, width), f32),
            pltpu.VMEM((members, 16, width), f32),
        ]
        + reduce_scratch(depth, 3 * share, low)[1:]
        + reduce_scratch(16, width, f32)
        + [pltpu.VMEM((groups // 2 - 1, depth, width), low)]
        + dma_sems(1, groups // 2) * 3
        + dma_sems(1, 3 * 2)
        + [dma((groups,))] * 2
        + dma_sems(3, 3),
    )

    table_new, table_state, level_new, level_state, norm_new, norm_state, *more = update_all(
        tables,
        table_moments,
        row_grad,
        hits,
        [qkv_zero, qkv_one, out_zero, out_one, in_zero, in_one, back_zero, back_one],
        small_sum,
        [level_table, level_moments, norm_params, norm_moments],
        [
            qkv_weight,
            qkv_moments,
            out_weight,
            out_moments,
            in_weight,
            in_moments,
            back_weight.transpose(0, 2, 1),
            back_moments.transpose(0, 1, 3, 2),
        ],
    )
    qkv_new, qkv_state, out_new, out_state, in_new, in_state, back_new, back_state = more
    back_new, back_state = back_new.transpose(0, 2, 1), back_state.transpose(0, 1, 3, 2)
    return (
        hidden,
        table_new,
        table_state,
        level_new,
        level_state,
        qkv_new,
        qkv_state,
        out_new,
        out_state,
        in_new,
        in_state,
        back_new,
        back_state,
        norm_new,
        norm_state,
    )


def solution(mesh):
    return jax.shard_map(
        fast_body if (mesh.shape["dp"], mesh.shape["mp"]) == (8, 4) else general_body,
        mesh=mesh,
        in_specs=(
            P(("dp", "mp")),
            P(("dp", "mp")),
            P("dp"),
            P(("dp", "mp"), None),
            P(None, ("dp", "mp"), None),
            P(None, None, ("dp", "mp"), None),
            P("dp", None),
            P(None, "dp", None),
            P(None, None, "dp", None),
            P(None, None, None, "dp", None),
            P(None, "dp", None),
            P(None, None, "dp", None),
            P(None, "dp", "mp"),
            P(None, None, "dp", "mp"),
            P(None, "mp", "dp"),
            P(None, None, "mp", "dp"),
            P(None, "dp"),
            P(None, None, "dp"),
        ),
        out_specs=(
            P(("dp", "mp"), None),
            P(None, ("dp", "mp"), None),
            P(None, None, ("dp", "mp"), None),
            P("dp", None),
            P(None, "dp", None),
            P(None, None, "dp", None),
            P(None, None, None, "dp", None),
            P(None, "dp", None),
            P(None, None, "dp", None),
            P(None, "dp", "mp"),
            P(None, None, "dp", "mp"),
            P(None, "mp", "dp"),
            P(None, None, "mp", "dp"),
            P(None, "dp"),
            P(None, None, "dp"),
        ),
        check_vma=False,
    )
```
